128 devices in a mesh: gx: 16 (over z, y_lo, core), gy: 8 (over x, y_hi).
Axes of the slice: x: 4, y: 4 (y_hi: 2, y_lo: 2; y = y_hi * 2 + y_lo), z: 4, core: 2. Of those that a mesh axis runs over, the one named last changes fastest.
Arguments:
- source_hat: float32 [2, 3, 256, 256, 256], P(None, None, 'gx', 'gy'), may hold values from -0.0014648438 to 0.0014648438
- particle_start: int32 [3, 262144], P(None, ('gx', 'gy')), may hold values from 0 to 255, as said below
- particle_offset: float32 [3, 262144], P(None, ('gx', 'gy')), may hold values from 0 to 1
- ghost_start: int32 [3, 3, 65536], P(None, None, ('gx', 'gy')), may hold values from 0 to 255, as said below
- ghost_offset: float32 [3, 3, 65536], P(None, None, ('gx', 'gy')), may hold values from 0 to 1, as said below
- ghost_slot: int32 [3, 65536], P(None, ('gx', 'gy')), may hold values from 0 to 2047, as said below
- counts: int32 [128, 4], P(('gx', 'gy')), may hold values from 0 to 2048, as said below
Outputs:
- velocity_far: float32 [3, 262144], P(None, ('gx', 'gy'))
- strain_far: float32 [5, 262144], P(None, ('gx', 'gy'))
The draws below stay inside these ranges and needn't reach their ends.
Inputs may be any that keep to these rules, and one draw needn't show every extreme that they name: `particle_start`: on device (a, b), a its gx index and b its gy index, every slot's x start lies in [b * 32, (b + 1) * 32) and its z start in [a * 16, (a + 1) * 16). `counts`: row of a device: its live own slots (the slots below this count are live), then the live entries of ghost groups 0, 1, 2 (the entries below each count are live); each ghost count is at most 512. `ghost_slot`: group 0 of device (a, b) lists particles of device (a, b - 1), group 1 of (a - 1, b), group 2 of (a - 1, b - 1), indices modulo the axis sizes; every entry is a slot index of that owner, below 2048; its live entries name distinct live slots of that owner, and they are exactly the owner's live particles whose support reaches the device's brick. `ghost_start`: A live ghost entry repeats the start of the owner's slot that ghost_slot names. `ghost_offset`: A live ghost entry repeats the offset of the owner's slot that ghost_slot names.
All inputs are finite; a program needn't handle non-finite values.
Results may differ from the reference program's by a relative error of at most 0.008.
Values sent between devices are 32-bit elements; how exact they have to be, the bound alone decides.
No kernel may reach another device: no remote copies, remote signals or barrier semaphores. Data moves between devices by JAX's collectives and lax.ppermute only.
A program may use at most 192 MiB of HBM per device.

```python
import math
import jax
import jax.numpy as jnp
from jax import lax

GRID = 256
SUPPORT = 8
OWN = 2048
GHOST = 512
N_GX = 16
N_GY = 8


def particle_tables(key):
    device_count = N_GX * N_GY
    brick_x = GRID // N_GY
    brick_z = GRID // N_GX
    devices_all = jnp.arange(device_count, dtype=jnp.int32)
    busiest = jax.random.randint(jax.random.fold_in(key, 11), (), 0, device_count)
    live_counts = jax.random.randint(jax.random.fold_in(key, 12), (device_count,), OWN // 8, OWN // 2 + 1)
    live_counts = jnp.where(devices_all == busiest, OWN, live_counts).astype(jnp.int32)
    quotas = live_counts // 8
    score_keys = jax.random.split(jax.random.fold_in(key, 13), device_count)
    scores = jax.vmap(lambda score_key: jax.random.permutation(score_key, OWN))(score_keys).astype(jnp.int32)
    slot_ids = jnp.arange(OWN, dtype=jnp.int32)
    masked = jnp.where(slot_ids[None, :] < live_counts[:, None], scores, scores + OWN)
    by_rank = jnp.argsort(masked, axis=1, stable=True).astype(jnp.int32)
    rank_table = jnp.argsort(by_rank, axis=1, stable=True).astype(jnp.int32)
    quota_col = quotas[:, None]
    cross_x = (rank_table < quota_col) | (rank_table >= 2 * quota_col) & (rank_table < 3 * quota_col)
    cross_z = (rank_table >= quota_col) & (rank_table < 3 * quota_col)
    low_x = jnp.where(cross_x, brick_x - SUPPORT + 1, 0)
    high_x = jnp.where(cross_x, brick_x, brick_x - SUPPORT + 1)
    low_z = jnp.where(cross_z, brick_z - SUPPORT + 1, 0)
    high_z = jnp.where(cross_z, brick_z, brick_z - SUPPORT + 1)
    local_x = jax.random.randint(jax.random.fold_in(key, 14), (device_count, OWN), low_x, high_x)
    local_z = jax.random.randint(jax.random.fold_in(key, 15), (device_count, OWN), low_z, high_z)
    start_y = jax.random.randint(jax.random.fold_in(key, 16), (device_count, OWN), 0, GRID)
    block_z = devices_all // N_GY
    block_x = devices_all % N_GY
    start_x = block_x[:, None] * brick_x + local_x
    start_z = block_z[:, None] * brick_z + local_z
    starts = jnp.stack([start_x, start_y, start_z]).astype(jnp.int32)
    owners = jnp.stack([block_z * N_GY + (block_x - 1) % N_GY, (block_z - 1) % N_GX * N_GY + block_x, (block_z - 1) % N_GX * N_GY + (block_x - 1) % N_GY]).astype(jnp.int32)
    owner_quota = quotas[owners]
    entry_index = jnp.arange(GHOST, dtype=jnp.int32)[None, :]
    first_quota = owner_quota[0][:, None]
    rank_first = jnp.where(entry_index < first_quota, entry_index, entry_index + first_quota)
    rank_second = owner_quota[1][:, None] + entry_index
    rank_third = 2 * owner_quota[2][:, None] + entry_index
    rank_all = jnp.minimum(jnp.stack([rank_first, rank_second, rank_third]), OWN - 1)
    slot_table = jnp.take_along_axis(by_rank[owners], rank_all, axis=2).astype(jnp.int32)
    counts_table = jnp.stack([live_counts, 2 * owner_quota[0], 2 * owner_quota[1], owner_quota[2]], axis=1).astype(jnp.int32)
    return (starts, owners, slot_table, counts_table)


def particle_offsets(key):
    uniform_draw = jax.random.uniform(jax.random.fold_in(key, 21), (3, N_GX * N_GY, OWN), jnp.float32)
    return uniform_draw


def draw_particle_start(key, part):
    starts, owners, slot_table, counts_table = particle_tables(key)
    return starts.reshape(3, N_GX * N_GY * OWN)


def draw_particle_offset(key, part):
    return particle_offsets(key).reshape(3, N_GX * N_GY * OWN)


def draw_ghost_start(key, part):
    starts, owners, slot_table, counts_table = particle_tables(key)
    return starts[:, owners[:, :, None], slot_table].reshape(3, 3, N_GX * N_GY * GHOST)


def draw_ghost_offset(key, part):
    starts, owners, slot_table, counts_table = particle_tables(key)
    return particle_offsets(key)[:, owners[:, :, None], slot_table].reshape(3, 3, N_GX * N_GY * GHOST)


def draw_ghost_slot(key, part):
    starts, owners, slot_table, counts_table = particle_tables(key)
    return slot_table.reshape(3, N_GX * N_GY * GHOST)


def draw_counts(key, part):
    starts, owners, slot_table, counts_table = particle_tables(key)
    return counts_table


def level_of(key, extent, cuts, low, largest):
    level, own = 1.0, jax.random.fold_in(key, 6)
    for dim, parts in cuts:
        heights = jnp.exp(jax.random.uniform(jax.random.fold_in(own, dim), (parts,), jnp.float32, low / len(cuts), largest / len(cuts)))
        level = level * jnp.repeat(heights, extent[dim] // parts).reshape([-1 if axis == dim else 1 for axis in range(len(extent))])
    return level


def scatter_about(own_key, dims, scale, limit, shards=(), kind=jnp.bfloat16):
    drawn = scale * jax.random.normal(own_key, dims, jnp.float32)
    if shards:
        drawn = drawn * level_of(own_key, dims, shards, -0.22, 0.18)
    return jnp.clip(drawn, -limit, limit).astype(kind)


def setup_inputs(seed: int = 0) -> dict:
    arg_keys = jax.random.split(jax.random.key(seed), 8)
    return {
        "source_hat": scatter_about(arg_keys[0], (2, 3, GRID, GRID, GRID), (GRID * GRID * GRID) ** -0.5, 0.0014648438, ((2, 16), (3, 8)), jnp.float32),
        "particle_start": draw_particle_start(jax.random.fold_in(arg_keys[7], 71), 0),
        "particle_offset": draw_particle_offset(jax.random.fold_in(arg_keys[7], 71), 0),
        "ghost_start": draw_ghost_start(jax.random.fold_in(arg_keys[7], 71), 0),
        "ghost_offset": draw_ghost_offset(jax.random.fold_in(arg_keys[7], 71), 0),
        "ghost_slot": draw_ghost_slot(jax.random.fold_in(arg_keys[7], 71), 0),
        "counts": draw_counts(jax.random.fold_in(arg_keys[7], 71), 0),
    }


TWO_PI = 2.0 * math.pi


def signed_modes(count_modes):
    indices = jnp.arange(count_modes, dtype=jnp.int32)
    return jnp.where(indices < count_modes // 2, indices, indices - count_modes).astype(jnp.float32)


def spread_weight(distance, offset_value):
    shifted = distance - (SUPPORT // 2 - 1) - offset_value
    return jnp.exp(-5.6 * shifted * shifted / SUPPORT)


def grid_fields(source_hat):
    modes_all = signed_modes(GRID)
    mode_x = modes_all[:, None, None]
    mode_y = modes_all[None, :, None]
    mode_z = modes_all[None, None, :]
    square = jnp.maximum(mode_x * mode_x + mode_y * mode_y + mode_z * mode_z, 1.0)
    inner_product = source_hat[:, 0] * mode_x + source_hat[:, 1] * mode_y + source_hat[:, 2] * mode_z
    mode_list = (mode_x, mode_y, mode_z)
    velocity = [source_hat[:, comp_index] - mode_list[comp_index] * inner_product / square for comp_index in range(3)]
    complex_velocity = [part_pair[0] + 1j * part_pair[1] for part_pair in velocity]
    waves = [TWO_PI / GRID * mode_item for mode_item in mode_list]

    def derivative(comp_index, axis_index):
        return 1j * waves[axis_index] * complex_velocity[comp_index]

    spectra = [complex_velocity[0], complex_velocity[1], complex_velocity[2],
               derivative(0, 0), derivative(1, 1),
               0.5 * (derivative(0, 1) + derivative(1, 0)),
               0.5 * (derivative(0, 2) + derivative(2, 0)),
               0.5 * (derivative(1, 2) + derivative(2, 1))]
    return jnp.stack([jnp.real(jnp.fft.ifftn(spectrum, norm="forward")).astype(jnp.bfloat16) for spectrum in spectra])


def device_values(fields, device, start_rows, offset_rows, live_rows):
    brick_x = GRID // N_GY
    brick_z = GRID // N_GX
    block_z = device // N_GY
    block_x = device % N_GY
    steps_all = jnp.arange(SUPPORT, dtype=jnp.int32)
    cells_x = (start_rows[0][:, None] + steps_all[None, :]) % GRID
    cells_y = (start_rows[1][:, None] + steps_all[None, :]) % GRID
    cells_z = (start_rows[2][:, None] + steps_all[None, :]) % GRID
    inside_x = (cells_x // brick_x == block_x).astype(jnp.float32)
    inside_z = (cells_z // brick_z == block_z).astype(jnp.float32)
    distance = steps_all.astype(jnp.float32)[None, :]
    weight_x = spread_weight(distance, offset_rows[0][:, None]) * inside_x
    weight_y = spread_weight(distance, offset_rows[1][:, None])
    weight_z = spread_weight(distance, offset_rows[2][:, None]) * inside_z
    weight_plane = weight_x[:, :, None] * weight_z[:, None, :] * live_rows[:, None, None]
    weight_plane = lax.optimization_barrier(weight_plane.astype(jnp.bfloat16)).astype(jnp.float32)
    window = fields[:, cells_x[:, :, None, None], cells_y[:, None, :, None], cells_z[:, None, None, :]].astype(jnp.float32)
    return jnp.einsum("frijk,rik,rj->rf", window, weight_plane, weight_y)


def reference(source_hat, particle_start, particle_offset, ghost_start, ghost_offset, ghost_slot, counts):
    fields = lax.optimization_barrier(grid_fields(source_hat))
    device_count = N_GX * N_GY
    own_start = jnp.transpose(particle_start.reshape(3, device_count, OWN), (1, 0, 2))
    own_offset = jnp.transpose(particle_offset.reshape(3, device_count, OWN), (1, 0, 2))
    ghost_starts = jnp.transpose(ghost_start.reshape(3, 3, device_count, GHOST), (2, 0, 1, 3)).reshape(device_count, 3, 3 * GHOST)
    ghost_offsets = jnp.transpose(ghost_offset.reshape(3, 3, device_count, GHOST), (2, 0, 1, 3)).reshape(device_count, 3, 3 * GHOST)
    start_rows = jnp.concatenate([own_start, ghost_starts], axis=2)
    offset_rows = jnp.concatenate([own_offset, ghost_offsets], axis=2)
    own_live = jnp.arange(OWN, dtype=jnp.int32)[None, :] < counts[:, 0:1]
    ghost_live = jnp.arange(GHOST, dtype=jnp.int32)[None, None, :] < counts[:, 1:4, None]
    live_rows = jnp.concatenate([own_live, ghost_live.reshape(device_count, 3 * GHOST)], axis=1).astype(jnp.float32)
    devices_all = jnp.arange(device_count, dtype=jnp.int32)
    values = lax.map(lambda packed: device_values(fields, packed[0], packed[1], packed[2], packed[3]),
                     (devices_all, start_rows, offset_rows, live_rows))
    own_values = values[:, :OWN]
    ghost_values = values[:, OWN:].reshape(device_count, 3, GHOST, 8)
    block_z = devices_all // N_GY
    block_x = devices_all % N_GY
    owners = jnp.stack([block_z * N_GY + (block_x - 1) % N_GY,
                        ((block_z - 1) % N_GX) * N_GY + block_x,
                        ((block_z - 1) % N_GX) * N_GY + (block_x - 1) % N_GY], axis=1).astype(jnp.int32)
    slot_rows = jnp.transpose(ghost_slot.reshape(3, device_count, GHOST), (1, 0, 2))
    totals = own_values.at[owners[:, :, None], slot_rows].add(ghost_values)
    totals = jnp.transpose(totals, (2, 0, 1)).reshape(8, device_count * OWN)
    return totals[:3], totals[3:]
```

```python
import math

import jax
import jax.numpy as jnp
import numpy as np
from jax import lax
from jax.experimental import pallas as pl
from jax.experimental.pallas import tpu as pltpu
from jax.sharding import PartitionSpec as P

F32 = jnp.float32
BF16 = jnp.bfloat16
SUPPORT = 8
GRID = 256
N_GX = 16
N_GY = 8
OWN = 2048
GHOST = 512
ROWS = OWN + GHOST
WAVE = 2.0 * math.pi / GRID
WINDOW = 48
BLOCK = 256


def numpy_halves(table):
    import ml_dtypes

    high = table.astype(ml_dtypes.bfloat16)
    low = (table - high.astype(np.float64)).astype(ml_dtypes.bfloat16)
    return high, low


def z_table():
    c, slab, part, step = np.meshgrid(
        np.arange(4), np.arange(N_GX), np.arange(2), np.arange(4), indexing="ij"
    )
    z = (16 * slab + 4 * step + c).reshape(-1, 1)
    part = part.reshape(-1, 1)
    angle = (z * np.arange(GRID)[None, :] % GRID) * (2.0 * np.pi / GRID)
    cosine, sine = np.cos(angle), np.sin(angle)
    from_real = np.where(part == 0, cosine, sine)
    from_imag = np.where(part == 0, -sine, cosine)
    return np.concatenate([from_real, from_imag], axis=1)


def x_table():
    index = np.arange(GRID)
    angle = (index[:, None] * index[None, :] % GRID) * (2.0 * np.pi / GRID)
    cosine, sine = np.cos(angle), np.sin(angle)
    return np.block([[cosine, -sine], [sine, cosine]])


def y_table():
    index = np.arange(GRID)
    angle = (index[:, None] * index[None, :] % GRID) * (2.0 * np.pi / GRID)
    cosine = np.cos(angle).reshape(N_GY, 1, GRID // N_GY, GRID)
    sine = -np.sin(angle).reshape(N_GY, 1, GRID // N_GY, GRID)
    return np.concatenate([cosine, sine], axis=1).reshape(N_GY, 2 * (GRID // N_GY), GRID)


def split(value):
    high = value.astype(BF16)
    return high, (value - high.astype(F32)).astype(BF16)


def signed(index):
    return jnp.where(index < GRID // 2, index, index - GRID).astype(F32)


NT = (((1,), (1,)), ((), ()))
NN = (((1,), (0,)), ((), ()))


def dot3(a_high, a_low, b_high, b_low, dims):
    def one(a, b):
        return lax.dot_general(a, b, dims, preferred_element_type=F32)

    return one(a_high, b_high) + (one(a_high, b_low) + one(a_low, b_high))


def z_kernel(place, source, t_high, t_low, out, x_high, x_low):
    quad = pl.program_id(0)
    row = lax.broadcasted_iota(jnp.int32, (32, GRID), 0)
    mode_y = signed(row + place[1] * 32)
    mode_z = signed(lax.broadcasted_iota(jnp.int32, (32, GRID), 1))
    wave_z = WAVE * mode_z
    partial_square = mode_y * mode_y + mode_z * mode_z
    for k in range(4):
        index_x = place[0] * 16 + quad * 4 + k
        mode_x = jnp.where(index_x < GRID // 2, index_x, index_x - GRID).astype(F32)
        square = jnp.maximum(mode_x * mode_x + partial_square, 1.0)
        inverse = 1.0 / square
        v = []
        for r in range(2):
            s1, s2, s3 = source[r, 0, k], source[r, 1, k], source[r, 2, k]
            ratio = (s1 * mode_x + s2 * mode_y + s3 * mode_z) * inverse
            v.append((s1 - mode_x * ratio, s2 - mode_y * ratio, s3 - mode_z * ratio))
        rows = [
            (v[0][0], v[1][0], k * 128),
            (v[0][1], v[1][1], k * 128 + 32),
            (v[0][2], v[1][2], k * 128 + 64),
            (-wave_z * v[1][0], wave_z * v[0][0], k * 128 + 96),
            (-wave_z * v[1][1], wave_z * v[0][1], 512 + k * 32),
        ]
        for real, imag, start in rows:
            for r, value in ((0, real), (1, imag)):
                high, low = split(value)
                x_high[start : start + 32, r * GRID : (r + 1) * GRID] = high
                x_low[start : start + 32, r * GRID : (r + 1) * GRID] = low

    def transformed(start, size):
        return dot3(
            t_high[...], t_low[...], x_high[start : start + size], x_low[start : start + size], NT
        )

    for pair in range(2):
        result = transformed(pair * 256, 256)
        for side in range(2):
            lanes = slice(side * 128, side * 128 + 128)
            for c in range(4):
                out[:, pair * 2 + side, c * 8 : c * 8 + 8, :] = result[
                    c * 128 : c * 128 + 128, lanes
                ].reshape(N_GX, 8, 128)
    last = transformed(512, 128)
    lane = lax.broadcasted_iota(jnp.int32, (128, 128), 1)
    lower64 = lane < 64
    lower32 = (lane & 32) == 0
    v = [last[c * 128 : c * 128 + 128] for c in range(4)]
    p0 = [jnp.where(lower64, v[c], pltpu.roll(v[c + 2], 64, 1)) for c in range(2)]
    p1 = [jnp.where(lower64, pltpu.roll(v[c], 64, 1), v[c + 2]) for c in range(2)]
    for k1, p in ((0, p0), (1, p1)):
        q0 = jnp.where(lower32, p[0], pltpu.roll(p[1], 32, 1))
        q1 = jnp.where(lower32, pltpu.roll(p[0], 96, 1), p[1])
        out[:, 2 * k1, 32:40, :] = q0.reshape(N_GX, 8, 128)
        out[:, 2 * k1 + 1, 32:40, :] = q1.reshape(N_GX, 8, 128)


def z_stage(place, source, t_high, t_low):
    return pl.pallas_call(
        z_kernel,
        out_shape=jax.ShapeDtypeStruct((N_GX, 16, 40, 128), F32),
        grid_spec=pltpu.PrefetchScalarGridSpec(
            num_scalar_prefetch=1,
            grid=(4,),
            in_specs=[
                pl.BlockSpec((2, 3, 4, 32, GRID), lambda i, _: (0, 0, i, 0, 0)),
                pl.BlockSpec((512, 512), lambda i, _: (0, 0)),
                pl.BlockSpec((512, 512), lambda i, _: (0, 0)),
            ],
            out_specs=pl.BlockSpec((N_GX, 4, 40, 128), lambda i, _: (0, i, 0, 0)),
            scratch_shapes=[pltpu.VMEM((640, 512), BF16), pltpu.VMEM((640, 512), BF16)],
        ),
        name="z_stage",
    )(place, source, t_high, t_low)


def weight(distance, offset):
    shifted = distance - (SUPPORT // 2 - 1) - offset
    inside = (distance >= 0.0) & (distance < SUPPORT)
    return jnp.where(inside, jnp.exp(-5.6 / SUPPORT * shifted * shifted), 0.0)


def wrapped(distance):
    return jnp.where(distance < 0.0, distance + GRID, distance)


def field_kernel(
    place, received, t_high, t_low, y_high, y_low, particles, out, field, d_high, d_low, window
):
    lane = lax.broadcasted_iota(jnp.int32, (GRID, 128), 1)
    group = lane // 32
    wave_x = WAVE * signed(lax.broadcasted_iota(jnp.int32, (GRID, 128), 0))
    wave_y = WAVE * signed(lane % 32 + place[1] * 32)
    last_group = group == 3
    on_left = jnp.where(group == 0, wave_y, 0.0)
    on_right = jnp.where((group == 1) | last_group, 0.5 * wave_y, 0.0)
    on_same = jnp.where((group == 1) | (group == 2), 0.5 * wave_x, 0.0)
    for c in range(4):

        def one_z(step, carry):
            def load(start):
                return received[pl.ds(start, GRID, stride=40), :]

            parts = []
            for q in range(2):
                value = load(c * 8 + q * 4 + step)
                extra = load(32 + q * 4 + step)
                if c != 3:
                    extra = pltpu.roll(extra, 32 * (3 - c), 1)
                parts.append((value, pltpu.roll(value, 96, 1), pltpu.roll(value, 32, 1), extra))
            (a_re, l_re, r_re, e_re), (a_im, l_im, r_im, e_im) = parts
            first_re = jnp.where(last_group, -wave_x * l_im, a_re)
            first_im = jnp.where(last_group, wave_x * l_re, a_im)
            plain_re = jnp.where(group == 2, 0.5 * l_re, jnp.where(last_group, 0.5 * e_re, 0.0))
            plain_im = jnp.where(group == 2, 0.5 * l_im, jnp.where(last_group, 0.5 * e_im, 0.0))
            second_re = plain_re - (on_left * l_im + on_right * r_im + on_same * a_im)
            second_im = plain_im + (on_left * l_re + on_right * r_re + on_same * a_re)
            for top, left, value in (
                (0, 0, first_re),
                (GRID, 0, first_im),
                (0, 128, second_re),
                (GRID, 128, second_im),
            ):
                high, low = split(value)
                d_high[top : top + GRID, left : left + 128] = high
                d_low[top : top + GRID, left : left + 128] = low
            result = dot3(t_high[...], t_low[...], d_high[...], d_low[...], NN).astype(BF16)
            z = step * 4 + c
            for q in range(2):
                field[z, 0:GRID, q * 256 : q * 256 + 256] = result[q * GRID : q * GRID + GRID]
                field[z, GRID : GRID + 16, q * 256 : q * 256 + 256] = result[
                    q * GRID : q * GRID + 16
                ]
            return carry

        lax.fori_loop(0, 4, one_z, 0)

    out[...] = jnp.zeros_like(out)
    base_z = (place[0] * 16).astype(F32)
    x_cell = lax.broadcasted_iota(jnp.int32, (WINDOW, BLOCK), 0).astype(F32)
    y_cell = lax.broadcasted_iota(jnp.int32, (GRID, BLOCK), 0).astype(F32)
    z_cell = lax.broadcasted_iota(jnp.int32, (16, BLOCK), 0).astype(F32) + base_z

    def one_owner(owner, carry):
        block = field[:, pl.ds(pl.multiple_of(owner * 32, 16), WINDOW), :]
        window[...] = block.reshape(16 * WINDOW, 512).T
        base_x = (owner * 32).astype(F32)

        def one_block(start):
            start = pl.multiple_of(start, BLOCK)
            data = particles[owner, :, pl.ds(start, BLOCK)]
            weight_x = weight(x_cell + base_x - data[0:1], data[3:4])
            weight_z = weight(wrapped(z_cell - data[2:3]), data[5:6])
            live = data[6:7]
            plane = jnp.concatenate(
                [(weight_x * weight_z[z : z + 1] * live).astype(BF16) for z in range(16)], axis=0
            )
            summed = lax.dot_general(window[...], plane, NN, preferred_element_type=F32)
            weight_y = weight(wrapped(y_cell - data[1:2]), data[4:5])
            w_high, w_low = split(weight_y)
            phases = dot3(y_high[...], y_low[...], w_high, w_low, NN)
            summed = summed.reshape(2, 8, 32, BLOCK)
            product = summed[0] * phases[None, 0:32] + summed[1] * phases[None, 32:64]
            out[owner, :, pl.ds(start, BLOCK)] = jnp.sum(product, axis=1)

        def own_block(index, carry):
            one_block(index * BLOCK)
            return carry

        def ghost_block(index, carry):
            one_block(OWN + index * BLOCK)
            return carry

        lax.fori_loop(0, (place[2 + owner] + BLOCK - 1) // BLOCK, own_block, 0)
        lax.fori_loop(0, (place[10 + owner] + BLOCK - 1) // BLOCK, ghost_block, 0)
        return carry

    lax.fori_loop(0, N_GY, one_owner, 0)


def field_stage(place, received, t_high, t_low, y_high, y_low, particles):
    def whole(shape):
        return pl.BlockSpec(
            shape, lambda i, _: (0,) * len(shape), pipeline_mode=pl.Buffered(1)
        )

    return pl.pallas_call(
        field_kernel,
        out_shape=jax.ShapeDtypeStruct((N_GY, 8, ROWS), F32),
        grid_spec=pltpu.PrefetchScalarGridSpec(
            num_scalar_prefetch=1,
            grid=(1,),
            in_specs=[
                whole((GRID * 40, 128)),
                whole((512, 512)),
                whole((512, 512)),
                whole((64, GRID)),
                whole((64, GRID)),
                whole((N_GY, 8, ROWS)),
            ],
            out_specs=whole((N_GY, 8, ROWS)),
            scratch_shapes=[
                pltpu.VMEM((16, GRID + 16, 512), BF16),
                pltpu.VMEM((512, 256), BF16),
                pltpu.VMEM((512, 256), BF16),
                pltpu.VMEM((512, 16 * WINDOW), BF16),
            ],
        ),
        name="field_stage",
    )(place, received, t_high, t_low, y_high, y_low, particles)


def ghost_kernel(values, slots, own, back):
    total = values[0]
    for source in range(1, N_GY):
        total = total + values[source]
    own[...] = total[:, :OWN]
    ghosts = total[:, OWN:]
    cell = lax.broadcasted_iota(jnp.int32, (OWN, GHOST), 0)
    chosen = (cell == slots[...]).astype(F32).astype(BF16)
    first, rest = split(ghosts)
    second, third = split(ghosts - first.astype(F32))
    parts = jnp.concatenate([first.astype(F32), second.astype(F32), third.astype(F32)], axis=0)
    placed = lax.dot_general(parts.astype(BF16), chosen, NT, preferred_element_type=F32)
    back[...] = placed[0:8] + (placed[8:16] + placed[16:24])


def ghost_stage(values, slots):
    return pl.pallas_call(
        ghost_kernel,
        out_shape=(
            jax.ShapeDtypeStruct((8, OWN), F32),
            jax.ShapeDtypeStruct((8, OWN), F32),
        ),
        name="ghost_stage",
    )(values, slots)


def per_device(
    source_hat, particle_start, particle_offset, ghost_start, ghost_offset, ghost_slot, counts
):
    index_gx = lax.axis_index("gx").astype(jnp.int32)
    index_gy = lax.axis_index("gy").astype(jnp.int32)
    index = jnp.arange(OWN, dtype=jnp.int32)
    own_live = (index < counts[0, 0]).astype(F32)
    ghost_live = (index[:GHOST] < counts[0, 2]).astype(F32)
    column = jnp.arange(ROWS, dtype=jnp.int32)
    count_row = jnp.where(
        column == 0, counts[0, 0], jnp.where(column == 1, counts[0, 2], 0)
    ).astype(F32)
    mine = jnp.concatenate(
        [
            jnp.concatenate([particle_start.astype(F32), ghost_start[:, 1].astype(F32)], axis=1),
            jnp.concatenate([particle_offset, ghost_offset[:, 1]], axis=1),
            jnp.concatenate([own_live, ghost_live])[None],
            count_row[None],
        ],
        axis=0,
    )
    copies = jnp.broadcast_to(mine[None], (N_GY, 8, ROWS))
    particles = lax.all_to_all(copies, "gy", split_axis=0, concat_axis=0, tiled=True)
    live_counts = particles[:, 7, 0:2].astype(jnp.int32)
    here = jnp.stack([index_gx, index_gy])
    place = jnp.concatenate([here, live_counts[:, 0], live_counts[:, 1]])

    z_high, z_low = numpy_halves(z_table())
    x_high, x_low = numpy_halves(x_table())
    y_high, y_low = numpy_halves(y_table())
    sent = z_stage(here, source_hat, jnp.asarray(z_high), jnp.asarray(z_low))
    received = lax.all_to_all(sent, "gx", split_axis=0, concat_axis=0, tiled=True)
    received = received.reshape(GRID * 40, 128)
    y_high = lax.dynamic_index_in_dim(jnp.asarray(y_high), index_gy, 0, keepdims=False)
    y_low = lax.dynamic_index_in_dim(jnp.asarray(y_low), index_gy, 0, keepdims=False)
    partial = field_stage(
        place, received, jnp.asarray(x_high), jnp.asarray(x_low), y_high, y_low, particles
    )
    partial = lax.all_to_all(partial, "gy", split_axis=0, concat_axis=0, tiled=True)
    own, back = ghost_stage(partial, ghost_slot[1:2])
    devices = range(lax.axis_size("gx"))
    route = [((i + 1) % len(devices), i) for i in devices]
    totals = own + lax.ppermute(back, "gx", route)
    return (totals[:3], totals[3:])


def solution(mesh):
    in_specs = (
        P(None, None, "gx", "gy", None),
        P(None, ("gx", "gy")),
        P(None, ("gx", "gy")),
        P(None, None, ("gx", "gy")),
        P(None, None, ("gx", "gy")),
        P(None, ("gx", "gy")),
        P(("gx", "gy"), None),
    )
    out_specs = (P(None, ("gx", "gy")), P(None, ("gx", "gy")))
    return jax.shard_map(
        per_device, mesh=mesh, in_specs=in_specs, out_specs=out_specs, check_vma=False
    )
```

```python
import math

import jax
import jax.numpy as jnp
import numpy as np
from jax import lax
from jax.experimental import pallas as pl
from jax.experimental.pallas import tpu as pltpu
from jax.sharding import PartitionSpec as P

F32 = jnp.float32
BF16 = jnp.bfloat16
SUPPORT = 8
GRID = 256
HALF = GRID // 2
N_GX = 16
N_GY = 8
OWN = 2048
GHOST = 512
ROWS = OWN + GHOST
WAVE = 2.0 * math.pi / GRID
WINDOW = 48
BLOCK = 256
CHUNKS = ((0, 1, 2, 3),)
EXTRA = 4


def numpy_halves(table):
    import ml_dtypes

    high = table.astype(ml_dtypes.bfloat16)
    low = (table - high.astype(np.float64)).astype(ml_dtypes.bfloat16)
    return high, low


def left_triple(table):
    high, low = numpy_halves(table)
    return np.concatenate([high, high, low], axis=-1)


def z_table():
    c1, slab, part, step = np.meshgrid(
        np.arange(2), np.arange(N_GX), np.arange(2), np.arange(4), indexing="ij"
    )
    position = (8 * slab + 2 * step + c1).reshape(-1, 1)
    part = part.reshape(-1, 1)
    angle = (position * np.arange(HALF)[None, :] % HALF) * (2.0 * np.pi / HALF)
    cosine, sine = np.cos(angle), np.sin(angle)
    from_real = np.where(part == 0, cosine, sine)
    from_imag = np.where(part == 0, -sine, cosine)
    return np.concatenate([from_real, from_imag], axis=1)


def x_table(parity):
    modes = 2 * np.arange(HALF) + parity
    angle = (np.arange(HALF)[:, None] * modes[None, :] % GRID) * (2.0 * np.pi / GRID)
    cosine, sine = np.cos(angle), np.sin(angle)
    return np.block([[cosine, -sine], [sine, cosine]])


def y_table():
    index = np.arange(GRID)
    angle = (index[:, None] * index[None, :] % GRID) * (2.0 * np.pi / GRID)
    cosine = np.cos(angle).reshape(N_GY, 1, GRID // N_GY, GRID)
    sine = -np.sin(angle).reshape(N_GY, 1, GRID // N_GY, GRID)
    return np.concatenate([cosine, sine], axis=1).reshape(N_GY, 2 * (GRID // N_GY), GRID)


def twiddles():
    angle = np.arange(HALF) * (2.0 * np.pi / GRID)
    table = np.stack([np.cos(angle), np.sin(angle)])
    return np.repeat(table[:, None, :], 32, axis=1).astype(np.float32)


def split(value):
    high = value.astype(BF16)
    return high, (value - high.astype(F32)).astype(BF16)


def signed(index):
    return jnp.where(index < GRID // 2, index, index - GRID).astype(F32)


NT = (((1,), (1,)), ((), ()))
NN = (((1,), (0,)), ((), ()))


def dot(a, b, dims):
    return lax.dot_general(a, b, dims, preferred_element_type=F32)


def z_kernel(pieces, place, source, table, twiddle, out, even, odd):
    quad = pl.program_id(0)
    with_extra = EXTRA in pieces
    parities = [p for p in range(2) if with_extra or any(c % 2 == p for c in pieces)]
    row = lax.broadcasted_iota(jnp.int32, (32, GRID), 0)
    mode_y = signed(row + place[1] * 32)
    mode_z = signed(lax.broadcasted_iota(jnp.int32, (32, GRID), 1))
    wave_z = WAVE * mode_z
    partial_square = mode_y * mode_y + mode_z * mode_z
    turn_re, turn_im = twiddle[0], twiddle[1]
    for k in range(4):
        index_x = place[0] * 16 + quad * 4 + k
        mode_x = jnp.where(index_x < GRID // 2, index_x, index_x - GRID).astype(F32)
        inverse = 1.0 / jnp.maximum(mode_x * mode_x + partial_square, 1.0)
        v = []
        for r in range(2):
            s1, s2, s3 = source[r, 0, k], source[r, 1, k], source[r, 2, k]
            ratio = (s1 * mode_x + s2 * mode_y + s3 * mode_z) * inverse
            v.append((s1 - mode_x * ratio, s2 - mode_y * ratio, s3 - mode_z * ratio))
        rows = [
            (v[0][0], v[1][0], k * 128),
            (v[0][1], v[1][1], k * 128 + 32),
            (v[0][2], v[1][2], k * 128 + 64),
            (-wave_z * v[1][0], wave_z * v[0][0], k * 128 + 96),
        ]
        if with_extra:
            rows.append((-wave_z * v[1][1], wave_z * v[0][1], 512 + k * 32))
        for real, imag, start in rows:
            here = slice(start, start + 32)
            for p in parities:
                if p == 0:
                    re = real[:, :HALF] + real[:, HALF:]
                    im = imag[:, :HALF] + imag[:, HALF:]
                    target = even
                else:
                    re0 = real[:, :HALF] - real[:, HALF:]
                    im0 = imag[:, :HALF] - imag[:, HALF:]
                    re = re0 * turn_re - im0 * turn_im
                    im = re0 * turn_im + im0 * turn_re
                    target = odd
                for r, value in ((0, re), (1, im)):
                    high, low = split(value)
                    target[here, r * HALF : (r + 1) * HALF] = high
                    target[here, GRID + r * HALF : GRID + (r + 1) * HALF] = low
                    target[here, 2 * GRID + r * HALF : 2 * GRID + (r + 1) * HALF] = high

    for p in parities:
        data = (even, odd)[p]
        wanted = [c for c in pieces if c != EXTRA and c % 2 == p]
        if not wanted:
            continue
        c_low, c_high = min(wanted) // 2, max(wanted) // 2 + 1
        for pair in range(2):
            result = dot(
                table[c_low * 128 : c_high * 128], data[pair * 256 : pair * 256 + 256], NT
            )
            for c in wanted:
                top = (c // 2 - c_low) * 128
                for side in range(2):
                    out[:, pieces.index(c), pair * 2 + side] = result[
                        top : top + 128, side * 128 : side * 128 + 128
                    ].reshape(N_GX, 8, 128)
    if with_extra:
        halves = [dot(table[...], data[512:640], NT) for data in (even, odd)]
        v = [halves[c % 2][(c // 2) * 128 : (c // 2) * 128 + 128] for c in range(4)]
        lane = lax.broadcasted_iota(jnp.int32, (128, 128), 1)
        lower64 = lane < 64
        lower32 = (lane & 32) == 0
        p0 = [jnp.where(lower64, v[c], pltpu.roll(v[c + 2], 64, 1)) for c in range(2)]
        p1 = [jnp.where(lower64, pltpu.roll(v[c], 64, 1), v[c + 2]) for c in range(2)]
        place_of = pieces.index(EXTRA)
        for k1, p in ((0, p0), (1, p1)):
            q0 = jnp.where(lower32, p[0], pltpu.roll(p[1], 32, 1))
            q1 = jnp.where(lower32, pltpu.roll(p[0], 96, 1), p[1])
            out[:, place_of, 2 * k1] = q0.reshape(N_GX, 8, 128)
            out[:, place_of, 2 * k1 + 1] = q1.reshape(N_GX, 8, 128)


def z_stage(pieces, place, source, table, twiddle):
    def kernel(*refs):
        z_kernel(pieces, *refs)

    return pl.pallas_call(
        kernel,
        out_shape=jax.ShapeDtypeStruct((N_GX, len(pieces), 16, 8, 128), F32),
        grid_spec=pltpu.PrefetchScalarGridSpec(
            num_scalar_prefetch=1,
            grid=(4,),
            in_specs=[
                pl.BlockSpec((2, 3, 4, 32, GRID), lambda i, _: (0, 0, i, 0, 0)),
                pl.BlockSpec((256, 768), lambda i, _: (0, 0)),
                pl.BlockSpec((2, 32, HALF), lambda i, _: (0, 0, 0)),
            ],
            out_specs=pl.BlockSpec(
                (N_GX, len(pieces), 4, 8, 128), lambda i, _: (0, 0, i, 0, 0)
            ),
            scratch_shapes=[pltpu.VMEM((640, 768), BF16), pltpu.VMEM((640, 768), BF16)],
        ),
        name="z_stage",
    )(place, source, table, twiddle)


def weight(distance, offset):
    shifted = distance - (SUPPORT // 2 - 1) - offset
    inside = (distance >= 0.0) & (distance < SUPPORT)
    return jnp.where(inside, jnp.exp(-5.6 / SUPPORT * shifted * shifted), 0.0)


def wrapped(distance):
    return jnp.where(distance < 0.0, distance + GRID, distance)


def gather_kernel(counts, after, start, offset, other_start, other_offset, out):
    own, ghosts = counts[0, 0], counts[0, 2]
    out[0:3, :OWN] = start[...].astype(F32)
    out[3:6, :OWN] = offset[...]
    out[0:3, OWN:] = other_start[...].astype(F32)
    out[3:6, OWN:] = other_offset[...]
    lane = lax.broadcasted_iota(jnp.int32, (1, ROWS), 1)
    bound = jnp.where(lane < OWN, own, OWN + ghosts)
    out[6:7, :] = jnp.where(lane < bound, 1.0, 0.0)
    out[7:8, :] = jnp.where(lane == 0, own, jnp.where(lane == 1, ghosts, 0)).astype(F32)


def gather_stage(counts, after, start, offset, other_start, other_offset):
    vmem = pl.BlockSpec(memory_space=pltpu.VMEM)
    return pl.pallas_call(
        gather_kernel,
        out_shape=jax.ShapeDtypeStruct((8, ROWS), F32),
        in_specs=[
            pl.BlockSpec(memory_space=pltpu.SMEM),
            pl.BlockSpec(memory_space=pl.ANY),
            vmem,
            vmem,
            vmem,
            vmem,
        ],
        out_specs=vmem,
        name="gather_stage",
    )(counts, after, start, offset, other_start, other_offset)


def for_live_blocks(place, owner, body):
    def own_block(index, carry):
        body(pl.multiple_of(index * BLOCK, BLOCK))
        return carry

    def ghost_block(index, carry):
        body(pl.multiple_of(OWN + index * BLOCK, BLOCK))
        return carry

    lax.fori_loop(0, (place[2 + owner] + BLOCK - 1) // BLOCK, own_block, 0)
    lax.fori_loop(0, (place[10 + owner] + BLOCK - 1) // BLOCK, ghost_block, 0)


def row_kernel(place, particles, table, phases):
    y_cell = lax.broadcasted_iota(jnp.int32, (GRID, BLOCK), 0).astype(F32)

    def one_block(start):
        data = particles[0, :, pl.ds(start, BLOCK)]
        weight_y = weight(wrapped(y_cell - data[1:2]), data[4:5])
        high, low = split(weight_y)
        phases[0, :, pl.ds(start, BLOCK)] = dot(
            table[...], jnp.concatenate([high, low, high], axis=0), NN
        )

    for_live_blocks(place, pl.program_id(0), one_block)


def row_stage(place, particles, table):
    return pl.pallas_call(
        row_kernel,
        out_shape=jax.ShapeDtypeStruct((N_GY, 64, ROWS), F32),
        grid_spec=pltpu.PrefetchScalarGridSpec(
            num_scalar_prefetch=1,
            grid=(N_GY,),
            in_specs=[
                pl.BlockSpec((1, 8, ROWS), lambda i, _: (i, 0, 0)),
                pl.BlockSpec((64, 768), lambda i, _: (0, 0)),
            ],
            out_specs=pl.BlockSpec((1, 64, ROWS), lambda i, _: (i, 0, 0)),
        ),
        name="row_stage",
    )(place, particles, table)


def field_kernel(
    steps, place, main, extra, t_even, t_odd, particles, phases_in, *rest
):
    if len(rest) == 8:
        previous, out, field, d_even, d_odd, window, phases, arrival = rest
    else:
        previous = None
        out, field, d_even, d_odd, window, phases, arrival = rest
    first_c = steps[0]
    step_c = pl.program_id(0)
    c = first_c + step_c
    copy = pltpu.make_async_copy(phases_in, phases, arrival)

    @pl.when(step_c == 0)
    def _():
        copy.start()

    lane = lax.broadcasted_iota(jnp.int32, (HALF, 128), 1)
    group = lane // 32
    row = lax.broadcasted_iota(jnp.int32, (HALF, 128), 0)
    wave_y = WAVE * signed(lane % 32 + place[1] * 32)
    last_group = group == 3
    on_left = jnp.where(group == 0, wave_y, 0.0)
    on_right = jnp.where((group == 1) | last_group, 0.5 * wave_y, 0.0)
    half_same = jnp.where((group == 1) | (group == 2), 0.5, 0.0)
    half_left = jnp.where(group == 2, 0.5, 0.0)
    half_extra = jnp.where(last_group, 0.5, 0.0)
    flat_main = main.reshape(GRID * 8, 128)
    flat_extra = extra.reshape(GRID * 8, 128)

    def one_z(step, carry):
        for parity, target in ((0, d_even), (1, d_odd)):
            wave_x = WAVE * signed(2 * row + parity)

            def load(flat, q):
                return flat[pl.ds(parity * 8 + q * 4 + step, HALF, stride=16), :]

            parts = []
            for q in range(2):
                value = load(flat_main, q)
                moved = pltpu.roll(load(flat_extra, q), 32 * (3 - c), 1)
                parts.append((value, pltpu.roll(value, 96, 1), pltpu.roll(value, 32, 1), moved))
            (a_re, l_re, r_re, e_re), (a_im, l_im, r_im, e_im) = parts
            on_same = half_same * wave_x
            first_re = jnp.where(last_group, -wave_x * l_im, a_re)
            first_im = jnp.where(last_group, wave_x * l_re, a_im)
            second_re = (half_left * l_re + half_extra * e_re) - (
                on_left * l_im + on_right * r_im + on_same * a_im
            )
            second_im = (half_left * l_im + half_extra * e_im) + (
                on_left * l_re + on_right * r_re + on_same * a_re
            )
            for top, left, value in (
                (0, 0, first_re),
                (HALF, 0, first_im),
                (0, 128, second_re),
                (HALF, 128, second_im),
            ):
                high, low = split(value)
                lanes = slice(left, left + 128)
                target[top : top + HALF, lanes] = high
                target[GRID + top : GRID + top + HALF, lanes] = low
                target[2 * GRID + top : 2 * GRID + top + HALF, lanes] = high
        from_even = dot(t_even[...], d_even[...], NN)
        from_odd = dot(t_odd[...], d_odd[...], NN)
        near = (from_even + from_odd).astype(BF16)
        far = (from_even - from_odd).astype(BF16)
        z = step_c * 4 + step
        for q in range(2):
            lanes = slice(q * 256, q * 256 + 256)
            field[z, 0:HALF, lanes] = near[q * HALF : q * HALF + HALF]
            field[z, HALF:GRID, lanes] = far[q * HALF : q * HALF + HALF]
            field[z, GRID : GRID + 16, lanes] = near[q * HALF : q * HALF + 16]
        return carry

    lax.fori_loop(0, 4, one_z, 0)

    @pl.when(step_c == len(steps) - 1)
    def _():
        if previous is None:
            out[...] = jnp.zeros_like(out)
        else:
            out[...] = previous[...]
        copy.wait()
        planes = 4 * len(steps)
        x_cell = lax.broadcasted_iota(jnp.int32, (WINDOW, BLOCK), 0).astype(F32)
        local_z = lax.broadcasted_iota(jnp.int32, (planes, BLOCK), 0)
        z_cell = (place[0] * 16 + first_c + 4 * (local_z % 4) + local_z // 4).astype(F32)

        def one_owner(index, carry):
            owner = (place[1] - index) & (N_GY - 1)
            block = field[:, pl.ds(pl.multiple_of(owner * 32, 16), WINDOW), :]
            window[...] = block.reshape(planes * WINDOW, 512).T
            base_x = (owner * 32).astype(F32)

            def one_block(start):
                data = particles[index, :, pl.ds(start, BLOCK)]
                weight_x = weight(x_cell + base_x - data[0:1], data[3:4])
                weight_z = weight(wrapped(z_cell - data[2:3]), data[5:6]) * data[6:7]
                plane = jnp.concatenate(
                    [(weight_x * weight_z[z : z + 1]).astype(BF16) for z in range(planes)], axis=0
                )
                summed = dot(window[...], plane, NN).reshape(2, 8, 32, BLOCK)
                phase = phases[index, :, pl.ds(start, BLOCK)]
                product = summed[0] * phase[None, 0:32] + summed[1] * phase[None, 32:64]
                value = jnp.sum(product, axis=1)
                if previous is not None:
                    value = value + out[owner, :, pl.ds(start, BLOCK)]
                out[owner, :, pl.ds(start, BLOCK)] = value

            for_live_blocks(place, index, one_block)
            return carry

        lax.fori_loop(0, N_GY, one_owner, 0)


def field_stage(steps, first, place, main, extra, extra_at, t_even, t_odd, particles, phases, previous):
    def whole(shape):
        return pl.BlockSpec(
            shape, lambda i, _: (0,) * len(shape), pipeline_mode=pl.Buffered(1)
        )

    def kernel(*refs):
        field_kernel(steps, *refs)

    piece = (N_GX, None, 16, 8, 128)
    in_specs = [
        pl.BlockSpec(piece, lambda i, _: (0, first + i, 0, 0, 0)),
        pl.BlockSpec(piece, lambda i, _: (0, extra_at, 0, 0, 0)),
        whole((256, 768)),
        whole((256, 768)),
        whole((N_GY, 8, ROWS)),
        pl.BlockSpec(memory_space=pl.ANY),
    ]
    operands = [place, main, extra, t_even, t_odd, particles, phases]
    if previous is not None:
        in_specs.append(whole((N_GY, 8, ROWS)))
        operands.append(previous)
    planes = 4 * len(steps)
    return pl.pallas_call(
        kernel,
        out_shape=jax.ShapeDtypeStruct((N_GY, 8, ROWS), F32),
        grid_spec=pltpu.PrefetchScalarGridSpec(
            num_scalar_prefetch=1,
            grid=(len(steps),),
            in_specs=in_specs,
            out_specs=whole((N_GY, 8, ROWS)),
            scratch_shapes=[
                pltpu.VMEM((planes, GRID + 16, 512), BF16),
                pltpu.VMEM((768, 256), BF16),
                pltpu.VMEM((768, 256), BF16),
                pltpu.VMEM((512, planes * WINDOW), BF16),
                pltpu.VMEM((N_GY, 64, ROWS), F32),
                pltpu.SemaphoreType.DMA,
            ],
        ),
        name="field_stage",
    )(*operands)


def ghost_kernel(values, slots, own, back):
    total = values[0]
    for source in range(1, N_GY):
        total = total + values[source]
    own[...] = total[:, :OWN]
    ghosts = total[:, OWN:]
    cell = lax.broadcasted_iota(jnp.int32, (OWN, GHOST), 0)
    chosen = (cell == slots[...]).astype(F32).astype(BF16)
    first, rest = split(ghosts)
    second, third = split(ghosts - first.astype(F32))
    parts = jnp.concatenate([first.astype(F32), second.astype(F32), third.astype(F32)], axis=0)
    placed = dot(parts.astype(BF16), chosen, NT)
    back[...] = placed[0:8] + (placed[8:16] + placed[16:24])


def ghost_stage(values, slots):
    return pl.pallas_call(
        ghost_kernel,
        out_shape=(
            jax.ShapeDtypeStruct((8, OWN), F32),
            jax.ShapeDtypeStruct((8, OWN), F32),
        ),
        name="ghost_stage",
    )(values, slots)


def final_kernel(own, arrived, velocity, strain):
    total = own[...] + arrived[...]
    velocity[...] = total[:3]
    strain[...] = total[3:]


def final_stage(own, arrived):
    return pl.pallas_call(
        final_kernel,
        out_shape=(
            jax.ShapeDtypeStruct((3, OWN), F32),
            jax.ShapeDtypeStruct((5, OWN), F32),
        ),
        name="final_stage",
    )(own, arrived)


def per_device(
    source_hat, particle_start, particle_offset, ghost_start, ghost_offset, ghost_slot, counts
):
    index_gx = lax.axis_index("gx").astype(jnp.int32)
    index_gy = lax.axis_index("gy").astype(jnp.int32)
    here = jnp.stack([index_gx, index_gy])

    table_z = jnp.asarray(left_triple(z_table()))
    twiddle = jnp.asarray(twiddles())
    sent = [
        z_stage(chunk + ((EXTRA,) if number == 0 else ()), here, source_hat, table_z, twiddle)
        for number, chunk in enumerate(CHUNKS)
    ]
    received = [
        lax.all_to_all(piece, "gx", split_axis=0, concat_axis=0, tiled=True) for piece in sent
    ]

    mine = gather_stage(
        counts, sent[0], particle_start, particle_offset, ghost_start[:, 1], ghost_offset[:, 1]
    )
    members = range(N_GY)
    particles = jnp.stack(
        [mine]
        + [
            lax.ppermute(mine, "gy", [(i, (i + shift) % N_GY) for i in members])
            for shift in range(1, N_GY)
        ]
    )
    live_counts = particles[:, 7, 0:2].astype(jnp.int32)
    place = jnp.concatenate([here, live_counts[:, 0], live_counts[:, 1]])
    table_y = jnp.asarray(left_triple(y_table()))
    table_y = lax.dynamic_index_in_dim(table_y, index_gy, 0, keepdims=False)
    phases = row_stage(place, particles, table_y)

    t_even = jnp.asarray(left_triple(x_table(0)))
    t_odd = jnp.asarray(left_triple(x_table(1)))
    partial = None
    for number, chunk in enumerate(CHUNKS):
        partial = field_stage(
            chunk, 0, place, received[number], received[0], len(CHUNKS[0]),
            t_even, t_odd, particles, phases, partial,
        )
    partial = lax.all_to_all(partial, "gy", split_axis=0, concat_axis=0, tiled=True)
    own, back = ghost_stage(partial, ghost_slot[1:2])
    devices = range(N_GX)
    route = [((i + 1) % N_GX, i) for i in devices]
    return final_stage(own, lax.ppermute(back, "gx", route))


def solution(mesh):
    in_specs = (
        P(None, None, "gx", "gy", None),
        P(None, ("gx", "gy")),
        P(None, ("gx", "gy")),
        P(None, None, ("gx", "gy")),
        P(None, None, ("gx", "gy")),
        P(None, ("gx", "gy")),
        P(("gx", "gy"), None),
    )
    out_specs = (P(None, ("gx", "gy")), P(None, ("gx", "gy")))
    return jax.shard_map(
        per_device, mesh=mesh, in_specs=in_specs, out_specs=out_specs, check_vma=False
    )
```

```python
import math

import jax
import jax.numpy as jnp
import numpy as np
from jax import lax
from jax.experimental import pallas as pl
from jax.experimental.pallas import tpu as pltpu
from jax.sharding import PartitionSpec as P

F32 = jnp.float32
BF16 = jnp.bfloat16
SUPPORT = 8
GRID = 256
HALF = GRID // 2
N_GX = 16
N_GY = 8
OWN = 2048
GHOST = 512
ROWS = OWN + GHOST
WAVE = 2.0 * math.pi / GRID
WINDOW = 48
BLOCK = 256
CHUNKS = ((0, 1, 2, 3),)
EXTRA = 4


def numpy_halves(table):
    import ml_dtypes

    high = table.astype(ml_dtypes.bfloat16)
    low = (table - high.astype(np.float64)).astype(ml_dtypes.bfloat16)
    return high, low


def left_triple(table):
    high, low = numpy_halves(table)
    return np.concatenate([high, high, low], axis=-1)


def z_table():
    c1, slab, part, step = np.meshgrid(
        np.arange(2), np.arange(N_GX), np.arange(2), np.arange(4), indexing="ij"
    )
    position = (8 * slab + 2 * step + c1).reshape(-1, 1)
    part = part.reshape(-1, 1)
    angle = (position * np.arange(HALF)[None, :] % HALF) * (2.0 * np.pi / HALF)
    cosine, sine = np.cos(angle), np.sin(angle)
    from_real = np.where(part == 0, cosine, sine)
    from_imag = np.where(part == 0, -sine, cosine)
    return np.concatenate([from_real, from_imag], axis=1)


def x_table(parity):
    modes = 2 * np.arange(HALF) + parity
    angle = (np.arange(HALF)[:, None] * modes[None, :] % GRID) * (2.0 * np.pi / GRID)
    cosine, sine = np.cos(angle), np.sin(angle)
    return np.block([[cosine, -sine], [sine, cosine]])


def y_table():
    index = np.arange(GRID)
    angle = (index[:, None] * index[None, :] % GRID) * (2.0 * np.pi / GRID)
    cosine = np.cos(angle).reshape(N_GY, 1, GRID // N_GY, GRID)
    sine = -np.sin(angle).reshape(N_GY, 1, GRID // N_GY, GRID)
    return np.concatenate([cosine, sine], axis=1).reshape(N_GY, 2 * (GRID // N_GY), GRID)


def twiddles():
    angle = np.arange(HALF) * (2.0 * np.pi / GRID)
    table = np.stack([np.cos(angle), np.sin(angle)])
    return np.repeat(table[:, None, :], 32, axis=1).astype(np.float32)


def split(value):
    high = value.astype(BF16)
    return high, (value - high.astype(F32)).astype(BF16)


def signed(index):
    return jnp.where(index < GRID // 2, index, index - GRID).astype(F32)


NT = (((1,), (1,)), ((), ()))
NN = (((1,), (0,)), ((), ()))


def dot(a, b, dims):
    return lax.dot_general(a, b, dims, preferred_element_type=F32)


def z_kernel(pieces, source, table, twiddle, out, even, odd):
    quad = pl.program_id(0)
    with_extra = EXTRA in pieces
    parities = [p for p in range(2) if with_extra or any(c % 2 == p for c in pieces)]
    row = lax.broadcasted_iota(jnp.int32, (32, GRID), 0)
    mode_y = signed(row + lax.axis_index("gy") * 32)
    mode_z = signed(lax.broadcasted_iota(jnp.int32, (32, GRID), 1))
    half_wave_z = 0.5 * WAVE * mode_z
    partial_square = mode_y * mode_y + mode_z * mode_z
    turn_re, turn_im = twiddle[0], twiddle[1]
    for k in range(4):
        index_x = lax.axis_index("gx") * 16 + quad * 4 + k
        mode_x = jnp.where(index_x < GRID // 2, index_x, index_x - GRID).astype(F32)
        inverse = 1.0 / jnp.maximum(mode_x * mode_x + partial_square, 1.0)
        v = []
        for r in range(2):
            s1, s2, s3 = source[r, 0, k], source[r, 1, k], source[r, 2, k]
            ratio = (s1 * mode_x + s2 * mode_y + s3 * mode_z) * inverse
            v.append((s1 - mode_x * ratio, s2 - mode_y * ratio, s3 - mode_z * ratio))
        rows = [
            (v[0][0], v[1][0], k * 128),
            (v[0][1], v[1][1], k * 128 + 32),
            (v[0][2], v[1][2], k * 128 + 64),
            (-half_wave_z * v[1][0], half_wave_z * v[0][0], k * 128 + 96),
        ]
        if with_extra:
            rows.append((-half_wave_z * v[1][1], half_wave_z * v[0][1], 512 + k * 32))
        for real, imag, start in rows:
            here = slice(start, start + 32)
            for p in parities:
                if p == 0:
                    re = real[:, :HALF] + real[:, HALF:]
                    im = imag[:, :HALF] + imag[:, HALF:]
                    target = even
                else:
                    re0 = real[:, :HALF] - real[:, HALF:]
                    im0 = imag[:, :HALF] - imag[:, HALF:]
                    re = re0 * turn_re - im0 * turn_im
                    im = re0 * turn_im + im0 * turn_re
                    target = odd
                for r, value in ((0, re), (1, im)):
                    high, low = split(value)
                    target[here, r * HALF : (r + 1) * HALF] = high
                    target[here, GRID + r * HALF : GRID + (r + 1) * HALF] = low
                    target[here, 2 * GRID + r * HALF : 2 * GRID + (r + 1) * HALF] = high

    for p in parities:
        data = (even, odd)[p]
        wanted = [c for c in pieces if c != EXTRA and c % 2 == p]
        if not wanted:
            continue
        c_low, c_high = min(wanted) // 2, max(wanted) // 2 + 1
        for pair in range(2):
            result = dot(
                table[c_low * 128 : c_high * 128], data[pair * 256 : pair * 256 + 256], NT
            )
            for c in wanted:
                top = (c // 2 - c_low) * 128
                for side in range(2):
                    out[:, pieces.index(c), pair * 2 + side] = result[
                        top : top + 128, side * 128 : side * 128 + 128
                    ].reshape(N_GX, 8, 128)
    if with_extra:
        halves = [dot(table[...], data[512:640], NT) for data in (even, odd)]
        v = [halves[c % 2][(c // 2) * 128 : (c // 2) * 128 + 128] for c in range(4)]
        lane = lax.broadcasted_iota(jnp.int32, (128, 128), 1)
        lower64 = lane < 64
        lower32 = (lane & 32) == 0
        p0 = [jnp.where(lower64, v[c], pltpu.roll(v[c + 2], 64, 1)) for c in range(2)]
        p1 = [jnp.where(lower64, pltpu.roll(v[c], 64, 1), v[c + 2]) for c in range(2)]
        place_of = pieces.index(EXTRA)
        for k1, p in ((0, p0), (1, p1)):
            q0 = jnp.where(lower32, p[0], pltpu.roll(p[1], 32, 1))
            q1 = jnp.where(lower32, pltpu.roll(p[0], 96, 1), p[1])
            out[:, place_of, 2 * k1] = q0.reshape(N_GX, 8, 128)
            out[:, place_of, 2 * k1 + 1] = q1.reshape(N_GX, 8, 128)


def z_stage(pieces, source, table, twiddle):
    def kernel(*refs):
        z_kernel(pieces, *refs)

    return pl.pallas_call(
        kernel,
        out_shape=jax.ShapeDtypeStruct((N_GX, len(pieces), 16, 8, 128), F32),
        grid=(4,),
        in_specs=[
            pl.BlockSpec((2, 3, 4, 32, GRID), lambda i: (0, 0, i, 0, 0)),
            pl.BlockSpec((256, 768), lambda i: (0, 0)),
            pl.BlockSpec((2, 32, HALF), lambda i: (0, 0, 0)),
        ],
        out_specs=pl.BlockSpec((N_GX, len(pieces), 4, 8, 128), lambda i: (0, 0, i, 0, 0)),
        scratch_shapes=[pltpu.VMEM((640, 768), BF16), pltpu.VMEM((640, 768), BF16)],
        name="z_stage",
    )(source, table, twiddle)


def weight(distance, offset):
    shifted = distance - (SUPPORT // 2 - 1) - offset
    inside = (distance >= 0.0) & (distance < SUPPORT)
    return jnp.where(inside, jnp.exp(-5.6 / SUPPORT * shifted * shifted), 0.0)


def wrapped(distance):
    return jnp.where(distance < 0.0, distance + GRID, distance)


def gather_kernel(counts, start, offset, other_start, other_offset, out):
    own, ghosts = counts[0, 0], counts[0, 2]
    out[0:3, :OWN] = start[...].astype(F32)
    out[3:6, :OWN] = offset[...]
    out[0:3, OWN:] = other_start[:, 1].astype(F32)
    out[3:6, OWN:] = other_offset[:, 1]
    lane = lax.broadcasted_iota(jnp.int32, (1, ROWS), 1)
    bound = jnp.where(lane < OWN, own, OWN + ghosts)
    out[6:7, :] = jnp.where(lane < bound, 1.0, 0.0)
    out[7:8, :] = jnp.where(lane == 0, own, jnp.where(lane == 1, ghosts, 0)).astype(F32)


def gather_stage(counts, start, offset, other_start, other_offset):
    vmem = pl.BlockSpec(memory_space=pltpu.VMEM)
    return pl.pallas_call(
        gather_kernel,
        out_shape=jax.ShapeDtypeStruct((8, ROWS), F32),
        in_specs=[
            pl.BlockSpec(memory_space=pltpu.SMEM),
            vmem,
            vmem,
            vmem,
            vmem,
        ],
        out_specs=vmem,
        name="gather_stage",
    )(counts, start, offset, other_start, other_offset)


def for_live_blocks(place, owner, body):
    def own_block(index, carry):
        body(pl.multiple_of(index * BLOCK, BLOCK))
        return carry

    def ghost_block(index, carry):
        body(pl.multiple_of(OWN + index * BLOCK, BLOCK))
        return carry

    lax.fori_loop(0, (place[2 + owner] + BLOCK - 1) // BLOCK, own_block, 0)
    lax.fori_loop(0, (place[10 + owner] + BLOCK - 1) // BLOCK, ghost_block, 0)


def row_kernel(place, particles, table, phases):
    y_cell = lax.broadcasted_iota(jnp.int32, (GRID, BLOCK), 0).astype(F32)

    def one_block(start):
        data = particles[0, :, pl.ds(start, BLOCK)]
        weight_y = weight(wrapped(y_cell - data[1:2]), data[4:5])
        high, low = split(weight_y)
        phases[0, :, pl.ds(start, BLOCK)] = dot(
            table[...], jnp.concatenate([high, low, high], axis=0), NN
        )

    for_live_blocks(place, pl.program_id(0), one_block)


def row_stage(place, particles, table):
    return pl.pallas_call(
        row_kernel,
        out_shape=jax.ShapeDtypeStruct((N_GY, 64, ROWS), F32),
        grid_spec=pltpu.PrefetchScalarGridSpec(
            num_scalar_prefetch=1,
            grid=(N_GY,),
            in_specs=[
                pl.BlockSpec((1, 8, ROWS), lambda i, _: (i, 0, 0)),
                pl.BlockSpec((64, 768), lambda i, _: (0, 0)),
            ],
            out_specs=pl.BlockSpec((1, 64, ROWS), lambda i, _: (i, 0, 0)),
        ),
        name="row_stage",
    )(place, particles, table)


def field_kernel(
    steps, place, main, extra, t_even, t_odd, particles, phases_in, *rest
):
    previous = rest[0] if len(rest) == 10 else None
    out, field, work0, work1, work2, work3, window, phases, arrival = rest[-9:]
    work = (work0, work1, work2, work3)
    first_c = steps[0]
    step_c = pl.program_id(0)
    c = first_c + step_c
    copy = pltpu.make_async_copy(phases_in, phases, arrival)

    @pl.when(step_c == 0)
    def _():
        copy.start()

    lane = lax.broadcasted_iota(jnp.int32, (HALF, 128), 1)
    group = lane // 32
    row = lax.broadcasted_iota(jnp.int32, (HALF, 128), 0)
    wave_y = WAVE * signed(lane % 32 + place[1] * 32)
    cross_y = jnp.where(group == 0, wave_y, jnp.where(group == 2, 0.0, 0.5 * wave_y))
    half_same = jnp.where((group == 1) | (group == 2), 0.5, 0.0)
    plain_left = group == 2
    plain_extra = group == 3
    cross_left = group == 0
    flat_main = main.reshape(GRID * 8, 128)
    flat_extra = extra.reshape(GRID * 8, 128)
    waves = [WAVE * signed(2 * row + parity) for parity in range(2)]
    for step in range(4):
        results = []
        for parity in range(2):
            target = work[2 * (step % 2) + parity]
            wave_x = waves[parity]
            cross_x = half_same * wave_x

            def load(flat, q):
                return flat[pl.ds(parity * 8 + q * 4 + step, HALF, stride=16), :]

            parts = []
            for q in range(2):
                value = load(flat_main, q)
                moved = pltpu.roll(load(flat_extra, q), 32 * (3 - c), 1)
                left = pltpu.roll(value, 96, 1)
                right = pltpu.roll(value, 32, 1)
                cross = cross_y * jnp.where(cross_left, left, right) + cross_x * value
                plain = jnp.where(plain_left, left, jnp.where(plain_extra, moved, 0.0))
                parts.append((value, wave_x * left, cross, plain))
            (a_re, x_re, c_re, p_re), (a_im, x_im, c_im, p_im) = parts
            for top, left, value in (
                (0, 0, jnp.where(plain_extra, -x_im, a_re)),
                (HALF, 0, jnp.where(plain_extra, x_re, a_im)),
                (0, 128, p_re - c_im),
                (HALF, 128, p_im + c_re),
            ):
                high, low = split(value)
                lanes = slice(left, left + 128)
                target[top : top + HALF, lanes] = high
                target[GRID + top : GRID + top + HALF, lanes] = low
                target[2 * GRID + top : 2 * GRID + top + HALF, lanes] = high
            results.append(dot((t_even, t_odd)[parity][...], target[...], NN))
        from_even, from_odd = results
        near = (from_even + from_odd).astype(BF16)
        far = (from_even - from_odd).astype(BF16)
        z = step_c * 4 + step
        for q in range(2):
            lanes = slice(q * 256, q * 256 + 256)
            field[z, 0:HALF, lanes] = near[q * HALF : q * HALF + HALF]
            field[z, HALF:GRID, lanes] = far[q * HALF : q * HALF + HALF]
            field[z, GRID : GRID + 16, lanes] = near[q * HALF : q * HALF + 16]

    @pl.when(step_c == len(steps) - 1)
    def _():
        if previous is None:
            out[...] = jnp.zeros_like(out)
        else:
            out[...] = previous[...]
        copy.wait()
        planes = 4 * len(steps)
        x_cell = lax.broadcasted_iota(jnp.int32, (WINDOW, BLOCK), 0).astype(F32)
        local_z = lax.broadcasted_iota(jnp.int32, (planes, BLOCK), 0)
        z_cell = (place[0] * 16 + first_c + 4 * (local_z % 4) + local_z // 4).astype(F32)

        def one_owner(index, carry):
            owner = index
            block = field[:, pl.ds(pl.multiple_of(owner * 32, 16), WINDOW), :]
            window[...] = block.reshape(planes * WINDOW, 512).T
            base_x = (owner * 32).astype(F32)

            def one_block(start):
                data = particles[index, :, pl.ds(start, BLOCK)]
                weight_x = weight(x_cell + base_x - data[0:1], data[3:4])
                weight_z = weight(wrapped(z_cell - data[2:3]), data[5:6]) * data[6:7]
                plane = jnp.concatenate(
                    [(weight_x * weight_z[z : z + 1]).astype(BF16) for z in range(planes)], axis=0
                )
                summed = dot(window[...], plane, NN).reshape(2, 8, 32, BLOCK)
                phase = phases[index, :, pl.ds(start, BLOCK)]
                product = summed[0] * phase[None, 0:32] + summed[1] * phase[None, 32:64]
                value = jnp.sum(product, axis=1)
                if previous is not None:
                    value = value + out[owner, :, pl.ds(start, BLOCK)]
                out[owner, :, pl.ds(start, BLOCK)] = value

            for_live_blocks(place, index, one_block)
            return carry

        lax.fori_loop(0, N_GY, one_owner, 0)


def field_stage(steps, first, place, main, extra, extra_at, t_even, t_odd, particles, phases, previous):
    def whole(shape):
        return pl.BlockSpec(
            shape, lambda i, _: (0,) * len(shape), pipeline_mode=pl.Buffered(1)
        )

    def kernel(*refs):
        field_kernel(steps, *refs)

    piece = (N_GX, None, 16, 8, 128)
    in_specs = [
        pl.BlockSpec(piece, lambda i, _: (0, first + i, 0, 0, 0)),
        pl.BlockSpec(piece, lambda i, _: (0, extra_at, 0, 0, 0)),
        whole((256, 768)),
        whole((256, 768)),
        whole((N_GY, 8, ROWS)),
        pl.BlockSpec(memory_space=pl.ANY),
    ]
    operands = [place, main, extra, t_even, t_odd, particles, phases]
    if previous is not None:
        in_specs.append(whole((N_GY, 8, ROWS)))
        operands.append(previous)
    planes = 4 * len(steps)
    return pl.pallas_call(
        kernel,
        out_shape=jax.ShapeDtypeStruct((N_GY, 8, ROWS), F32),
        grid_spec=pltpu.PrefetchScalarGridSpec(
            num_scalar_prefetch=1,
            grid=(len(steps),),
            in_specs=in_specs,
            out_specs=whole((N_GY, 8, ROWS)),
            scratch_shapes=[
                pltpu.VMEM((planes, GRID + 16, 512), BF16),
                pltpu.VMEM((768, 256), BF16),
                pltpu.VMEM((768, 256), BF16),
                pltpu.VMEM((768, 256), BF16),
                pltpu.VMEM((768, 256), BF16),
                pltpu.VMEM((512, planes * WINDOW), BF16),
                pltpu.VMEM((N_GY, 64, ROWS), F32),
                pltpu.SemaphoreType.DMA,
            ],
        ),
        name="field_stage",
    )(*operands)


def ghost_kernel(values, slots, own, back):
    total = values[0]
    for source in range(1, N_GY):
        total = total + values[source]
    own[...] = total[:, :OWN]
    ghosts = total[:, OWN:]
    cell = lax.broadcasted_iota(jnp.int32, (OWN, GHOST), 0)
    chosen = (cell == slots[1:2]).astype(F32).astype(BF16)
    first, rest = split(ghosts)
    second, third = split(ghosts - first.astype(F32))
    parts = jnp.concatenate([first.astype(F32), second.astype(F32), third.astype(F32)], axis=0)
    placed = dot(parts.astype(BF16), chosen, NT)
    back[...] = placed[0:8] + (placed[8:16] + placed[16:24])


def ghost_stage(values, slots):
    return pl.pallas_call(
        ghost_kernel,
        out_shape=(
            jax.ShapeDtypeStruct((8, OWN), F32),
            jax.ShapeDtypeStruct((8, OWN), F32),
        ),
        name="ghost_stage",
    )(values, slots)


def final_kernel(own, arrived, velocity, strain):
    total = own[...] + arrived[...]
    velocity[...] = total[:3]
    strain[...] = total[3:]


def final_stage(own, arrived):
    return pl.pallas_call(
        final_kernel,
        out_shape=(
            jax.ShapeDtypeStruct((3, OWN), F32),
            jax.ShapeDtypeStruct((5, OWN), F32),
        ),
        name="final_stage",
    )(own, arrived)


def per_device(
    source_hat, particle_start, particle_offset, ghost_start, ghost_offset, ghost_slot, counts
):
    index_gx = lax.axis_index("gx").astype(jnp.int32)
    index_gy = lax.axis_index("gy").astype(jnp.int32)
    mine = gather_stage(counts, particle_start, particle_offset, ghost_start, ghost_offset)
    copies = jnp.broadcast_to(mine[None], (N_GY, 8, ROWS))
    particles = lax.all_to_all(copies, "gy", split_axis=0, concat_axis=0, tiled=True)

    table_z = jnp.asarray(left_triple(z_table()))
    twiddle = jnp.asarray(twiddles())
    sent = [
        z_stage(chunk + ((EXTRA,) if number == 0 else ()), source_hat, table_z, twiddle)
        for number, chunk in enumerate(CHUNKS)
    ]
    received = [
        lax.all_to_all(piece, "gx", split_axis=0, concat_axis=0, tiled=True) for piece in sent
    ]

    live_counts = particles[:, 7, 0:2].astype(jnp.int32)
    place = jnp.concatenate(
        [jnp.stack([index_gx, index_gy]), live_counts[:, 0], live_counts[:, 1]]
    )
    table_y = jnp.asarray(left_triple(y_table()))
    table_y = lax.dynamic_index_in_dim(table_y, index_gy, 0, keepdims=False)
    phases = row_stage(place, particles, table_y)

    t_even = jnp.asarray(left_triple(x_table(0)))
    t_odd = jnp.asarray(left_triple(x_table(1)))
    partial = None
    for number, chunk in enumerate(CHUNKS):
        partial = field_stage(
            chunk, 0, place, received[number], received[0], len(CHUNKS[0]),
            t_even, t_odd, particles, phases, partial,
        )
    partial = lax.all_to_all(partial, "gy", split_axis=0, concat_axis=0, tiled=True)
    own, back = ghost_stage(partial, ghost_slot)
    devices = range(N_GX)
    route = [((i + 1) % N_GX, i) for i in devices]
    return final_stage(own, lax.ppermute(back, "gx", route))


def solution(mesh):
    in_specs = (
        P(None, None, "gx", "gy", None),
        P(None, ("gx", "gy")),
        P(None, ("gx", "gy")),
        P(None, None, ("gx", "gy")),
        P(None, None, ("gx", "gy")),
        P(None, ("gx", "gy")),
        P(("gx", "gy"), None),
    )
    out_specs = (P(None, ("gx", "gy")), P(None, ("gx", "gy")))
    return jax.shard_map(
        per_device, mesh=mesh, in_specs=in_specs, out_specs=out_specs, check_vma=False
    )
```

```python
import math

import jax
import jax.numpy as jnp
import numpy as np
from jax import lax
from jax.experimental import pallas as pl
from jax.experimental.pallas import tpu as pltpu
from jax.sharding import PartitionSpec as P


F32 = jnp.float32
BF16 = jnp.bfloat16
SUPPORT = 8
GRID = 256
HALF = GRID // 2
N_GX = 16
N_GY = 8
OWN = 2048
GHOST = 512
ROWS = OWN + GHOST
WAVE = 2.0 * math.pi / GRID
WINDOW = 48
BLOCK = 256
CHUNKS = ((0, 1, 2, 3),)
EXTRA = 4
BLOCKS = ROWS // BLOCK
JOBS = N_GY * BLOCKS + 2
HEAD = 3
AHEAD = 8


def numpy_halves(table):
    import ml_dtypes

    high = table.astype(ml_dtypes.bfloat16)
    low = (table - high.astype(np.float64)).astype(ml_dtypes.bfloat16)
    return high, low


def left_triple(table):
    high, low = numpy_halves(table)
    return np.concatenate([high, high, low], axis=-1)


def z_table():
    c1, slab, part, step = np.meshgrid(
        np.arange(2), np.arange(N_GX), np.arange(2), np.arange(4), indexing="ij"
    )
    position = (8 * slab + 2 * step + c1).reshape(-1, 1)
    part = part.reshape(-1, 1)
    angle = (position * np.arange(HALF)[None, :] % HALF) * (2.0 * np.pi / HALF)
    cosine, sine = np.cos(angle), np.sin(angle)
    from_real = np.where(part == 0, cosine, sine)
    from_imag = np.where(part == 0, -sine, cosine)
    return np.concatenate([from_real, from_imag], axis=1)


def x_table(parity):
    modes = 2 * np.arange(HALF) + parity
    angle = (np.arange(HALF)[:, None] * modes[None, :] % GRID) * (2.0 * np.pi / GRID)
    cosine, sine = np.cos(angle), np.sin(angle)
    return np.block([[cosine, -sine], [sine, cosine]])


def y_table():
    index = np.arange(GRID)
    angle = (index[:, None] * index[None, :] % GRID) * (2.0 * np.pi / GRID)
    cosine = np.cos(angle).reshape(N_GY, 1, GRID // N_GY, GRID)
    sine = -np.sin(angle).reshape(N_GY, 1, GRID // N_GY, GRID)
    return np.concatenate([cosine, sine], axis=1).reshape(N_GY, 2 * (GRID // N_GY), GRID)


def twiddles():
    angle = np.arange(HALF) * (2.0 * np.pi / GRID)
    table = np.stack([np.cos(angle), np.sin(angle)])
    return np.repeat(table[:, None, :], 32, axis=1).astype(np.float32)


def split(value):
    high = value.astype(BF16)
    return high, (value - high.astype(F32)).astype(BF16)


def signed(index):
    return jnp.where(index < GRID // 2, index, index - GRID).astype(F32)


NT = (((1,), (1,)), ((), ()))
NN = (((1,), (0,)), ((), ()))


def dot(a, b, dims):
    return lax.dot_general(a, b, dims, preferred_element_type=F32)


def z_kernel(pieces, source, table, twiddle, out, even, odd):
    quad = pl.program_id(0)
    with_extra = EXTRA in pieces
    parities = [p for p in range(2) if with_extra or any(c % 2 == p for c in pieces)]
    row = lax.broadcasted_iota(jnp.int32, (32, GRID), 0)
    mode_y = signed(row + lax.axis_index("gy") * 32)
    mode_z = signed(lax.broadcasted_iota(jnp.int32, (32, GRID), 1))
    half_wave_z = 0.5 * WAVE * mode_z
    partial_square = mode_y * mode_y + mode_z * mode_z
    turn_re, turn_im = twiddle[0], twiddle[1]
    for k in range(4):
        index_x = lax.axis_index("gx") * 16 + quad * 4 + k
        mode_x = jnp.where(index_x < GRID // 2, index_x, index_x - GRID).astype(F32)
        inverse = 1.0 / jnp.maximum(mode_x * mode_x + partial_square, 1.0)
        v = []
        for r in range(2):
            s1, s2, s3 = source[r, 0, k], source[r, 1, k], source[r, 2, k]
            ratio = (s1 * mode_x + s2 * mode_y + s3 * mode_z) * inverse
            v.append((s1 - mode_x * ratio, s2 - mode_y * ratio, s3 - mode_z * ratio))
        rows = [
            (v[0][0], v[1][0], k * 128),
            (v[0][1], v[1][1], k * 128 + 32),
            (v[0][2], v[1][2], k * 128 + 64),
            (-half_wave_z * v[1][0], half_wave_z * v[0][0], k * 128 + 96),
        ]
        if with_extra:
            rows.append((-half_wave_z * v[1][1], half_wave_z * v[0][1], 512 + k * 32))
        for real, imag, start in rows:
            here = slice(start, start + 32)
            for p in parities:
                if p == 0:
                    re = real[:, :HALF] + real[:, HALF:]
                    im = imag[:, :HALF] + imag[:, HALF:]
                    target = even
                else:
                    re0 = real[:, :HALF] - real[:, HALF:]
                    im0 = imag[:, :HALF] - imag[:, HALF:]
                    re = re0 * turn_re - im0 * turn_im
                    im = re0 * turn_im + im0 * turn_re
                    target = odd
                for r, value in ((0, re), (1, im)):
                    high, low = split(value)
                    target[here, r * HALF : (r + 1) * HALF] = high
                    target[here, GRID + r * HALF : GRID + (r + 1) * HALF] = low
                    target[here, 2 * GRID + r * HALF : 2 * GRID + (r + 1) * HALF] = high

    for p in parities:
        data = (even, odd)[p]
        wanted = [c for c in pieces if c != EXTRA and c % 2 == p]
        if not wanted:
            continue
        c_low, c_high = min(wanted) // 2, max(wanted) // 2 + 1
        for pair in range(2):
            result = dot(
                table[c_low * 128 : c_high * 128], data[pair * 256 : pair * 256 + 256], NT
            )
            for c in wanted:
                top = (c // 2 - c_low) * 128
                for side in range(2):
                    out[:, pieces.index(c), pair * 2 + side] = result[
                        top : top + 128, side * 128 : side * 128 + 128
                    ].reshape(N_GX, 8, 128)
    if with_extra:
        halves = [dot(table[...], data[512:640], NT) for data in (even, odd)]
        v = [halves[c % 2][(c // 2) * 128 : (c // 2) * 128 + 128] for c in range(4)]
        lane = lax.broadcasted_iota(jnp.int32, (128, 128), 1)
        lower64 = lane < 64
        lower32 = (lane & 32) == 0
        p0 = [jnp.where(lower64, v[c], pltpu.roll(v[c + 2], 64, 1)) for c in range(2)]
        p1 = [jnp.where(lower64, pltpu.roll(v[c], 64, 1), v[c + 2]) for c in range(2)]
        place_of = pieces.index(EXTRA)
        for k1, p in ((0, p0), (1, p1)):
            q0 = jnp.where(lower32, p[0], pltpu.roll(p[1], 32, 1))
            q1 = jnp.where(lower32, pltpu.roll(p[0], 96, 1), p[1])
            out[:, place_of, 2 * k1] = q0.reshape(N_GX, 8, 128)
            out[:, place_of, 2 * k1 + 1] = q1.reshape(N_GX, 8, 128)


def z_stage(pieces, source, table, twiddle):
    def kernel(*refs):
        z_kernel(pieces, *refs)

    return pl.pallas_call(
        kernel,
        out_shape=jax.ShapeDtypeStruct((N_GX, len(pieces), 16, 8, 128), F32),
        grid=(4,),
        in_specs=[
            pl.BlockSpec((2, 3, 4, 32, GRID), lambda i: (0, 0, i, 0, 0)),
            pl.BlockSpec((256, 768), lambda i: (0, 0)),
            pl.BlockSpec((2, 32, HALF), lambda i: (0, 0, 0)),
        ],
        out_specs=pl.BlockSpec((N_GX, len(pieces), 4, 8, 128), lambda i: (0, 0, i, 0, 0)),
        scratch_shapes=[pltpu.VMEM((640, 768), BF16), pltpu.VMEM((640, 768), BF16)],
        name="z_stage",
    )(source, table, twiddle)


def weight(distance, offset):
    shifted = distance - (SUPPORT // 2 - 1) - offset
    inside = (distance >= 0.0) & (distance < SUPPORT)
    return jnp.where(inside, jnp.exp(-5.6 / SUPPORT * shifted * shifted), 0.0)


def wrapped(distance):
    return jnp.where(distance < 0.0, distance + GRID, distance)


def gather_kernel(counts, start, offset, other_start, other_offset, out):
    own, ghosts = counts[0, 0], counts[0, 2]
    out[0:3, :OWN] = start[...].astype(F32)
    out[3:6, :OWN] = offset[...]
    out[0:3, OWN:] = other_start[:, 1].astype(F32)
    out[3:6, OWN:] = other_offset[:, 1]
    lane = lax.broadcasted_iota(jnp.int32, (1, ROWS), 1)
    bound = jnp.where(lane < OWN, own, OWN + ghosts)
    out[6:7, :] = jnp.where(lane < bound, 1.0, 0.0)
    out[7:8, :] = jnp.where(lane == 0, own, jnp.where(lane == 1, ghosts, 0)).astype(F32)


def gather_stage(counts, start, offset, other_start, other_offset):
    vmem = pl.BlockSpec(memory_space=pltpu.VMEM)
    return pl.pallas_call(
        gather_kernel,
        out_shape=jax.ShapeDtypeStruct((8, ROWS), F32),
        in_specs=[
            pl.BlockSpec(memory_space=pltpu.SMEM),
            vmem,
            vmem,
            vmem,
            vmem,
        ],
        out_specs=vmem,
        name="gather_stage",
    )(counts, start, offset, other_start, other_offset)


def row_kernel(place, particles, table, phases, planes, phase, plane, sent_phase, sent_plane):
    y_cell = lax.broadcasted_iota(jnp.int32, (GRID, BLOCK), 0).astype(F32)
    x_cell = lax.broadcasted_iota(jnp.int32, (WINDOW, BLOCK), 0).astype(F32)
    local_z = lax.broadcasted_iota(jnp.int32, (16, BLOCK), 0)
    z_cell = (place[0] * 16 + 4 * (local_z % 4) + local_z // 4).astype(F32)
    jobs = 2 * ((place[2] + 1) // 2)

    def copies(slot, job):
        return (
            pltpu.make_async_copy(phase.at[slot], phases.at[job], sent_phase.at[slot]),
            pltpu.make_async_copy(plane.at[slot], planes.at[job], sent_plane.at[slot]),
        )

    def one_job(job, carry):
        slot = job & 1

        @pl.when(job >= 2)
        def _():
            for copy in copies(slot, job):
                copy.wait()

        entry, block = place[HEAD + job], place[HEAD + JOBS + job]
        owner = place[HEAD + 2 * JOBS + job]
        data = particles[entry, :, pl.ds(pl.multiple_of(block * BLOCK, BLOCK), BLOCK)]
        weight_y = weight(wrapped(y_cell - data[1:2]), data[4:5])
        high, low = split(weight_y)
        phase[slot] = dot(table[...], jnp.concatenate([high, low, high], axis=0), NN)
        weight_x = weight(x_cell + (owner * 32).astype(F32) - data[0:1], data[3:4])
        weight_z = weight(wrapped(z_cell - data[2:3]), data[5:6]) * data[6:7]
        for z in range(16):
            plane[slot, z * WINDOW : (z + 1) * WINDOW] = (weight_x * weight_z[z : z + 1]).astype(
                BF16
            )
        for copy in copies(slot, job):
            copy.start()
        return carry

    lax.fori_loop(0, jobs, one_job, 0)
    for slot in range(2):

        @pl.when(jobs > slot)
        def _():
            for copy in copies(slot, 0):
                copy.wait()


def row_stage(place, particles, table):
    return pl.pallas_call(
        row_kernel,
        out_shape=(
            jax.ShapeDtypeStruct((JOBS, 64, BLOCK), F32),
            jax.ShapeDtypeStruct((JOBS, 16 * WINDOW, BLOCK), BF16),
        ),
        grid_spec=pltpu.PrefetchScalarGridSpec(
            num_scalar_prefetch=1,
            grid=(1,),
            in_specs=[
                pl.BlockSpec((N_GY, 8, ROWS), lambda i, _: (0, 0, 0)),
                pl.BlockSpec((64, 768), lambda i, _: (0, 0)),
            ],
            out_specs=(pl.BlockSpec(memory_space=pl.ANY), pl.BlockSpec(memory_space=pl.ANY)),
            scratch_shapes=[
                pltpu.VMEM((2, 64, BLOCK), F32),
                pltpu.VMEM((2, 16 * WINDOW, BLOCK), BF16),
                pltpu.SemaphoreType.DMA((2,)),
                pltpu.SemaphoreType.DMA((2,)),
            ],
        ),
        name="row_stage",
    )(place, particles, table)


def field_kernel(steps, place, main, extra, t_even, t_odd, phases, planes, *rest):
    previous = rest[0] if len(rest) == 11 else None
    out, field, work0, work1, work2, work3, window, phase, plane, arrived = rest[-10:]
    work = (work0, work1, work2, work3)
    first_c = steps[0]
    depth = 4 * len(steps)
    step_c = pl.program_id(0)
    c = first_c + step_c
    pairs = (place[2] + 1) // 2

    def copies(pair, base):
        found = []
        for side in range(2):
            job, slot = 2 * pair + side, base + side
            rows = pl.ds(first_c * 4 * WINDOW, depth * WINDOW)
            found.append(
                pltpu.make_async_copy(phases.at[job], phase.at[slot], arrived.at[0, slot])
            )
            found.append(
                pltpu.make_async_copy(planes.at[job, rows], plane.at[slot], arrived.at[1, slot])
            )
        return found

    for ahead in range(AHEAD - 1):

        @pl.when((step_c == 0) & (pairs > ahead))
        def _():
            for copy in copies(ahead, 2 * ahead):
                copy.start()

    lane = lax.broadcasted_iota(jnp.int32, (HALF, 128), 1)
    group = lane // 32
    row = lax.broadcasted_iota(jnp.int32, (HALF, 128), 0)
    wave_y = WAVE * signed(lane % 32 + place[1] * 32)
    cross_y = jnp.where(group == 0, wave_y, jnp.where(group == 2, 0.0, 0.5 * wave_y))
    half_same = jnp.where((group == 1) | (group == 2), 0.5, 0.0)
    plain_left = group == 2
    plain_extra = group == 3
    cross_left = group == 0
    flat_main = main.reshape(GRID * 8, 128)
    flat_extra = extra.reshape(GRID * 8, 128)
    waves = [WAVE * signed(2 * row + parity) for parity in range(2)]
    for step in range(4):
        results = []
        for parity in range(2):
            target = work[2 * (step % 2) + parity]
            wave_x = waves[parity]
            cross_x = half_same * wave_x

            def load(flat, q):
                return flat[pl.ds(parity * 8 + q * 4 + step, HALF, stride=16), :]

            parts = []
            for q in range(2):
                value = load(flat_main, q)
                moved = pltpu.roll(load(flat_extra, q), 32 * (3 - c), 1)
                left = pltpu.roll(value, 96, 1)
                right = pltpu.roll(value, 32, 1)
                cross = cross_y * jnp.where(cross_left, left, right) + cross_x * value
                plain = jnp.where(plain_left, left, jnp.where(plain_extra, moved, 0.0))
                parts.append((value, wave_x * left, cross, plain))
            (a_re, x_re, c_re, p_re), (a_im, x_im, c_im, p_im) = parts
            for top, left, value in (
                (0, 0, jnp.where(plain_extra, -x_im, a_re)),
                (HALF, 0, jnp.where(plain_extra, x_re, a_im)),
                (0, 128, p_re - c_im),
                (HALF, 128, p_im + c_re),
            ):
                high, low = split(value)
                lanes = slice(left, left + 128)
                target[top : top + HALF, lanes] = high
                target[GRID + top : GRID + top + HALF, lanes] = low
                target[2 * GRID + top : 2 * GRID + top + HALF, lanes] = high
            results.append(dot((t_even, t_odd)[parity][...], target[...], NN))
        from_even, from_odd = results
        near = (from_even + from_odd).astype(BF16)
        far = (from_even - from_odd).astype(BF16)
        z = step_c * 4 + step
        for q in range(2):
            lanes = slice(q * 256, q * 256 + 256)
            field[z, 0:HALF, lanes] = near[q * HALF : q * HALF + HALF]
            field[z, HALF:GRID, lanes] = far[q * HALF : q * HALF + HALF]
            field[z, GRID : GRID + 16, lanes] = near[q * HALF : q * HALF + 16]

    @pl.when(step_c == len(steps) - 1)
    def _():
        if previous is None:
            out[...] = jnp.zeros_like(out)
        else:
            out[...] = previous[...]

        for owner in range(N_GY):
            block = field[:, owner * 32 : owner * 32 + WINDOW, :]
            window[owner] = block.reshape(depth * WINDOW, 512).T

        def one_pair(pair, carry):
            base = 2 * (pair & (AHEAD - 1))
            for copy in copies(pair, base):
                copy.wait()

            @pl.when(pair + AHEAD - 1 < pairs)
            def _():
                for copy in copies(pair + AHEAD - 1, 2 * ((pair + AHEAD - 1) & (AHEAD - 1))):
                    copy.start()

            for side in range(2):
                job = 2 * pair + side
                owner, block = place[HEAD + 2 * JOBS + job], place[HEAD + JOBS + job]
                lanes = pl.ds(pl.multiple_of(block * BLOCK, BLOCK), BLOCK)
                summed = dot(window[owner], plane[base + side], NN).reshape(2, 8, 32, BLOCK)
                turn = phase[base + side]
                product = summed[0] * turn[None, 0:32] + summed[1] * turn[None, 32:64]
                value = jnp.sum(product, axis=1)
                if previous is not None:
                    value = value + previous[owner, :, lanes]
                out[owner, :, lanes] = value
            return carry

        lax.fori_loop(0, pairs, one_pair, 0)


def field_stage(steps, first, place, main, extra, extra_at, t_even, t_odd, rows, previous):
    def whole(shape):
        return pl.BlockSpec(
            shape, lambda i, _: (0,) * len(shape), pipeline_mode=pl.Buffered(1)
        )

    def kernel(*refs):
        field_kernel(steps, *refs)

    piece = (N_GX, None, 16, 8, 128)
    in_specs = [
        pl.BlockSpec(piece, lambda i, _: (0, first + i, 0, 0, 0)),
        pl.BlockSpec(piece, lambda i, _: (0, extra_at, 0, 0, 0)),
        whole((256, 768)),
        whole((256, 768)),
        pl.BlockSpec(memory_space=pl.ANY),
        pl.BlockSpec(memory_space=pl.ANY),
    ]
    operands = [place, main, extra, t_even, t_odd, *rows]
    if previous is not None:
        in_specs.append(whole((N_GY, 8, ROWS)))
        operands.append(previous)
    depth = 4 * len(steps)
    return pl.pallas_call(
        kernel,
        out_shape=jax.ShapeDtypeStruct((N_GY, 8, ROWS), F32),
        grid_spec=pltpu.PrefetchScalarGridSpec(
            num_scalar_prefetch=1,
            grid=(len(steps),),
            in_specs=in_specs,
            out_specs=whole((N_GY, 8, ROWS)),
            scratch_shapes=[
                pltpu.VMEM((depth, GRID + 16, 512), BF16),
                pltpu.VMEM((768, 256), BF16),
                pltpu.VMEM((768, 256), BF16),
                pltpu.VMEM((768, 256), BF16),
                pltpu.VMEM((768, 256), BF16),
                pltpu.VMEM((N_GY, 512, depth * WINDOW), BF16),
                pltpu.VMEM((2 * AHEAD, 64, BLOCK), F32),
                pltpu.VMEM((2 * AHEAD, depth * WINDOW, BLOCK), BF16),
                pltpu.SemaphoreType.DMA((2, 2 * AHEAD)),
            ],
        ),
        name="field_stage",
    )(*operands)


def ghost_kernel(values, slots, own, back):
    total = values[0]
    for source in range(1, N_GY):
        total = total + values[source]
    own[...] = total[:, :OWN]
    ghosts = total[:, OWN:]
    cell = lax.broadcasted_iota(jnp.int32, (OWN, GHOST), 0)
    chosen = (cell == slots[1:2]).astype(F32).astype(BF16)
    first, _ = split(ghosts)
    second, third = split(ghosts - first.astype(F32))
    parts = jnp.concatenate([first.astype(F32), second.astype(F32), third.astype(F32)], axis=0)
    placed = dot(parts.astype(BF16), chosen, NT)
    back[...] = placed[0:8] + (placed[8:16] + placed[16:24])


def ghost_stage(values, slots):
    return pl.pallas_call(
        ghost_kernel,
        out_shape=(
            jax.ShapeDtypeStruct((8, OWN), F32),
            jax.ShapeDtypeStruct((8, OWN), F32),
        ),
        name="ghost_stage",
    )(values, slots)


def final_kernel(own, arrived, velocity, strain):
    total = own[...] + arrived[...]
    velocity[...] = total[:3]
    strain[...] = total[3:]


def final_stage(own, arrived):
    return pl.pallas_call(
        final_kernel,
        out_shape=(
            jax.ShapeDtypeStruct((3, OWN), F32),
            jax.ShapeDtypeStruct((5, OWN), F32),
        ),
        name="final_stage",
    )(own, arrived)


def job_list(live, owners, index_gx, index_gy):
    needed = (live + BLOCK - 1) // BLOCK
    block = jnp.arange(BLOCKS, dtype=jnp.int32)[None, :]
    own = OWN // BLOCK
    valid = jnp.where(block < own, block < needed[:, 0:1], block - own < needed[:, 1:2])
    valid = valid.reshape(-1).astype(jnp.int32)
    item = jnp.arange(N_GY * BLOCKS, dtype=jnp.int32)
    before = jnp.sum(jnp.where(item[None, :] < item[:, None], valid[None, :], 0), axis=1)
    jobs = jnp.sum(valid)
    wanted = jnp.minimum(jnp.arange(JOBS, dtype=jnp.int32), jobs - 1)
    chosen = (before[None, :] == wanted[:, None]) & (valid[None, :] > 0)
    found = jnp.sum(jnp.where(chosen, item[None, :], 0), axis=1)
    entry = found // BLOCKS
    at_entry = entry[:, None] == jnp.arange(N_GY, dtype=jnp.int32)[None, :]
    owner = jnp.sum(jnp.where(at_entry, owners[None, :], 0), axis=1)
    return jnp.concatenate(
        [jnp.stack([index_gx, index_gy, jobs]), entry, found % BLOCKS, owner]
    )


def per_device(
    source_hat, particle_start, particle_offset, ghost_start, ghost_offset, ghost_slot, counts
):
    index_gx = lax.axis_index("gx").astype(jnp.int32)
    index_gy = lax.axis_index("gy").astype(jnp.int32)
    members = range(N_GY)
    mine = gather_stage(counts, particle_start, particle_offset, ghost_start, ghost_offset)
    partner = lax.ppermute(mine, "gy", [(i, i ^ 1) for i in members])

    table_z = jnp.asarray(left_triple(z_table()))
    twiddle = jnp.asarray(twiddles())
    sent = [
        z_stage(chunk + ((EXTRA,) if number == 0 else ()), source_hat, table_z, twiddle)
        for number, chunk in enumerate(CHUNKS)
    ]
    received = [
        lax.all_to_all(piece, "gx", split_axis=0, concat_axis=0, tiled=True)
        for piece in sent
    ]
    pair = jnp.stack([mine, partner])
    pairs = [pair]
    for shift in (2, 6, 4):
        route = [(i, (i + shift) % N_GY) for i in members]
        pairs.append(lax.ppermute(pair, "gy", route))
    particles = jnp.concatenate(pairs, axis=0)
    shifts = jnp.array([0, 0, 2, 2, 6, 6, 4, 4], jnp.int32)
    owners = jnp.bitwise_xor(
        (index_gy - shifts) & (N_GY - 1), jnp.arange(N_GY, dtype=jnp.int32) & 1
    )
    place = job_list(particles[:, 7, 0:2].astype(jnp.int32), owners, index_gx, index_gy)
    table_y = jnp.asarray(left_triple(y_table()))
    table_y = lax.dynamic_index_in_dim(table_y, index_gy, 0, keepdims=False)
    rows = row_stage(place, particles, table_y)

    t_even = jnp.asarray(left_triple(x_table(0)))
    t_odd = jnp.asarray(left_triple(x_table(1)))
    partial = None
    for number, chunk in enumerate(CHUNKS):
        partial = field_stage(
            chunk, 0, place, received[number], received[0], len(CHUNKS[0]),
            t_even, t_odd, rows, partial,
        )
    partial = lax.all_to_all(partial, "gy", split_axis=0, concat_axis=0, tiled=True)
    own, back = ghost_stage(partial, ghost_slot)
    devices = range(N_GX)
    route = [((i + 1) % N_GX, i) for i in devices]
    return final_stage(own, lax.ppermute(back, "gx", route))


def solution(mesh):
    in_specs = (
        P(None, None, "gx", "gy", None),
        P(None, ("gx", "gy")),
        P(None, ("gx", "gy")),
        P(None, None, ("gx", "gy")),
        P(None, None, ("gx", "gy")),
        P(None, ("gx", "gy")),
        P(("gx", "gy"), None),
    )
    out_specs = (P(None, ("gx", "gy")), P(None, ("gx", "gy")))
    return jax.shard_map(
        per_device, mesh=mesh, in_specs=in_specs, out_specs=out_specs, check_vma=False
    )
```

```python
import math

import jax
import jax.numpy as jnp
import numpy as np
from jax import lax
from jax.experimental import pallas as pl
from jax.experimental.pallas import tpu as pltpu
from jax.sharding import PartitionSpec as P


F32 = jnp.float32
BF16 = jnp.bfloat16
SUPPORT = 8
GRID = 256
HALF = GRID // 2
N_GX = 16
N_GY = 8
OWN = 2048
GHOST = 512
ROWS = OWN + GHOST
WAVE = 2.0 * math.pi / GRID
WINDOW = 48
BLOCK = 256
CHUNKS = ((0, 1, 2, 3),)
EXTRA = 4
BLOCKS = ROWS // BLOCK
JOBS = N_GY * BLOCKS + 2
HEAD = 3
AHEAD = 8


def numpy_halves(table):
    import ml_dtypes

    high = table.astype(ml_dtypes.bfloat16)
    low = (table - high.astype(np.float64)).astype(ml_dtypes.bfloat16)
    return high, low


def left_triple(table):
    high, low = numpy_halves(table)
    return np.concatenate([high, high, low], axis=-1)


def z_table():
    c1, slab, part, step = np.meshgrid(
        np.arange(2), np.arange(N_GX), np.arange(2), np.arange(4), indexing="ij"
    )
    position = (8 * slab + 2 * step + c1).reshape(-1, 1)
    part = part.reshape(-1, 1)
    angle = (position * np.arange(HALF)[None, :] % HALF) * (2.0 * np.pi / HALF)
    cosine, sine = np.cos(angle), np.sin(angle)
    from_real = np.where(part == 0, cosine, sine)
    from_imag = np.where(part == 0, -sine, cosine)
    return np.concatenate([from_real, from_imag], axis=1)


def x_table(parity):
    modes = 2 * np.arange(HALF) + parity
    angle = (np.arange(HALF)[:, None] * modes[None, :] % GRID) * (2.0 * np.pi / GRID)
    cosine, sine = np.cos(angle), np.sin(angle)
    return np.block([[cosine, -sine], [sine, cosine]])


def y_table():
    index = np.arange(GRID)
    angle = (index[:, None] * index[None, :] % GRID) * (2.0 * np.pi / GRID)
    cosine = np.cos(angle).reshape(N_GY, 1, GRID // N_GY, GRID)
    sine = -np.sin(angle).reshape(N_GY, 1, GRID // N_GY, GRID)
    return np.concatenate([cosine, sine], axis=1).reshape(N_GY, 2 * (GRID // N_GY), GRID)


def twiddles():
    angle = np.arange(HALF) * (2.0 * np.pi / GRID)
    table = np.stack([np.cos(angle), np.sin(angle)])
    return np.repeat(table[:, None, :], 32, axis=1).astype(np.float32)


def split(value):
    high = value.astype(BF16)
    return high, (value - high.astype(F32)).astype(BF16)


def signed(index):
    return jnp.where(index < GRID // 2, index, index - GRID).astype(F32)


NT = (((1,), (1,)), ((), ()))
NN = (((1,), (0,)), ((), ()))


def dot(a, b, dims):
    return lax.dot_general(a, b, dims, preferred_element_type=F32)


def z_kernel(pieces, source, table, twiddle, out, even, odd):
    quad = pl.program_id(0)
    with_extra = EXTRA in pieces
    parities = [p for p in range(2) if with_extra or any(c % 2 == p for c in pieces)]
    row = lax.broadcasted_iota(jnp.int32, (32, GRID), 0)
    mode_y = signed(row + lax.axis_index("gy") * 32)
    mode_z = signed(lax.broadcasted_iota(jnp.int32, (32, GRID), 1))
    half_wave_z = 0.5 * WAVE * mode_z
    partial_square = mode_y * mode_y + mode_z * mode_z
    turn_re, turn_im = twiddle[0], twiddle[1]

    def build(k):
        index_x = lax.axis_index("gx") * 16 + quad * 4 + k
        mode_x = jnp.where(index_x < GRID // 2, index_x, index_x - GRID).astype(F32)
        inverse = 1.0 / jnp.maximum(mode_x * mode_x + partial_square, 1.0)
        v = []
        for r in range(2):
            s1, s2, s3 = source[r, 0, k], source[r, 1, k], source[r, 2, k]
            ratio = (s1 * mode_x + s2 * mode_y + s3 * mode_z) * inverse
            v.append((s1 - mode_x * ratio, s2 - mode_y * ratio, s3 - mode_z * ratio))
        rows = [
            (v[0][0], v[1][0], k * 128),
            (v[0][1], v[1][1], k * 128 + 32),
            (v[0][2], v[1][2], k * 128 + 64),
            (-half_wave_z * v[1][0], half_wave_z * v[0][0], k * 128 + 96),
        ]
        if with_extra:
            rows.append((-half_wave_z * v[1][1], half_wave_z * v[0][1], 512 + k * 32))
        for real, imag, start in rows:
            here = slice(start, start + 32)
            for p in parities:
                if p == 0:
                    re = real[:, :HALF] + real[:, HALF:]
                    im = imag[:, :HALF] + imag[:, HALF:]
                    target = even
                else:
                    re0 = real[:, :HALF] - real[:, HALF:]
                    im0 = imag[:, :HALF] - imag[:, HALF:]
                    re = re0 * turn_re - im0 * turn_im
                    im = re0 * turn_im + im0 * turn_re
                    target = odd
                for r, value in ((0, re), (1, im)):
                    high, low = split(value)
                    target[here, r * HALF : (r + 1) * HALF] = high
                    target[here, GRID + r * HALF : GRID + (r + 1) * HALF] = low
                    target[here, 2 * GRID + r * HALF : 2 * GRID + (r + 1) * HALF] = high

    def transform(pair):
        for p in parities:
            wanted = [c for c in pieces if c != EXTRA and c % 2 == p]
            if not wanted:
                continue
            c_low, c_high = min(wanted) // 2, max(wanted) // 2 + 1
            data = (even, odd)[p][pair * 256 : pair * 256 + 256]
            result = dot(table[c_low * 128 : c_high * 128], data, NT)
            for c in wanted:
                top = (c // 2 - c_low) * 128
                for side in range(2):
                    out[:, pieces.index(c), side, pair] = result[
                        top : top + 128, side * 128 : side * 128 + 128
                    ].reshape(N_GX, 8, 128)

    build(0)
    build(1)
    transform(0)
    build(2)
    build(3)
    transform(1)
    if with_extra:
        halves = [dot(table[...], data[512:640], NT) for data in (even, odd)]
        v = [halves[c % 2][(c // 2) * 128 : (c // 2) * 128 + 128] for c in range(4)]
        lane = lax.broadcasted_iota(jnp.int32, (128, 128), 1)
        lower64 = lane < 64
        lower32 = (lane & 32) == 0
        p0 = [jnp.where(lower64, v[c], pltpu.roll(v[c + 2], 64, 1)) for c in range(2)]
        p1 = [jnp.where(lower64, pltpu.roll(v[c], 64, 1), v[c + 2]) for c in range(2)]
        place_of = pieces.index(EXTRA)
        for k1, p in ((0, p0), (1, p1)):
            q0 = jnp.where(lower32, p[0], pltpu.roll(p[1], 32, 1))
            q1 = jnp.where(lower32, pltpu.roll(p[0], 96, 1), p[1])
            out[:, place_of, 0, k1] = q0.reshape(N_GX, 8, 128)
            out[:, place_of, 1, k1] = q1.reshape(N_GX, 8, 128)


def z_stage(pieces, source, table, twiddle):
    def kernel(*refs):
        z_kernel(pieces, *refs)

    return pl.pallas_call(
        kernel,
        out_shape=jax.ShapeDtypeStruct((N_GX, len(pieces), 2, 8, 8, 128), F32),
        grid=(4,),
        in_specs=[
            pl.BlockSpec((2, 3, 4, 32, GRID), lambda i: (0, 0, i, 0, 0)),
            pl.BlockSpec((256, 768), lambda i: (0, 0)),
            pl.BlockSpec((2, 32, HALF), lambda i: (0, 0, 0)),
        ],
        out_specs=pl.BlockSpec(
            (N_GX, len(pieces), 2, 2, 8, 128), lambda i: (0, 0, 0, i, 0, 0)
        ),
        scratch_shapes=[pltpu.VMEM((640, 768), BF16), pltpu.VMEM((640, 768), BF16)],
        name="z_stage",
    )(source, table, twiddle)


def weight(distance, offset):
    shifted = distance - (SUPPORT // 2 - 1) - offset
    inside = (distance >= 0.0) & (distance < SUPPORT)
    return jnp.where(inside, jnp.exp(-5.6 / SUPPORT * shifted * shifted), 0.0)


def wrapped(distance):
    return jnp.where(distance < 0.0, distance + GRID, distance)


def gather_kernel(counts, start, offset, other_start, other_offset, out, packed):
    own, ghosts = counts[0, 0], counts[0, 2]
    lane = lax.broadcasted_iota(jnp.int32, (8, ROWS), 1)
    packed[...] = jnp.zeros_like(packed)
    packed[0:3, :GHOST] = other_start[:, 1].astype(F32)
    packed[3:6, :GHOST] = other_offset[:, 1]
    moved = pltpu.roll(packed[...], own, 1)
    packed[0:3, :OWN] = start[...].astype(F32)
    packed[3:6, :OWN] = offset[...]
    out[...] = jnp.where(lane < own, packed[...], moved)
    lane = lane[0:1]
    out[6:7, :] = jnp.where(lane < own + ghosts, 1.0, 0.0)
    out[7:8, :] = jnp.where(lane == 0, own + ghosts, 0).astype(F32)


def gather_stage(counts, start, offset, other_start, other_offset):
    vmem = pl.BlockSpec(memory_space=pltpu.VMEM)
    return pl.pallas_call(
        gather_kernel,
        out_shape=jax.ShapeDtypeStruct((8, ROWS), F32),
        in_specs=[
            pl.BlockSpec(memory_space=pltpu.SMEM),
            vmem,
            vmem,
            vmem,
            vmem,
        ],
        out_specs=vmem,
        scratch_shapes=[pltpu.VMEM((8, ROWS), F32)],
        name="gather_stage",
    )(counts, start, offset, other_start, other_offset)


def row_kernel(place, particles, table, phases, planes, phase, plane, sent_phase, sent_plane):
    y_cell = lax.broadcasted_iota(jnp.int32, (GRID, BLOCK), 0).astype(F32)
    x_cell = lax.broadcasted_iota(jnp.int32, (WINDOW, BLOCK), 0).astype(F32)
    local_z = lax.broadcasted_iota(jnp.int32, (16, BLOCK), 0)
    z_cell = (place[0] * 16 + 4 * (local_z % 4) + local_z // 4).astype(F32)
    jobs = 2 * ((place[2] + 1) // 2)

    def copies(slot, job):
        return (
            pltpu.make_async_copy(phase.at[slot], phases.at[job], sent_phase.at[slot]),
            pltpu.make_async_copy(plane.at[slot], planes.at[job], sent_plane.at[slot]),
        )

    def one_job(job, carry):
        slot = job & 1

        @pl.when(job >= 2)
        def _():
            for copy in copies(slot, job):
                copy.wait()

        entry, block = place[HEAD + job], place[HEAD + JOBS + job]
        owner = place[HEAD + 2 * JOBS + job]
        data = particles[entry, :, pl.ds(pl.multiple_of(block * BLOCK, BLOCK), BLOCK)]
        weight_y = weight(wrapped(y_cell - data[1:2]), data[4:5])
        high, low = split(weight_y)
        phase[slot] = dot(table[...], jnp.concatenate([high, low, high], axis=0), NN)
        weight_x = weight(x_cell + (owner * 32).astype(F32) - data[0:1], data[3:4])
        weight_z = weight(wrapped(z_cell - data[2:3]), data[5:6]) * data[6:7]
        for z in range(16):
            plane[slot, z * WINDOW : (z + 1) * WINDOW] = (weight_x * weight_z[z : z + 1]).astype(
                BF16
            )
        for copy in copies(slot, job):
            copy.start()
        return carry

    lax.fori_loop(0, jobs, one_job, 0)
    for slot in range(2):

        @pl.when(jobs > slot)
        def _():
            for copy in copies(slot, 0):
                copy.wait()


def row_stage(place, particles, table):
    return pl.pallas_call(
        row_kernel,
        out_shape=(
            jax.ShapeDtypeStruct((JOBS, 64, BLOCK), F32),
            jax.ShapeDtypeStruct((JOBS, 16 * WINDOW, BLOCK), BF16),
        ),
        grid_spec=pltpu.PrefetchScalarGridSpec(
            num_scalar_prefetch=1,
            grid=(1,),
            in_specs=[
                pl.BlockSpec((N_GY, 8, ROWS), lambda i, _: (0, 0, 0)),
                pl.BlockSpec((64, 768), lambda i, _: (0, 0)),
            ],
            out_specs=(pl.BlockSpec(memory_space=pl.ANY), pl.BlockSpec(memory_space=pl.ANY)),
            scratch_shapes=[
                pltpu.VMEM((2, 64, BLOCK), F32),
                pltpu.VMEM((2, 16 * WINDOW, BLOCK), BF16),
                pltpu.SemaphoreType.DMA((2,)),
                pltpu.SemaphoreType.DMA((2,)),
            ],
        ),
        name="row_stage",
    )(place, particles, table)


def field_kernel(steps, place, main, extra, t_even, t_odd, phases, planes, *rest):
    previous = rest[0] if len(rest) == 11 else None
    out, field, work0, work1, work2, work3, window, phase, plane, arrived = rest[-10:]
    work = (work0, work1, work2, work3)
    first_c = steps[0]
    depth = 4 * len(steps)
    step_c = pl.program_id(0)
    c = first_c + step_c
    pairs = (place[2] + 1) // 2

    def copies(pair, base):
        found = []
        for side in range(2):
            job, slot = 2 * pair + side, base + side
            rows = pl.ds(first_c * 4 * WINDOW, depth * WINDOW)
            found.append(
                pltpu.make_async_copy(phases.at[job], phase.at[slot], arrived.at[0, slot])
            )
            found.append(
                pltpu.make_async_copy(planes.at[job, rows], plane.at[slot], arrived.at[1, slot])
            )
        return found

    for ahead in range(AHEAD - 1):

        @pl.when((step_c == 0) & (pairs > ahead))
        def _():
            for copy in copies(ahead, 2 * ahead):
                copy.start()

    lane = lax.broadcasted_iota(jnp.int32, (HALF, 128), 1)
    group = lane // 32
    row = lax.broadcasted_iota(jnp.int32, (HALF, 128), 0)
    wave_y = WAVE * signed(lane % 32 + place[1] * 32)
    cross_y = jnp.where(group == 0, wave_y, jnp.where(group == 2, 0.0, 0.5 * wave_y))
    half_same = jnp.where((group == 1) | (group == 2), 0.5, 0.0)
    plain_left = group == 2
    plain_extra = group == 3
    cross_left = group == 0
    flat_main = main.reshape(GRID * 8, 128)
    flat_extra = extra.reshape(GRID * 8, 128)
    waves = [WAVE * signed(2 * row + parity) for parity in range(2)]
    for step in range(4):
        results = []
        for parity in range(2):
            target = work[2 * (step % 2) + parity]
            wave_x = waves[parity]
            cross_x = half_same * wave_x

            def load(flat, q):
                top = parity * 64 + q * 4 + step
                return jnp.concatenate(
                    [flat[pl.ds(source * 128 + top, 8, stride=8), :] for source in range(N_GX)]
                )

            parts = []
            for q in range(2):
                value = load(flat_main, q)
                moved = pltpu.roll(load(flat_extra, q), 32 * (3 - c), 1)
                left = pltpu.roll(value, 96, 1)
                right = pltpu.roll(value, 32, 1)
                cross = cross_y * jnp.where(cross_left, left, right) + cross_x * value
                plain = jnp.where(plain_left, left, jnp.where(plain_extra, moved, 0.0))
                parts.append((value, wave_x * left, cross, plain))
            (a_re, x_re, c_re, p_re), (a_im, x_im, c_im, p_im) = parts
            for top, left, value in (
                (0, 0, jnp.where(plain_extra, -x_im, a_re)),
                (HALF, 0, jnp.where(plain_extra, x_re, a_im)),
                (0, 128, p_re - c_im),
                (HALF, 128, p_im + c_re),
            ):
                high, low = split(value)
                lanes = slice(left, left + 128)
                target[top : top + HALF, lanes] = high
                target[GRID + top : GRID + top + HALF, lanes] = low
                target[2 * GRID + top : 2 * GRID + top + HALF, lanes] = high
            results.append(dot((t_even, t_odd)[parity][...], target[...], NN))
        from_even, from_odd = results
        near = (from_even + from_odd).astype(BF16)
        far = (from_even - from_odd).astype(BF16)
        z = step_c * 4 + step
        for q in range(2):
            lanes = slice(q * 256, q * 256 + 256)
            field[z, 0:HALF, lanes] = near[q * HALF : q * HALF + HALF]
            field[z, HALF:GRID, lanes] = far[q * HALF : q * HALF + HALF]
            field[z, GRID : GRID + 16, lanes] = near[q * HALF : q * HALF + 16]

    @pl.when(step_c == len(steps) - 1)
    def _():
        if previous is None:
            out[...] = jnp.zeros_like(out)
        else:
            out[...] = previous[...]

        for owner in range(N_GY):
            block = field[:, owner * 32 : owner * 32 + WINDOW, :]
            window[owner] = block.reshape(depth * WINDOW, 512).T

        def one_pair(pair, carry):
            base = 2 * (pair & (AHEAD - 1))
            for copy in copies(pair, base):
                copy.wait()

            @pl.when(pair + AHEAD - 1 < pairs)
            def _():
                for copy in copies(pair + AHEAD - 1, 2 * ((pair + AHEAD - 1) & (AHEAD - 1))):
                    copy.start()

            for side in range(2):
                job = 2 * pair + side
                owner, block = place[HEAD + 2 * JOBS + job], place[HEAD + JOBS + job]
                lanes = pl.ds(pl.multiple_of(block * BLOCK, BLOCK), BLOCK)
                summed = dot(window[owner], plane[base + side], NN).reshape(2, 8, 32, BLOCK)
                turn = phase[base + side]
                product = summed[0] * turn[None, 0:32] + summed[1] * turn[None, 32:64]
                value = jnp.sum(product, axis=1)
                if previous is not None:
                    value = value + previous[owner, :, lanes]
                out[owner, :, lanes] = value
            return carry

        lax.fori_loop(0, pairs, one_pair, 0)


def field_stage(steps, first, place, main, extra, extra_at, t_even, t_odd, rows, previous):
    def whole(shape):
        return pl.BlockSpec(
            shape, lambda i, _: (0,) * len(shape), pipeline_mode=pl.Buffered(1)
        )

    def kernel(*refs):
        field_kernel(steps, *refs)

    piece = (N_GX, None, 2, 8, 8, 128)
    in_specs = [
        pl.BlockSpec(piece, lambda i, _: (0, first + i, 0, 0, 0, 0)),
        pl.BlockSpec(piece, lambda i, _: (0, extra_at, 0, 0, 0, 0)),
        whole((256, 768)),
        whole((256, 768)),
        pl.BlockSpec(memory_space=pl.ANY),
        pl.BlockSpec(memory_space=pl.ANY),
    ]
    operands = [place, main, extra, t_even, t_odd, *rows]
    if previous is not None:
        in_specs.append(whole((N_GY, 8, ROWS)))
        operands.append(previous)
    depth = 4 * len(steps)
    return pl.pallas_call(
        kernel,
        out_shape=jax.ShapeDtypeStruct((N_GY, 8, ROWS), F32),
        grid_spec=pltpu.PrefetchScalarGridSpec(
            num_scalar_prefetch=1,
            grid=(len(steps),),
            in_specs=in_specs,
            out_specs=whole((N_GY, 8, ROWS)),
            scratch_shapes=[
                pltpu.VMEM((depth, GRID + 16, 512), BF16),
                pltpu.VMEM((768, 256), BF16),
                pltpu.VMEM((768, 256), BF16),
                pltpu.VMEM((768, 256), BF16),
                pltpu.VMEM((768, 256), BF16),
                pltpu.VMEM((N_GY, 512, depth * WINDOW), BF16),
                pltpu.VMEM((2 * AHEAD, 64, BLOCK), F32),
                pltpu.VMEM((2 * AHEAD, depth * WINDOW, BLOCK), BF16),
                pltpu.SemaphoreType.DMA((2, 2 * AHEAD)),
            ],
        ),
        name="field_stage",
    )(*operands)


def ghost_kernel(counts, values, slots, own, back):
    total = values[0]
    for source in range(1, N_GY):
        total = total + values[source]
    lane = lax.broadcasted_iota(jnp.int32, (8, OWN), 1)
    own[...] = jnp.where(lane < counts[0, 0], total[:, :OWN], 0.0)
    ghosts = pltpu.roll(total, ROWS - counts[0, 0], 1)[:, :GHOST]
    cell = lax.broadcasted_iota(jnp.int32, (OWN, GHOST), 0)
    chosen = (cell == slots[1:2]).astype(F32).astype(BF16)
    first, _ = split(ghosts)
    second, third = split(ghosts - first.astype(F32))
    parts = jnp.concatenate([first.astype(F32), second.astype(F32), third.astype(F32)], axis=0)
    placed = dot(parts.astype(BF16), chosen, NT)
    back[...] = placed[0:8] + (placed[8:16] + placed[16:24])


def ghost_stage(counts, values, slots):
    vmem = pl.BlockSpec(memory_space=pltpu.VMEM)
    return pl.pallas_call(
        ghost_kernel,
        out_shape=(
            jax.ShapeDtypeStruct((8, OWN), F32),
            jax.ShapeDtypeStruct((8, OWN), F32),
        ),
        in_specs=[pl.BlockSpec(memory_space=pltpu.SMEM), vmem, vmem],
        out_specs=(vmem, vmem),
        name="ghost_stage",
    )(counts, values, slots)


def job_list(live, owners, index_gx, index_gy):
    needed = (live + BLOCK - 1) // BLOCK
    valid = jnp.arange(BLOCKS, dtype=jnp.int32)[None, :] < needed[:, None]
    valid = valid.reshape(-1).astype(jnp.int32)
    item = jnp.arange(N_GY * BLOCKS, dtype=jnp.int32)
    before = jnp.sum(jnp.where(item[None, :] < item[:, None], valid[None, :], 0), axis=1)
    jobs = jnp.sum(valid)
    wanted = jnp.minimum(jnp.arange(JOBS, dtype=jnp.int32), jobs - 1)
    chosen = (before[None, :] == wanted[:, None]) & (valid[None, :] > 0)
    found = jnp.sum(jnp.where(chosen, item[None, :], 0), axis=1)
    entry = found // BLOCKS
    at_entry = entry[:, None] == jnp.arange(N_GY, dtype=jnp.int32)[None, :]
    owner = jnp.sum(jnp.where(at_entry, owners[None, :], 0), axis=1)
    return jnp.concatenate(
        [jnp.stack([index_gx, index_gy, jobs]), entry, found % BLOCKS, owner]
    )


def per_device(
    source_hat, particle_start, particle_offset, ghost_start, ghost_offset, ghost_slot, counts
):
    index_gx = lax.axis_index("gx").astype(jnp.int32)
    index_gy = lax.axis_index("gy").astype(jnp.int32)
    members = range(N_GY)
    mine = gather_stage(counts, particle_start, particle_offset, ghost_start, ghost_offset)
    partner = lax.ppermute(mine, "gy", [(i, i ^ 1) for i in members])

    table_z = jnp.asarray(left_triple(z_table()))
    twiddle = jnp.asarray(twiddles())
    sent = [
        z_stage(chunk + ((EXTRA,) if number == 0 else ()), source_hat, table_z, twiddle)
        for number, chunk in enumerate(CHUNKS)
    ]
    received = [
        lax.all_to_all(piece, "gx", split_axis=0, concat_axis=0, tiled=True)
        for piece in sent
    ]
    pair = jnp.stack([mine, partner])
    pairs = [pair]
    for shift in (2, 6, 4):
        route = [(i, (i + shift) % N_GY) for i in members]
        pairs.append(lax.ppermute(pair, "gy", route))
    particles = jnp.concatenate(pairs, axis=0)
    shifts = jnp.array([0, 0, 2, 2, 6, 6, 4, 4], jnp.int32)
    owners = jnp.bitwise_xor(
        (index_gy - shifts) & (N_GY - 1), jnp.arange(N_GY, dtype=jnp.int32) & 1
    )
    place = job_list(particles[:, 7, 0].astype(jnp.int32), owners, index_gx, index_gy)
    table_y = jnp.asarray(left_triple(y_table()))
    table_y = lax.dynamic_index_in_dim(table_y, index_gy, 0, keepdims=False)
    rows = row_stage(place, particles, table_y)

    t_even = jnp.asarray(left_triple(x_table(0)))
    t_odd = jnp.asarray(left_triple(x_table(1)))
    partial = None
    for number, chunk in enumerate(CHUNKS):
        partial = field_stage(
            chunk, 0, place, received[number], received[0], len(CHUNKS[0]),
            t_even, t_odd, rows, partial,
        )
    partial = lax.all_to_all(partial, "gy", split_axis=0, concat_axis=0, tiled=True)
    own, back = ghost_stage(counts, partial, ghost_slot)
    devices = range(N_GX)
    route = [((i + 1) % N_GX, i) for i in devices]
    arrived = lax.ppermute(back, "gx", route)
    return (own[:3] + arrived[:3], own[3:] + arrived[3:])


def solution(mesh):
    in_specs = (
        P(None, None, "gx", "gy", None),
        P(None, ("gx", "gy")),
        P(None, ("gx", "gy")),
        P(None, None, ("gx", "gy")),
        P(None, None, ("gx", "gy")),
        P(None, ("gx", "gy")),
        P(("gx", "gy"), None),
    )
    out_specs = (P(None, ("gx", "gy")), P(None, ("gx", "gy")))
    return jax.shard_map(
        per_device, mesh=mesh, in_specs=in_specs, out_specs=out_specs, check_vma=False
    )
```

```python
import math

import jax
import jax.numpy as jnp
import numpy as np
from jax import lax
from jax.experimental import pallas as pl
from jax.experimental.pallas import tpu as pltpu
from jax.sharding import PartitionSpec as P


F32 = jnp.float32
BF16 = jnp.bfloat16
SUPPORT = 8
GRID = 256
HALF = GRID // 2
N_GX = 16
N_GY = 8
OWN = 2048
GHOST = 512
ROWS = OWN + GHOST
WAVE = 2.0 * math.pi / GRID
WINDOW = 48
BLOCK = 256
CHUNKS = ((0, 1, 2, 3),)
EXTRA = 4
BLOCKS = ROWS // BLOCK
JOBS = N_GY * BLOCKS + 2
HEAD = 3
AHEAD = 8


def numpy_halves(table):
    import ml_dtypes

    high = table.astype(ml_dtypes.bfloat16)
    low = (table - high.astype(np.float64)).astype(ml_dtypes.bfloat16)
    return high, low


def left_triple(table):
    high, low = numpy_halves(table)
    return np.concatenate([high, high, low], axis=-1)


def z_table():
    c1, slab, part, step = np.meshgrid(
        np.arange(2), np.arange(N_GX), np.arange(2), np.arange(4), indexing="ij"
    )
    position = (8 * slab + 2 * step + c1).reshape(-1, 1)
    part = part.reshape(-1, 1)
    angle = (position * np.arange(HALF)[None, :] % HALF) * (2.0 * np.pi / HALF)
    cosine, sine = np.cos(angle), np.sin(angle)
    from_real = np.where(part == 0, cosine, sine)
    from_imag = np.where(part == 0, -sine, cosine)
    return np.concatenate([from_real, from_imag], axis=1)


def x_table(parity):
    modes = 2 * np.arange(HALF) + parity
    angle = (np.arange(HALF)[:, None] * modes[None, :] % GRID) * (2.0 * np.pi / GRID)
    cosine, sine = np.cos(angle), np.sin(angle)
    return np.block([[cosine, -sine], [sine, cosine]])


def y_table():
    index = np.arange(GRID)
    angle = (index[:, None] * index[None, :] % GRID) * (2.0 * np.pi / GRID)
    cosine = np.cos(angle).reshape(N_GY, 1, GRID // N_GY, GRID)
    sine = -np.sin(angle).reshape(N_GY, 1, GRID // N_GY, GRID)
    return np.concatenate([cosine, sine], axis=1).reshape(N_GY, 2 * (GRID // N_GY), GRID)


def twiddles():
    angle = np.arange(HALF) * (2.0 * np.pi / GRID)
    table = np.stack([np.cos(angle), np.sin(angle)])
    return np.repeat(table[:, None, :], 32, axis=1).astype(np.float32)


def split(value):
    high = value.astype(BF16)
    return high, (value - high.astype(F32)).astype(BF16)


def signed(index):
    return jnp.where(index < GRID // 2, index, index - GRID).astype(F32)


NT = (((1,), (1,)), ((), ()))
NN = (((1,), (0,)), ((), ()))


def dot(a, b, dims):
    return lax.dot_general(a, b, dims, preferred_element_type=F32)


def z_kernel(pieces, source, table, twiddle, out, even, odd):
    quad = pl.program_id(0)
    with_extra = EXTRA in pieces
    parities = [p for p in range(2) if with_extra or any(c % 2 == p for c in pieces)]
    row = lax.broadcasted_iota(jnp.int32, (32, GRID), 0)
    mode_y = signed(row + lax.axis_index("gy") * 32)
    mode_z = signed(lax.broadcasted_iota(jnp.int32, (32, GRID), 1))
    half_wave_z = 0.5 * WAVE * mode_z
    partial_square = mode_y * mode_y + mode_z * mode_z
    turn_re, turn_im = twiddle[0], twiddle[1]

    def build(k):
        index_x = lax.axis_index("gx") * 16 + quad * 4 + k
        mode_x = jnp.where(index_x < GRID // 2, index_x, index_x - GRID).astype(F32)
        inverse = 1.0 / jnp.maximum(mode_x * mode_x + partial_square, 1.0)
        v = []
        for r in range(2):
            s1, s2, s3 = source[r, 0, k], source[r, 1, k], source[r, 2, k]
            ratio = (s1 * mode_x + s2 * mode_y + s3 * mode_z) * inverse
            v.append((s1 - mode_x * ratio, s2 - mode_y * ratio, s3 - mode_z * ratio))
        rows = [
            (v[0][0], v[1][0], k * 128),
            (v[0][1], v[1][1], k * 128 + 32),
            (v[0][2], v[1][2], k * 128 + 64),
            (-half_wave_z * v[1][0], half_wave_z * v[0][0], k * 128 + 96),
        ]
        if with_extra:
            rows.append((-half_wave_z * v[1][1], half_wave_z * v[0][1], 512 + k * 32))
        for real, imag, start in rows:
            here = slice(start, start + 32)
            for p in parities:
                if p == 0:
                    re = real[:, :HALF] + real[:, HALF:]
                    im = imag[:, :HALF] + imag[:, HALF:]
                    target = even
                else:
                    re0 = real[:, :HALF] - real[:, HALF:]
                    im0 = imag[:, :HALF] - imag[:, HALF:]
                    re = re0 * turn_re - im0 * turn_im
                    im = re0 * turn_im + im0 * turn_re
                    target = odd
                for r, value in ((0, re), (1, im)):
                    high, low = split(value)
                    target[here, r * HALF : (r + 1) * HALF] = high
                    target[here, GRID + r * HALF : GRID + (r + 1) * HALF] = low
                    target[here, 2 * GRID + r * HALF : 2 * GRID + (r + 1) * HALF] = high

    def transform(pair):
        for p in parities:
            wanted = [c for c in pieces if c != EXTRA and c % 2 == p]
            if not wanted:
                continue
            c_low, c_high = min(wanted) // 2, max(wanted) // 2 + 1
            data = (even, odd)[p][pair * 256 : pair * 256 + 256]
            result = dot(table[c_low * 128 : c_high * 128], data, NT)
            for c in wanted:
                top = (c // 2 - c_low) * 128
                for side in range(2):
                    out[:, pieces.index(c), side, pair] = result[
                        top : top + 128, side * 128 : side * 128 + 128
                    ].reshape(N_GX, 8, 128)

    build(0)
    build(1)
    transform(0)
    build(2)
    build(3)
    transform(1)
    if with_extra:
        halves = [dot(table[...], data[512:640], NT) for data in (even, odd)]
        v = [halves[c % 2][(c // 2) * 128 : (c // 2) * 128 + 128] for c in range(4)]
        lane = lax.broadcasted_iota(jnp.int32, (128, 128), 1)
        lower64 = lane < 64
        lower32 = (lane & 32) == 0
        p0 = [jnp.where(lower64, v[c], pltpu.roll(v[c + 2], 64, 1)) for c in range(2)]
        p1 = [jnp.where(lower64, pltpu.roll(v[c], 64, 1), v[c + 2]) for c in range(2)]
        place_of = pieces.index(EXTRA)
        for k1, p in ((0, p0), (1, p1)):
            q0 = jnp.where(lower32, p[0], pltpu.roll(p[1], 32, 1))
            q1 = jnp.where(lower32, pltpu.roll(p[0], 96, 1), p[1])
            out[:, place_of, 0, k1] = q0.reshape(N_GX, 8, 128)
            out[:, place_of, 1, k1] = q1.reshape(N_GX, 8, 128)


def z_stage(pieces, source, table, twiddle):
    def kernel(*refs):
        z_kernel(pieces, *refs)

    return pl.pallas_call(
        kernel,
        out_shape=jax.ShapeDtypeStruct((N_GX, len(pieces), 2, 8, 8, 128), F32),
        grid=(4,),
        in_specs=[
            pl.BlockSpec((2, 3, 4, 32, GRID), lambda i: (0, 0, i, 0, 0)),
            pl.BlockSpec((256, 768), lambda i: (0, 0)),
            pl.BlockSpec((2, 32, HALF), lambda i: (0, 0, 0)),
        ],
        out_specs=pl.BlockSpec(
            (N_GX, len(pieces), 2, 2, 8, 128), lambda i: (0, 0, 0, i, 0, 0)
        ),
        scratch_shapes=[pltpu.VMEM((640, 768), BF16), pltpu.VMEM((640, 768), BF16)],
        name="z_stage",
    )(source, table, twiddle)


def weight(distance, offset):
    shifted = distance - (SUPPORT // 2 - 1) - offset
    inside = (distance >= 0.0) & (distance < SUPPORT)
    return jnp.where(inside, jnp.exp(-5.6 / SUPPORT * shifted * shifted), 0.0)


def wrapped(distance):
    return jnp.where(distance < 0.0, distance + GRID, distance)


def gather_kernel(counts, start, offset, other_start, other_offset, out, packed):
    own, ghosts = counts[0, 0], counts[0, 2]
    lane = lax.broadcasted_iota(jnp.int32, (8, ROWS), 1)
    packed[...] = jnp.zeros_like(packed)
    packed[0:3, :GHOST] = other_start[:, 1].astype(F32)
    packed[3:6, :GHOST] = other_offset[:, 1]
    moved = pltpu.roll(packed[...], own, 1)
    packed[0:3, :OWN] = start[...].astype(F32)
    packed[3:6, :OWN] = offset[...]
    out[...] = jnp.where(lane < own, packed[...], moved)
    lane = lane[0:1]
    out[6:7, :] = jnp.where(lane < own + ghosts, 1.0, 0.0)
    out[7:8, :] = jnp.where(lane == 0, own + ghosts, 0).astype(F32)


def gather_stage(counts, start, offset, other_start, other_offset):
    vmem = pl.BlockSpec(memory_space=pltpu.VMEM)
    return pl.pallas_call(
        gather_kernel,
        out_shape=jax.ShapeDtypeStruct((8, ROWS), F32),
        in_specs=[
            pl.BlockSpec(memory_space=pltpu.SMEM),
            vmem,
            vmem,
            vmem,
            vmem,
        ],
        out_specs=vmem,
        scratch_shapes=[pltpu.VMEM((8, ROWS), F32)],
        name="gather_stage",
    )(counts, start, offset, other_start, other_offset)


def row_kernel(place, particles, table, phases, planes, phase, plane, sent_phase, sent_plane):
    y_cell = lax.broadcasted_iota(jnp.int32, (GRID, BLOCK), 0).astype(F32)
    x_cell = lax.broadcasted_iota(jnp.int32, (WINDOW, BLOCK), 0).astype(F32)
    local_z = lax.broadcasted_iota(jnp.int32, (16, BLOCK), 0)
    z_cell = (place[0] * 16 + 4 * (local_z % 4) + local_z // 4).astype(F32)
    jobs = 2 * ((place[2] + 1) // 2)

    def copies(slot, job):
        return (
            pltpu.make_async_copy(phase.at[slot], phases.at[job], sent_phase.at[slot]),
            pltpu.make_async_copy(plane.at[slot], planes.at[job], sent_plane.at[slot]),
        )

    def one_job(job, carry):
        slot = job & 1

        @pl.when(job >= 2)
        def _():
            for copy in copies(slot, job):
                copy.wait()

        entry, block = place[HEAD + job], place[HEAD + JOBS + job]
        owner = place[HEAD + 2 * JOBS + job]
        data = particles[entry, :, pl.ds(pl.multiple_of(block * BLOCK, BLOCK), BLOCK)]
        weight_y = weight(wrapped(y_cell - data[1:2]), data[4:5])
        high, low = split(weight_y)
        phase[slot] = dot(table[...], jnp.concatenate([high, low, high], axis=0), NN)
        weight_x = weight(x_cell + (owner * 32).astype(F32) - data[0:1], data[3:4])
        weight_z = weight(wrapped(z_cell - data[2:3]), data[5:6]) * data[6:7]
        for z in range(16):
            plane[slot, z * WINDOW : (z + 1) * WINDOW] = (weight_x * weight_z[z : z + 1]).astype(
                BF16
            )
        for copy in copies(slot, job):
            copy.start()
        return carry

    lax.fori_loop(0, jobs, one_job, 0)
    for slot in range(2):

        @pl.when(jobs > slot)
        def _():
            for copy in copies(slot, 0):
                copy.wait()


def row_stage(place, particles, table):
    return pl.pallas_call(
        row_kernel,
        out_shape=(
            jax.ShapeDtypeStruct((JOBS, 64, BLOCK), F32),
            jax.ShapeDtypeStruct((JOBS, 16 * WINDOW, BLOCK), BF16),
        ),
        grid_spec=pltpu.PrefetchScalarGridSpec(
            num_scalar_prefetch=1,
            grid=(1,),
            in_specs=[
                pl.BlockSpec((N_GY, 8, ROWS), lambda i, _: (0, 0, 0)),
                pl.BlockSpec((64, 768), lambda i, _: (0, 0)),
            ],
            out_specs=(pl.BlockSpec(memory_space=pl.ANY), pl.BlockSpec(memory_space=pl.ANY)),
            scratch_shapes=[
                pltpu.VMEM((2, 64, BLOCK), F32),
                pltpu.VMEM((2, 16 * WINDOW, BLOCK), BF16),
                pltpu.SemaphoreType.DMA((2,)),
                pltpu.SemaphoreType.DMA((2,)),
            ],
        ),
        name="row_stage",
    )(place, particles, table)


def field_kernel(steps, place, main, extra, t_even, t_odd, phases, planes, *rest):
    previous = rest[0] if len(rest) == 11 else None
    out, field, work0, work1, work2, work3, window, phase, plane, arrived = rest[-10:]
    work = (work0, work1, work2, work3)
    first_c = steps[0]
    depth = 4 * len(steps)
    step_c = pl.program_id(0)
    c = first_c + step_c
    pairs = (place[2] + 1) // 2

    def copies(pair, base):
        found = []
        for side in range(2):
            job, slot = 2 * pair + side, base + side
            rows = pl.ds(first_c * 4 * WINDOW, depth * WINDOW)
            found.append(
                pltpu.make_async_copy(phases.at[job], phase.at[slot], arrived.at[0, slot])
            )
            found.append(
                pltpu.make_async_copy(planes.at[job, rows], plane.at[slot], arrived.at[1, slot])
            )
        return found

    for ahead in range(AHEAD - 1):

        @pl.when((step_c == 0) & (pairs > ahead))
        def _():
            for copy in copies(ahead, 2 * ahead):
                copy.start()

    lane = lax.broadcasted_iota(jnp.int32, (HALF, 128), 1)
    group = lane // 32
    row = lax.broadcasted_iota(jnp.int32, (HALF, 128), 0)
    wave_y = WAVE * signed(lane % 32 + place[1] * 32)
    cross_y = jnp.where(group == 0, wave_y, jnp.where(group == 2, 0.0, 0.5 * wave_y))
    half_same = jnp.where((group == 1) | (group == 2), 0.5, 0.0)
    plain_left = group == 2
    plain_extra = group == 3
    cross_left = group == 0
    flat_main = main.reshape(GRID * 8, 128)
    flat_extra = extra.reshape(GRID * 8, 128)
    waves = [WAVE * signed(2 * row + parity) for parity in range(2)]
    for step in range(4):
        results = []
        for parity in range(2):
            target = work[2 * (step % 2) + parity]
            wave_x = waves[parity]
            cross_x = half_same * wave_x

            def load(flat, q):
                top = parity * 64 + q * 4 + step
                return jnp.concatenate(
                    [flat[pl.ds(source * 128 + top, 8, stride=8), :] for source in range(N_GX)]
                )

            parts = []
            for q in range(2):
                value = load(flat_main, q)
                moved = pltpu.roll(load(flat_extra, q), 32 * (3 - c), 1)
                left = pltpu.roll(value, 96, 1)
                right = pltpu.roll(value, 32, 1)
                cross = cross_y * jnp.where(cross_left, left, right) + cross_x * value
                plain = jnp.where(plain_left, left, jnp.where(plain_extra, moved, 0.0))
                parts.append((value, wave_x * left, cross, plain))
            (a_re, x_re, c_re, p_re), (a_im, x_im, c_im, p_im) = parts
            for top, left, value in (
                (0, 0, jnp.where(plain_extra, -x_im, a_re)),
                (HALF, 0, jnp.where(plain_extra, x_re, a_im)),
                (0, 128, p_re - c_im),
                (HALF, 128, p_im + c_re),
            ):
                high, low = split(value)
                lanes = slice(left, left + 128)
                target[top : top + HALF, lanes] = high
                target[GRID + top : GRID + top + HALF, lanes] = low
                target[2 * GRID + top : 2 * GRID + top + HALF, lanes] = high
            results.append(dot((t_even, t_odd)[parity][...], target[...], NN))
        from_even, from_odd = results
        near = (from_even + from_odd).astype(BF16)
        far = (from_even - from_odd).astype(BF16)
        z = step_c * 4 + step
        for q in range(2):
            lanes = slice(q * 256, q * 256 + 256)
            field[z, 0:HALF, lanes] = near[q * HALF : q * HALF + HALF]
            field[z, HALF:GRID, lanes] = far[q * HALF : q * HALF + HALF]
            field[z, GRID : GRID + 16, lanes] = near[q * HALF : q * HALF + 16]

    @pl.when(step_c == len(steps) - 1)
    def _():
        if previous is None:
            out[...] = jnp.zeros_like(out)
        else:
            out[...] = previous[...]

        for owner in range(N_GY):
            block = field[:, owner * 32 : owner * 32 + WINDOW, :]
            window[owner] = block.reshape(depth * WINDOW, 512).T

        def one_pair(pair, carry):
            base = 2 * (pair & (AHEAD - 1))
            for copy in copies(pair, base):
                copy.wait()

            @pl.when(pair + AHEAD - 1 < pairs)
            def _():
                for copy in copies(pair + AHEAD - 1, 2 * ((pair + AHEAD - 1) & (AHEAD - 1))):
                    copy.start()

            for side in range(2):
                job = 2 * pair + side
                owner, block = place[HEAD + 2 * JOBS + job], place[HEAD + JOBS + job]
                lanes = pl.ds(pl.multiple_of(block * BLOCK, BLOCK), BLOCK)
                summed = dot(window[owner], plane[base + side], NN).reshape(2, 8, 32, BLOCK)
                turn = phase[base + side]
                product = summed[0] * turn[None, 0:32] + summed[1] * turn[None, 32:64]
                value = jnp.sum(product, axis=1)
                if previous is not None:
                    value = value + previous[owner, :, lanes]
                out[owner, :, lanes] = value
            return carry

        lax.fori_loop(0, pairs, one_pair, 0)


def field_stage(steps, first, place, main, extra, extra_at, t_even, t_odd, rows, previous):
    def whole(shape):
        return pl.BlockSpec(
            shape, lambda i, _: (0,) * len(shape), pipeline_mode=pl.Buffered(1)
        )

    def kernel(*refs):
        field_kernel(steps, *refs)

    piece = (N_GX, None, 2, 8, 8, 128)
    in_specs = [
        pl.BlockSpec(piece, lambda i, _: (0, first + i, 0, 0, 0, 0)),
        pl.BlockSpec(piece, lambda i, _: (0, extra_at, 0, 0, 0, 0)),
        whole((256, 768)),
        whole((256, 768)),
        pl.BlockSpec(memory_space=pl.ANY),
        pl.BlockSpec(memory_space=pl.ANY),
    ]
    operands = [place, main, extra, t_even, t_odd, *rows]
    if previous is not None:
        in_specs.append(whole((N_GY, 8, ROWS)))
        operands.append(previous)
    depth = 4 * len(steps)
    return pl.pallas_call(
        kernel,
        out_shape=jax.ShapeDtypeStruct((N_GY, 8, ROWS), F32),
        grid_spec=pltpu.PrefetchScalarGridSpec(
            num_scalar_prefetch=1,
            grid=(len(steps),),
            in_specs=in_specs,
            out_specs=whole((N_GY, 8, ROWS)),
            scratch_shapes=[
                pltpu.VMEM((depth, GRID + 16, 512), BF16),
                pltpu.VMEM((768, 256), BF16),
                pltpu.VMEM((768, 256), BF16),
                pltpu.VMEM((768, 256), BF16),
                pltpu.VMEM((768, 256), BF16),
                pltpu.VMEM((N_GY, 512, depth * WINDOW), BF16),
                pltpu.VMEM((2 * AHEAD, 64, BLOCK), F32),
                pltpu.VMEM((2 * AHEAD, depth * WINDOW, BLOCK), BF16),
                pltpu.SemaphoreType.DMA((2, 2 * AHEAD)),
            ],
        ),
        name="field_stage",
    )(*operands)


def ghost_kernel(counts, values, slots, own, back):
    total = values[0]
    for source in range(1, N_GY):
        total = total + values[source]
    lane = lax.broadcasted_iota(jnp.int32, (8, OWN), 1)
    own[...] = jnp.where(lane < counts[0, 0], total[:, :OWN], 0.0)
    ghosts = pltpu.roll(total, ROWS - counts[0, 0], 1)[:, :GHOST]
    cell = lax.broadcasted_iota(jnp.int32, (OWN, GHOST), 0)
    chosen = (cell == slots[1:2]).astype(F32).astype(BF16)
    first, _ = split(ghosts)
    second, third = split(ghosts - first.astype(F32))
    parts = jnp.concatenate([first.astype(F32), second.astype(F32), third.astype(F32)], axis=0)
    placed = dot(parts.astype(BF16), chosen, NT)
    back[...] = placed[0:8] + (placed[8:16] + placed[16:24])


def ghost_stage(counts, values, slots):
    vmem = pl.BlockSpec(memory_space=pltpu.VMEM)
    return pl.pallas_call(
        ghost_kernel,
        out_shape=(
            jax.ShapeDtypeStruct((8, OWN), F32),
            jax.ShapeDtypeStruct((8, OWN), F32),
        ),
        in_specs=[pl.BlockSpec(memory_space=pltpu.SMEM), vmem, vmem],
        out_specs=(vmem, vmem),
        name="ghost_stage",
    )(counts, values, slots)


def final_kernel(own, arrived, velocity, strain):
    total = own[...] + arrived[...]
    velocity[...] = total[:3]
    strain[...] = total[3:]


def final_stage(own, arrived):
    return pl.pallas_call(
        final_kernel,
        out_shape=(
            jax.ShapeDtypeStruct((3, OWN), F32),
            jax.ShapeDtypeStruct((5, OWN), F32),
        ),
        name="final_stage",
    )(own, arrived)


def job_list(live, owners, index_gx, index_gy):
    needed = (live + BLOCK - 1) // BLOCK
    valid = jnp.arange(BLOCKS, dtype=jnp.int32)[None, :] < needed[:, None]
    valid = valid.reshape(-1).astype(jnp.int32)
    item = jnp.arange(N_GY * BLOCKS, dtype=jnp.int32)
    before = jnp.sum(jnp.where(item[None, :] < item[:, None], valid[None, :], 0), axis=1)
    jobs = jnp.sum(valid)
    wanted = jnp.minimum(jnp.arange(JOBS, dtype=jnp.int32), jobs - 1)
    chosen = (before[None, :] == wanted[:, None]) & (valid[None, :] > 0)
    found = jnp.sum(jnp.where(chosen, item[None, :], 0), axis=1)
    entry = found // BLOCKS
    at_entry = entry[:, None] == jnp.arange(N_GY, dtype=jnp.int32)[None, :]
    owner = jnp.sum(jnp.where(at_entry, owners[None, :], 0), axis=1)
    return jnp.concatenate(
        [jnp.stack([index_gx, index_gy, jobs]), entry, found % BLOCKS, owner]
    )


def per_device(
    source_hat, particle_start, particle_offset, ghost_start, ghost_offset, ghost_slot, counts
):
    index_gx = lax.axis_index("gx").astype(jnp.int32)
    index_gy = lax.axis_index("gy").astype(jnp.int32)
    members = range(N_GY)
    mine = gather_stage(counts, particle_start, particle_offset, ghost_start, ghost_offset)
    partner = lax.ppermute(mine, "gy", [(i, i ^ 1) for i in members])

    table_z = jnp.asarray(left_triple(z_table()))
    twiddle = jnp.asarray(twiddles())
    sent = [
        z_stage(chunk + ((EXTRA,) if number == 0 else ()), source_hat, table_z, twiddle)
        for number, chunk in enumerate(CHUNKS)
    ]
    received = [
        lax.all_to_all(piece, "gx", split_axis=0, concat_axis=0, tiled=True)
        for piece in sent
    ]
    pair = jnp.stack([mine, partner])
    pairs = [pair]
    for shift in (2, 6, 4):
        route = [(i, (i + shift) % N_GY) for i in members]
        pairs.append(lax.ppermute(pair, "gy", route))
    particles = jnp.concatenate(pairs, axis=0)
    shifts = jnp.array([0, 0, 2, 2, 6, 6, 4, 4], jnp.int32)
    owners = jnp.bitwise_xor(
        (index_gy - shifts) & (N_GY - 1), jnp.arange(N_GY, dtype=jnp.int32) & 1
    )
    place = job_list(particles[:, 7, 0].astype(jnp.int32), owners, index_gx, index_gy)
    table_y = jnp.asarray(left_triple(y_table()))
    table_y = lax.dynamic_index_in_dim(table_y, index_gy, 0, keepdims=False)
    rows = row_stage(place, particles, table_y)

    t_even = jnp.asarray(left_triple(x_table(0)))
    t_odd = jnp.asarray(left_triple(x_table(1)))
    partial = None
    for number, chunk in enumerate(CHUNKS):
        partial = field_stage(
            chunk, 0, place, received[number], received[0], len(CHUNKS[0]),
            t_even, t_odd, rows, partial,
        )
    partial = lax.all_to_all(partial, "gy", split_axis=0, concat_axis=0, tiled=True)
    own, back = ghost_stage(counts, partial, ghost_slot)
    devices = range(N_GX)
    route = [((i + 1) % N_GX, i) for i in devices]
    return final_stage(own, lax.ppermute(back, "gx", route))


def solution(mesh):
    in_specs = (
        P(None, None, "gx", "gy", None),
        P(None, ("gx", "gy")),
        P(None, ("gx", "gy")),
        P(None, None, ("gx", "gy")),
        P(None, None, ("gx", "gy")),
        P(None, ("gx", "gy")),
        P(("gx", "gy"), None),
    )
    out_specs = (P(None, ("gx", "gy")), P(None, ("gx", "gy")))
    return jax.shard_map(
        per_device, mesh=mesh, in_specs=in_specs, out_specs=out_specs, check_vma=False
    )
```

```python
import math

import jax
import jax.numpy as jnp
import numpy as np
from jax import lax
from jax.experimental import pallas as pl
from jax.experimental.pallas import tpu as pltpu
from jax.sharding import PartitionSpec as P


F32 = jnp.float32
BF16 = jnp.bfloat16
SUPPORT = 8
GRID = 256
HALF = GRID // 2
N_GX = 16
N_GY = 8
OWN = 2048
GHOST = 512
ROWS = OWN + GHOST
WAVE = 2.0 * math.pi / GRID
WINDOW = 48
BLOCK = 256
CHUNKS = ((0, 2), (1, 3))
ORDER = (0, 2, 1, 3)
FIELDS = 7
EXTRA = 4
BLOCKS = ROWS // BLOCK
JOBS = N_GY * BLOCKS + 2
HEAD = 3
AHEAD = 8


def numpy_halves(table):
    import ml_dtypes

    high = table.astype(ml_dtypes.bfloat16)
    low = (table - high.astype(np.float64)).astype(ml_dtypes.bfloat16)
    return high, low


def left_triple(table):
    high, low = numpy_halves(table)
    return np.concatenate([high, high, low], axis=-1)


def z_table():
    c1, slab, part, step = np.meshgrid(
        np.arange(2), np.arange(N_GX), np.arange(2), np.arange(4), indexing="ij"
    )
    position = (8 * slab + 2 * step + c1).reshape(-1, 1)
    part = part.reshape(-1, 1)
    angle = (position * np.arange(HALF)[None, :] % HALF) * (2.0 * np.pi / HALF)
    cosine, sine = np.cos(angle), np.sin(angle)
    from_real = np.where(part == 0, cosine, sine)
    from_imag = np.where(part == 0, -sine, cosine)
    return np.concatenate([from_real, from_imag], axis=1)


def x_table(parity):
    modes = 2 * np.arange(HALF) + parity
    angle = (np.arange(HALF)[:, None] * modes[None, :] % GRID) * (2.0 * np.pi / GRID)
    cosine, sine = np.cos(angle), np.sin(angle)
    return np.block([[cosine, -sine], [sine, cosine]])


def y_table():
    index = np.arange(GRID)
    angle = (index[:, None] * index[None, :] % GRID) * (2.0 * np.pi / GRID)
    cosine = np.cos(angle).reshape(N_GY, 1, GRID // N_GY, GRID)
    sine = -np.sin(angle).reshape(N_GY, 1, GRID // N_GY, GRID)
    return np.concatenate([cosine, sine], axis=1).reshape(N_GY, 2 * (GRID // N_GY), GRID)


def twiddles():
    angle = np.arange(HALF) * (2.0 * np.pi / GRID)
    table = np.stack([np.cos(angle), np.sin(angle)])
    return np.repeat(table[:, None, :], 32, axis=1).astype(np.float32)


def split(value):
    high = value.astype(BF16)
    return high, (value - high.astype(F32)).astype(BF16)


def signed(index):
    return jnp.where(index < GRID // 2, index, index - GRID).astype(F32)


NT = (((1,), (1,)), ((), ()))
NN = (((1,), (0,)), ((), ()))


def dot(a, b, dims):
    return lax.dot_general(a, b, dims, preferred_element_type=F32)


def z_kernel(pieces, source, table, twiddle, out, even, odd):
    quad = pl.program_id(0)
    with_extra = EXTRA in pieces
    parities = [p for p in range(2) if any(c != EXTRA and c % 2 == p for c in pieces)]
    row = lax.broadcasted_iota(jnp.int32, (32, GRID), 0)
    mode_y = signed(row + lax.axis_index("gy") * 32)
    mode_z = signed(lax.broadcasted_iota(jnp.int32, (32, GRID), 1))
    half_wave_z = 0.5 * WAVE * mode_z
    partial_square = mode_y * mode_y + mode_z * mode_z
    turn_re, turn_im = twiddle[0], twiddle[1]

    def build(k):
        index_x = lax.axis_index("gx") * 16 + quad * 4 + k
        mode_x = jnp.where(index_x < GRID // 2, index_x, index_x - GRID).astype(F32)
        inverse = 1.0 / jnp.maximum(mode_x * mode_x + partial_square, 1.0)
        v = []
        for r in range(2):
            s1, s2, s3 = source[r, 0, k], source[r, 1, k], source[r, 2, k]
            ratio = (s1 * mode_x + s2 * mode_y + s3 * mode_z) * inverse
            v.append((s1 - mode_x * ratio, s2 - mode_y * ratio, s3 - mode_z * ratio))
        rows = [
            (v[0][0], v[1][0], k * 128),
            (v[0][1], v[1][1], k * 128 + 32),
            (v[0][2], v[1][2], k * 128 + 64),
            (-half_wave_z * v[1][0], half_wave_z * v[0][0], k * 128 + 96),
        ]
        if with_extra:
            rows.append((-half_wave_z * v[1][1], half_wave_z * v[0][1], 512 + k * 32))
        for real, imag, start in rows:
            here = slice(start, start + 32)
            for p in parities if start < 512 else range(2):
                if p == 0:
                    re = real[:, :HALF] + real[:, HALF:]
                    im = imag[:, :HALF] + imag[:, HALF:]
                    target = even
                else:
                    re0 = real[:, :HALF] - real[:, HALF:]
                    im0 = imag[:, :HALF] - imag[:, HALF:]
                    re = re0 * turn_re - im0 * turn_im
                    im = re0 * turn_im + im0 * turn_re
                    target = odd
                for r, value in ((0, re), (1, im)):
                    high, low = split(value)
                    target[here, r * HALF : (r + 1) * HALF] = high
                    target[here, GRID + r * HALF : GRID + (r + 1) * HALF] = low
                    target[here, 2 * GRID + r * HALF : 2 * GRID + (r + 1) * HALF] = high

    def transform(pair):
        for p in parities:
            wanted = [c for c in pieces if c != EXTRA and c % 2 == p]
            if not wanted:
                continue
            c_low, c_high = min(wanted) // 2, max(wanted) // 2 + 1
            data = (even, odd)[p][pair * 256 : pair * 256 + 256]
            result = dot(table[c_low * 128 : c_high * 128], data, NT)
            for c in wanted:
                top = (c // 2 - c_low) * 128
                for side in range(2):
                    out[:, pieces.index(c), side, pair] = result[
                        top : top + 128, side * 128 : side * 128 + 128
                    ].reshape(N_GX, 8, 128)

    build(0)
    build(1)
    transform(0)
    build(2)
    build(3)
    transform(1)
    if with_extra:
        halves = [dot(table[...], data[512:640], NT) for data in (even, odd)]
        v = [halves[c % 2][(c // 2) * 128 : (c // 2) * 128 + 128] for c in range(4)]
        lane = lax.broadcasted_iota(jnp.int32, (128, 128), 1)
        lower64 = lane < 64
        lower32 = (lane & 32) == 0
        p0 = [jnp.where(lower64, v[c], pltpu.roll(v[c + 2], 64, 1)) for c in range(2)]
        p1 = [jnp.where(lower64, pltpu.roll(v[c], 64, 1), v[c + 2]) for c in range(2)]
        place_of = pieces.index(EXTRA)
        for k1, p in ((0, p0), (1, p1)):
            q0 = jnp.where(lower32, p[0], pltpu.roll(p[1], 32, 1))
            q1 = jnp.where(lower32, pltpu.roll(p[0], 96, 1), p[1])
            out[:, place_of, 0, k1] = q0.reshape(N_GX, 8, 128)
            out[:, place_of, 1, k1] = q1.reshape(N_GX, 8, 128)


def z_stage(pieces, source, table, twiddle):
    def kernel(*refs):
        z_kernel(pieces, *refs)

    return pl.pallas_call(
        kernel,
        out_shape=jax.ShapeDtypeStruct((N_GX, len(pieces), 2, 8, 8, 128), F32),
        grid=(4,),
        in_specs=[
            pl.BlockSpec((2, 3, 4, 32, GRID), lambda i: (0, 0, i, 0, 0)),
            pl.BlockSpec((256, 768), lambda i: (0, 0)),
            pl.BlockSpec((2, 32, HALF), lambda i: (0, 0, 0)),
        ],
        out_specs=pl.BlockSpec(
            (N_GX, len(pieces), 2, 2, 8, 128), lambda i: (0, 0, 0, i, 0, 0)
        ),
        scratch_shapes=[pltpu.VMEM((640, 768), BF16), pltpu.VMEM((640, 768), BF16)],
        name="z_stage",
    )(source, table, twiddle)


def weight(distance, offset):
    shifted = distance - (SUPPORT // 2 - 1) - offset
    inside = (distance >= 0.0) & (distance < SUPPORT)
    return jnp.where(inside, jnp.exp(-5.6 / SUPPORT * shifted * shifted), 0.0)


def wrapped(distance):
    return jnp.where(distance < 0.0, distance + GRID, distance)


def gather_kernel(counts, start, offset, other_start, other_offset, out, packed):
    own, ghosts = counts[0, 0], counts[0, 2]
    lane = lax.broadcasted_iota(jnp.int32, (8, ROWS), 1)
    packed[...] = jnp.zeros_like(packed)
    packed[0:3, :GHOST] = other_start[:, 1].astype(F32)
    packed[3:6, :GHOST] = other_offset[:, 1]
    moved = pltpu.roll(packed[...], own, 1)
    packed[0:3, :OWN] = start[...].astype(F32)
    packed[3:6, :OWN] = offset[...]
    out[...] = jnp.where(lane < own, packed[...], moved)
    lane = lane[0:1]
    out[6:7, :] = jnp.where(lane < own + ghosts, 1.0, 0.0)
    out[7:8, :] = jnp.where(lane == 0, own + ghosts, 0).astype(F32)


def gather_stage(counts, start, offset, other_start, other_offset):
    vmem = pl.BlockSpec(memory_space=pltpu.VMEM)
    return pl.pallas_call(
        gather_kernel,
        out_shape=jax.ShapeDtypeStruct((8, ROWS), F32),
        in_specs=[
            pl.BlockSpec(memory_space=pltpu.SMEM),
            vmem,
            vmem,
            vmem,
            vmem,
        ],
        out_specs=vmem,
        scratch_shapes=[pltpu.VMEM((8, ROWS), F32)],
        name="gather_stage",
    )(counts, start, offset, other_start, other_offset)


def row_kernel(place, particles, table, phases, planes, phase, plane, sent_phase, sent_plane):
    y_cell = lax.broadcasted_iota(jnp.int32, (GRID, BLOCK), 0).astype(F32)
    x_cell = lax.broadcasted_iota(jnp.int32, (WINDOW, BLOCK), 0).astype(F32)
    local_z = lax.broadcasted_iota(jnp.int32, (16, BLOCK), 0)
    turn_of = local_z // 4
    c = 2 * (turn_of & 1) + turn_of // 2
    z_cell = (place[0] * 16 + 4 * (local_z % 4) + c).astype(F32)
    jobs = 2 * ((place[2] + 1) // 2)

    def copies(slot, job):
        return (
            pltpu.make_async_copy(phase.at[slot], phases.at[job], sent_phase.at[slot]),
            pltpu.make_async_copy(plane.at[slot], planes.at[job], sent_plane.at[slot]),
        )

    def one_job(job, carry):
        slot = job & 1

        @pl.when(job >= 2)
        def _():
            for copy in copies(slot, job):
                copy.wait()

        entry, block = place[HEAD + job], place[HEAD + JOBS + job]
        owner = place[HEAD + 2 * JOBS + job]
        data = particles[entry, :, pl.ds(pl.multiple_of(block * BLOCK, BLOCK), BLOCK)]
        weight_y = weight(wrapped(y_cell - data[1:2]), data[4:5])
        high, low = split(weight_y)
        phase[slot] = dot(table[...], jnp.concatenate([high, low, high], axis=0), NN)
        weight_x = weight(x_cell + (owner * 32).astype(F32) - data[0:1], data[3:4])
        weight_z = weight(wrapped(z_cell - data[2:3]), data[5:6]) * data[6:7]
        for z in range(16):
            plane[slot, z * WINDOW : (z + 1) * WINDOW] = (weight_x * weight_z[z : z + 1]).astype(
                BF16
            )
        for copy in copies(slot, job):
            copy.start()
        return carry

    lax.fori_loop(0, jobs, one_job, 0)
    for slot in range(2):

        @pl.when(jobs > slot)
        def _():
            for copy in copies(slot, 0):
                copy.wait()


def row_stage(place, particles, table):
    return pl.pallas_call(
        row_kernel,
        out_shape=(
            jax.ShapeDtypeStruct((JOBS, 64, BLOCK), F32),
            jax.ShapeDtypeStruct((JOBS, 16 * WINDOW, BLOCK), BF16),
        ),
        grid_spec=pltpu.PrefetchScalarGridSpec(
            num_scalar_prefetch=1,
            grid=(1,),
            in_specs=[
                pl.BlockSpec((N_GY, 8, ROWS), lambda i, _: (0, 0, 0)),
                pl.BlockSpec((64, 768), lambda i, _: (0, 0)),
            ],
            out_specs=(pl.BlockSpec(memory_space=pl.ANY), pl.BlockSpec(memory_space=pl.ANY)),
            scratch_shapes=[
                pltpu.VMEM((2, 64, BLOCK), F32),
                pltpu.VMEM((2, 16 * WINDOW, BLOCK), BF16),
                pltpu.SemaphoreType.DMA((2,)),
                pltpu.SemaphoreType.DMA((2,)),
            ],
        ),
        name="row_stage",
    )(place, particles, table)


def field_kernel(steps, place, main, extra, t_even, t_odd, phases, planes, *rest):
    previous = rest[0] if len(rest) == 11 else None
    out, field, work0, work1, work2, work3, window, phase, plane, arrived = rest[-10:]
    work = (work0, work1, work2, work3)
    first_c = ORDER.index(steps[0])
    depth = 4 * len(steps)
    step_c = pl.program_id(0)
    turn_of = first_c + step_c
    c = 2 * (turn_of & 1) + turn_of // 2
    pairs = (place[2] + 1) // 2

    def copies(pair, base):
        found = []
        for side in range(2):
            job, slot = 2 * pair + side, base + side
            rows = pl.ds(first_c * 4 * WINDOW, depth * WINDOW)
            found.append(
                pltpu.make_async_copy(phases.at[job], phase.at[slot], arrived.at[0, slot])
            )
            found.append(
                pltpu.make_async_copy(planes.at[job, rows], plane.at[slot], arrived.at[1, slot])
            )
        return found

    for ahead in range(AHEAD - 1):

        @pl.when((step_c == 0) & (pairs > ahead))
        def _():
            for copy in copies(ahead, 2 * ahead):
                copy.start()

    lane = lax.broadcasted_iota(jnp.int32, (HALF, 128), 1)
    group = lane // 32
    row = lax.broadcasted_iota(jnp.int32, (HALF, 128), 0)
    wave_y = WAVE * signed(lane % 32 + place[1] * 32)
    cross_y = jnp.where((group == 1) | (group == 3), 0.5 * wave_y, 0.0)
    half_same = jnp.where((group == 1) | (group == 2), 0.5, 0.0)
    plain_left = group == 2
    plain_extra = group == 3
    flat_main = main.reshape(GRID * 8, 128)
    flat_extra = extra.reshape(GRID * 8, 128)
    waves = [WAVE * signed(2 * row + parity) for parity in range(2)]
    for step in range(4):
        results = []
        for parity in range(2):
            target = work[2 * (step % 2) + parity]
            wave_x = waves[parity]
            cross_x = half_same * wave_x

            def load(flat, q):
                top = parity * 64 + q * 4 + step
                return jnp.concatenate(
                    [flat[pl.ds(source * 128 + top, 8, stride=8), :] for source in range(N_GX)]
                )

            parts = []
            for q in range(2):
                value = load(flat_main, q)
                moved = pltpu.roll(load(flat_extra, q), 32 * (3 - c), 1)
                left = pltpu.roll(value, 96, 1)
                right = pltpu.roll(value, 32, 1)
                cross = cross_y * right + cross_x * value
                plain = jnp.where(plain_left, left, jnp.where(plain_extra, moved, 0.0))
                parts.append((value, wave_x * left, cross, plain))
            (a_re, x_re, c_re, p_re), (a_im, x_im, c_im, p_im) = parts
            for top, left, value in (
                (0, 0, jnp.where(plain_extra, -x_im, a_re)),
                (HALF, 0, jnp.where(plain_extra, x_re, a_im)),
                (0, 128, p_re - c_im),
                (HALF, 128, p_im + c_re),
            ):
                high, low = split(value)
                lanes = slice(left, left + 128)
                target[top : top + HALF, lanes] = high
                target[GRID + top : GRID + top + HALF, lanes] = low
                target[2 * GRID + top : 2 * GRID + top + HALF, lanes] = high
            results.append(dot((t_even, t_odd)[parity][...], target[...], NN))
        from_even, from_odd = results
        near = (from_even + from_odd).astype(BF16)
        far = (from_even - from_odd).astype(BF16)
        z = step_c * 4 + step
        for q in range(2):
            lanes = slice(q * 256, q * 256 + 256)
            field[z, 0:HALF, lanes] = near[q * HALF : q * HALF + HALF]
            field[z, HALF:GRID, lanes] = far[q * HALF : q * HALF + HALF]
            field[z, GRID : GRID + 16, lanes] = near[q * HALF : q * HALF + 16]

    @pl.when(step_c == len(steps) - 1)
    def _():
        if previous is None:
            out[...] = jnp.zeros_like(out)
        else:
            out[...] = previous[...]

        for owner in range(N_GY):
            block = field[:, owner * 32 : owner * 32 + WINDOW, :]
            turned = block.reshape(depth * WINDOW, 512).T
            for q in range(2):
                top = q * 32 * FIELDS
                window[owner, top : top + 128] = turned[q * 256 : q * 256 + 128]
                window[owner, top + 128 : top + 224] = turned[q * 256 + 160 : q * 256 + 256]
        wave_rows = WAVE * signed(
            lax.broadcasted_iota(jnp.int32, (32, BLOCK), 0) + place[1] * 32
        )

        def one_pair(pair, carry):
            base = 2 * (pair & (AHEAD - 1))
            for copy in copies(pair, base):
                copy.wait()

            @pl.when(pair + AHEAD - 1 < pairs)
            def _():
                for copy in copies(pair + AHEAD - 1, 2 * ((pair + AHEAD - 1) & (AHEAD - 1))):
                    copy.start()

            for side in range(2):
                job = 2 * pair + side
                owner, block = place[HEAD + 2 * JOBS + job], place[HEAD + JOBS + job]
                lanes = pl.ds(pl.multiple_of(block * BLOCK, BLOCK), BLOCK)
                summed = dot(window[owner], plane[base + side], NN)
                summed = summed.reshape(2, FIELDS, 32, BLOCK)
                turn_re, turn_im = phase[base + side, 0:32], phase[base + side, 32:64]
                product = summed[0] * turn_re[None] + summed[1] * turn_im[None]
                along_y = wave_rows * (summed[0, 1] * turn_im - summed[1, 1] * turn_re)
                value = jnp.concatenate(
                    [jnp.sum(product, axis=1), jnp.sum(along_y, axis=0, keepdims=True)], axis=0
                )
                if previous is not None:
                    value = value + previous[owner, :, lanes]
                out[owner, :, lanes] = value
            return carry

        lax.fori_loop(0, pairs, one_pair, 0)


def field_stage(steps, first, place, main, extra, extra_at, t_even, t_odd, rows, previous):
    def whole(shape):
        return pl.BlockSpec(
            shape, lambda i, _: (0,) * len(shape), pipeline_mode=pl.Buffered(1)
        )

    def kernel(*refs):
        field_kernel(steps, *refs)

    piece = (N_GX, None, 2, 8, 8, 128)
    in_specs = [
        pl.BlockSpec(piece, lambda i, _: (0, first + i, 0, 0, 0, 0)),
        pl.BlockSpec(piece, lambda i, _: (0, extra_at, 0, 0, 0, 0)),
        whole((256, 768)),
        whole((256, 768)),
        pl.BlockSpec(memory_space=pl.ANY),
        pl.BlockSpec(memory_space=pl.ANY),
    ]
    operands = [place, main, extra, t_even, t_odd, *rows]
    if previous is not None:
        in_specs.append(whole((N_GY, 8, ROWS)))
        operands.append(previous)
    depth = 4 * len(steps)
    return pl.pallas_call(
        kernel,
        out_shape=jax.ShapeDtypeStruct((N_GY, 8, ROWS), F32),
        grid_spec=pltpu.PrefetchScalarGridSpec(
            num_scalar_prefetch=1,
            grid=(len(steps),),
            in_specs=in_specs,
            out_specs=whole((N_GY, 8, ROWS)),
            scratch_shapes=[
                pltpu.VMEM((depth, GRID + 16, 512), BF16),
                pltpu.VMEM((768, 256), BF16),
                pltpu.VMEM((768, 256), BF16),
                pltpu.VMEM((768, 256), BF16),
                pltpu.VMEM((768, 256), BF16),
                pltpu.VMEM((N_GY, 64 * FIELDS, depth * WINDOW), BF16),
                pltpu.VMEM((2 * AHEAD, 64, BLOCK), F32),
                pltpu.VMEM((2 * AHEAD, depth * WINDOW, BLOCK), BF16),
                pltpu.SemaphoreType.DMA((2, 2 * AHEAD)),
            ],
        ),
        name="field_stage",
    )(*operands)


def ghost_kernel(counts, values, slots, own, back):
    total = values[0]
    for source in range(1, N_GY):
        total = total + values[source]
    lane = lax.broadcasted_iota(jnp.int32, (8, OWN), 1)
    own[...] = jnp.where(lane < counts[0, 0], total[:, :OWN], 0.0)
    ghosts = pltpu.roll(total, ROWS - counts[0, 0], 1)[:, :GHOST]
    cell = lax.broadcasted_iota(jnp.int32, (OWN, GHOST), 0)
    chosen = (cell == slots[1:2]).astype(F32).astype(BF16)
    first, _ = split(ghosts)
    second, third = split(ghosts - first.astype(F32))
    parts = jnp.concatenate([first.astype(F32), second.astype(F32), third.astype(F32)], axis=0)
    placed = dot(parts.astype(BF16), chosen, NT)
    back[...] = placed[0:8] + (placed[8:16] + placed[16:24])


def ghost_stage(counts, values, slots):
    vmem = pl.BlockSpec(memory_space=pltpu.VMEM)
    return pl.pallas_call(
        ghost_kernel,
        out_shape=(
            jax.ShapeDtypeStruct((8, OWN), F32),
            jax.ShapeDtypeStruct((8, OWN), F32),
        ),
        in_specs=[pl.BlockSpec(memory_space=pltpu.SMEM), vmem, vmem],
        out_specs=(vmem, vmem),
        name="ghost_stage",
    )(counts, values, slots)


def final_kernel(own, arrived, velocity, strain):
    total = own[...] + arrived[...]
    velocity[...] = total[:3]
    strain[0:1] = total[3:4]
    strain[1:2] = total[7:8]
    strain[2:5] = total[4:7]


def final_stage(own, arrived):
    return pl.pallas_call(
        final_kernel,
        out_shape=(
            jax.ShapeDtypeStruct((3, OWN), F32),
            jax.ShapeDtypeStruct((5, OWN), F32),
        ),
        name="final_stage",
    )(own, arrived)


def job_list(live, owners, index_gx, index_gy):
    needed = (live + BLOCK - 1) // BLOCK
    valid = jnp.arange(BLOCKS, dtype=jnp.int32)[None, :] < needed[:, None]
    valid = valid.reshape(-1).astype(jnp.int32)
    item = jnp.arange(N_GY * BLOCKS, dtype=jnp.int32)
    before = jnp.sum(jnp.where(item[None, :] < item[:, None], valid[None, :], 0), axis=1)
    jobs = jnp.sum(valid)
    wanted = jnp.minimum(jnp.arange(JOBS, dtype=jnp.int32), jobs - 1)
    chosen = (before[None, :] == wanted[:, None]) & (valid[None, :] > 0)
    found = jnp.sum(jnp.where(chosen, item[None, :], 0), axis=1)
    entry = found // BLOCKS
    at_entry = entry[:, None] == jnp.arange(N_GY, dtype=jnp.int32)[None, :]
    owner = jnp.sum(jnp.where(at_entry, owners[None, :], 0), axis=1)
    return jnp.concatenate(
        [jnp.stack([index_gx, index_gy, jobs]), entry, found % BLOCKS, owner]
    )


def per_device(
    source_hat, particle_start, particle_offset, ghost_start, ghost_offset, ghost_slot, counts
):
    index_gx = lax.axis_index("gx").astype(jnp.int32)
    index_gy = lax.axis_index("gy").astype(jnp.int32)
    members = range(N_GY)
    mine = gather_stage(counts, particle_start, particle_offset, ghost_start, ghost_offset)
    partner = lax.ppermute(mine, "gy", [(i, i ^ 1) for i in members])

    table_z = jnp.asarray(left_triple(z_table()))
    twiddle = jnp.asarray(twiddles())
    sent = [
        z_stage(chunk + ((EXTRA,) if number == 0 else ()), source_hat, table_z, twiddle)
        for number, chunk in enumerate(CHUNKS)
    ]
    received = []
    for piece in sent:
        received.append(lax.all_to_all(piece, "gx", split_axis=0, concat_axis=0, tiled=True))
    pair = jnp.stack([mine, partner])
    pairs = [pair]
    for shift in (2, 6, 4):
        route = [(i, (i + shift) % N_GY) for i in members]
        pairs.append(lax.ppermute(pair, "gy", route))
    particles = jnp.concatenate(pairs, axis=0)
    shifts = jnp.array([0, 0, 2, 2, 6, 6, 4, 4], jnp.int32)
    owners = jnp.bitwise_xor(
        (index_gy - shifts) & (N_GY - 1), jnp.arange(N_GY, dtype=jnp.int32) & 1
    )
    place = job_list(particles[:, 7, 0].astype(jnp.int32), owners, index_gx, index_gy)
    table_y = jnp.asarray(left_triple(y_table()))
    table_y = lax.dynamic_index_in_dim(table_y, index_gy, 0, keepdims=False)
    rows = row_stage(place, particles, table_y)

    t_even = jnp.asarray(left_triple(x_table(0)))
    t_odd = jnp.asarray(left_triple(x_table(1)))
    partial = None
    for number, chunk in enumerate(CHUNKS):
        partial = field_stage(
            chunk, 0, place, received[number], received[0], len(CHUNKS[0]),
            t_even, t_odd, rows, partial,
        )
    partial = lax.all_to_all(partial, "gy", split_axis=0, concat_axis=0, tiled=True)
    own, back = ghost_stage(counts, partial, ghost_slot)
    devices = range(N_GX)
    route = [((i + 1) % N_GX, i) for i in devices]
    return final_stage(own, lax.ppermute(back, "gx", route))


def solution(mesh):
    in_specs = (
        P(None, None, "gx", "gy", None),
        P(None, ("gx", "gy")),
        P(None, ("gx", "gy")),
        P(None, None, ("gx", "gy")),
        P(None, None, ("gx", "gy")),
        P(None, ("gx", "gy")),
        P(("gx", "gy"), None),
    )
    out_specs = (P(None, ("gx", "gy")), P(None, ("gx", "gy")))
    return jax.shard_map(
        per_device, mesh=mesh, in_specs=in_specs, out_specs=out_specs, check_vma=False
    )
```

```python
import math

import jax
import jax.numpy as jnp
import numpy as np
from jax import lax
from jax.experimental import pallas as pl
from jax.experimental.pallas import tpu as pltpu
from jax.sharding import PartitionSpec as P


F32 = jnp.float32
BF16 = jnp.bfloat16
SUPPORT = 8
GRID = 256
HALF = GRID // 2
N_GX = 16
N_GY = 8
OWN = 2048
GHOST = 512
ROWS = OWN + GHOST
WAVE = 2.0 * math.pi / GRID
WINDOW = 48
BLOCK = 256
CHUNKS = ((0, 2, 1, 3),)
ORDER = (0, 2, 1, 3)
FIELDS = 7
EXTRA = 4
BLOCKS = ROWS // BLOCK
JOBS = N_GY * BLOCKS + 2
HEAD = 3
AHEAD = 8
SLOTS = 8


def numpy_halves(table):
    import ml_dtypes

    high = table.astype(ml_dtypes.bfloat16)
    low = (table - high.astype(np.float64)).astype(ml_dtypes.bfloat16)
    return high, low


def left_triple(table):
    high, low = numpy_halves(table)
    return np.concatenate([high, high, low], axis=-1)


def z_table():
    c1, slab, part, step = np.meshgrid(
        np.arange(2), np.arange(N_GX), np.arange(2), np.arange(4), indexing="ij"
    )
    position = (8 * slab + 2 * step + c1).reshape(-1, 1)
    part = part.reshape(-1, 1)
    angle = (position * np.arange(HALF)[None, :] % HALF) * (2.0 * np.pi / HALF)
    cosine, sine = np.cos(angle), np.sin(angle)
    from_real = np.where(part == 0, cosine, sine)
    from_imag = np.where(part == 0, -sine, cosine)
    return np.concatenate([from_real, from_imag], axis=1)


def x_table(parity):
    modes = 2 * np.arange(HALF) + parity
    angle = (np.arange(HALF)[:, None] * modes[None, :] % GRID) * (2.0 * np.pi / GRID)
    cosine, sine = np.cos(angle), np.sin(angle)
    return np.block([[cosine, -sine], [sine, cosine]])


def y_table():
    index = np.arange(GRID)
    angle = (index[:, None] * index[None, :] % GRID) * (2.0 * np.pi / GRID)
    cosine = np.cos(angle).reshape(N_GY, 1, GRID // N_GY, GRID)
    sine = -np.sin(angle).reshape(N_GY, 1, GRID // N_GY, GRID)
    return np.concatenate([cosine, sine], axis=1).reshape(N_GY, 2 * (GRID // N_GY), GRID)


def y_tables():
    full = y_table()
    high, low = numpy_halves(full)
    none = np.zeros_like(high[..., :SUPPORT])
    near_high, near_low = high[..., :SUPPORT], low[..., :SUPPORT]
    return np.concatenate([high, low, near_high, near_high, near_low, none], axis=-1)


def twiddles():
    angle = np.arange(HALF) * (2.0 * np.pi / GRID)
    table = np.stack([np.cos(angle), np.sin(angle)])
    return np.repeat(table[:, None, :], 32, axis=1).astype(np.float32)


def split(value):
    high = value.astype(BF16)
    return high, (value - high.astype(F32)).astype(BF16)


def signed(index):
    return jnp.where(index < GRID // 2, index, index - GRID).astype(F32)


NT = (((1,), (1,)), ((), ()))
NN = (((1,), (0,)), ((), ()))


def dot(a, b, dims):
    return lax.dot_general(a, b, dims, preferred_element_type=F32)


def z_kernel(groups, source, table, twiddle, *rest):
    outs, even, odd = rest[:-2], rest[-2], rest[-1]
    home = {c: (outs[g], group.index(c)) for g, group in enumerate(groups) for c in group}
    pieces = tuple(home)
    quad = pl.program_id(0)
    with_extra = EXTRA in pieces
    parities = [p for p in range(2) if any(c != EXTRA and c % 2 == p for c in pieces)]
    row = lax.broadcasted_iota(jnp.int32, (32, GRID), 0)
    mode_y = signed(row + lax.axis_index("gy") * 32)
    mode_z = signed(lax.broadcasted_iota(jnp.int32, (32, GRID), 1))
    half_wave_z = 0.5 * WAVE * mode_z
    partial_square = mode_y * mode_y + mode_z * mode_z
    turn_re, turn_im = twiddle[0], twiddle[1]

    def build(k):
        index_x = lax.axis_index("gx") * 16 + quad * 4 + k
        mode_x = jnp.where(index_x < GRID // 2, index_x, index_x - GRID).astype(F32)
        inverse = 1.0 / jnp.maximum(mode_x * mode_x + partial_square, 1.0)
        v = []
        for r in range(2):
            s1, s2, s3 = source[r, 0, k], source[r, 1, k], source[r, 2, k]
            ratio = (s1 * mode_x + s2 * mode_y + s3 * mode_z) * inverse
            v.append((s1 - mode_x * ratio, s2 - mode_y * ratio, s3 - mode_z * ratio))
        rows = [
            (v[0][0], v[1][0], k * 128),
            (v[0][1], v[1][1], k * 128 + 32),
            (v[0][2], v[1][2], k * 128 + 64),
            (-half_wave_z * v[1][0], half_wave_z * v[0][0], k * 128 + 96),
        ]
        if with_extra:
            rows.append((-half_wave_z * v[1][1], half_wave_z * v[0][1], 512 + k * 32))
        for real, imag, start in rows:
            here = slice(start, start + 32)
            for p in parities if start < 512 else range(2):
                if p == 0:
                    re = real[:, :HALF] + real[:, HALF:]
                    im = imag[:, :HALF] + imag[:, HALF:]
                    target = even
                else:
                    re0 = real[:, :HALF] - real[:, HALF:]
                    im0 = imag[:, :HALF] - imag[:, HALF:]
                    re = re0 * turn_re - im0 * turn_im
                    im = re0 * turn_im + im0 * turn_re
                    target = odd
                for r, value in ((0, re), (1, im)):
                    high, low = split(value)
                    target[here, r * HALF : (r + 1) * HALF] = high
                    target[here, GRID + r * HALF : GRID + (r + 1) * HALF] = low
                    target[here, 2 * GRID + r * HALF : 2 * GRID + (r + 1) * HALF] = high

    def transform(pair):
        for p in parities:
            wanted = [c for c in pieces if c != EXTRA and c % 2 == p]
            if not wanted:
                continue
            c_low, c_high = min(wanted) // 2, max(wanted) // 2 + 1
            data = (even, odd)[p][pair * 256 : pair * 256 + 256]
            result = dot(table[c_low * 128 : c_high * 128], data, NT)
            for c in wanted:
                top = (c // 2 - c_low) * 128
                out, at = home[c]
                for side in range(2):
                    out[:, at, side, pair] = result[
                        top : top + 128, side * 128 : side * 128 + 128
                    ].reshape(N_GX, 8, 128)

    build(0)
    build(1)
    transform(0)
    build(2)
    build(3)
    transform(1)
    if with_extra:
        halves = [dot(table[...], data[512:640], NT) for data in (even, odd)]
        v = [halves[c % 2][(c // 2) * 128 : (c // 2) * 128 + 128] for c in range(4)]
        lane = lax.broadcasted_iota(jnp.int32, (128, 128), 1)
        lower64 = lane < 64
        lower32 = (lane & 32) == 0
        p0 = [jnp.where(lower64, v[c], pltpu.roll(v[c + 2], 64, 1)) for c in range(2)]
        p1 = [jnp.where(lower64, pltpu.roll(v[c], 64, 1), v[c + 2]) for c in range(2)]
        out, at = home[EXTRA]
        for k1, p in ((0, p0), (1, p1)):
            q0 = jnp.where(lower32, p[0], pltpu.roll(p[1], 32, 1))
            q1 = jnp.where(lower32, pltpu.roll(p[0], 96, 1), p[1])
            out[:, at, 0, k1] = q0.reshape(N_GX, 8, 128)
            out[:, at, 1, k1] = q1.reshape(N_GX, 8, 128)


def z_stage(groups, source, table, twiddle):
    def kernel(*refs):
        z_kernel(groups, *refs)

    return pl.pallas_call(
        kernel,
        out_shape=tuple(
            jax.ShapeDtypeStruct((N_GX, len(group), 2, 8, 8, 128), F32) for group in groups
        ),
        grid=(4,),
        in_specs=[
            pl.BlockSpec((2, 3, 4, 32, GRID), lambda i: (0, 0, i, 0, 0)),
            pl.BlockSpec((256, 768), lambda i: (0, 0)),
            pl.BlockSpec((2, 32, HALF), lambda i: (0, 0, 0)),
        ],
        out_specs=tuple(
            pl.BlockSpec((N_GX, len(group), 2, 2, 8, 128), lambda i: (0, 0, 0, i, 0, 0))
            for group in groups
        ),
        scratch_shapes=[pltpu.VMEM((640, 768), BF16), pltpu.VMEM((640, 768), BF16)],
        name="z_stage",
    )(source, table, twiddle)


def weight(distance, offset):
    shifted = distance - (SUPPORT // 2 - 1) - offset
    inside = (distance >= 0.0) & (distance < SUPPORT)
    return jnp.where(inside, jnp.exp(-5.6 / SUPPORT * shifted * shifted), 0.0)


def wrapped(distance):
    return jnp.where(distance < 0.0, distance + GRID, distance)


def gather_kernel(counts, start, offset, other_start, other_offset, out, packed):
    own, ghosts = counts[0, 0], counts[0, 2]
    lane = lax.broadcasted_iota(jnp.int32, (8, ROWS), 1)
    packed[...] = jnp.zeros_like(packed)
    packed[0:3, :GHOST] = other_start[:, 1].astype(F32)
    packed[3:6, :GHOST] = other_offset[:, 1]
    moved = pltpu.roll(packed[...], own, 1)
    packed[0:3, :OWN] = start[...].astype(F32)
    packed[3:6, :OWN] = offset[...]
    out[...] = jnp.where(lane < own, packed[...], moved)
    lane = lane[0:1]
    out[6:7, :] = jnp.where(lane < own + ghosts, 1.0, 0.0)
    out[7:8, :] = jnp.where(lane == 0, own + ghosts, 0).astype(F32)


def gather_stage(counts, start, offset, other_start, other_offset):
    vmem = pl.BlockSpec(memory_space=pltpu.VMEM)
    return pl.pallas_call(
        gather_kernel,
        out_shape=jax.ShapeDtypeStruct((8, ROWS), F32),
        in_specs=[
            pl.BlockSpec(memory_space=pltpu.SMEM),
            vmem,
            vmem,
            vmem,
            vmem,
        ],
        out_specs=vmem,
        scratch_shapes=[pltpu.VMEM((8, ROWS), F32)],
        name="gather_stage",
    )(counts, start, offset, other_start, other_offset)


def row_kernel(place, particles, table, near_table, phases, planes, phase, plane, sent_phase, sent_plane):
    y_cell = lax.broadcasted_iota(jnp.int32, (GRID, BLOCK), 0).astype(F32)
    support = lax.broadcasted_iota(jnp.int32, (SUPPORT, BLOCK), 0).astype(F32)
    x_cell = lax.broadcasted_iota(jnp.int32, (WINDOW, BLOCK), 0).astype(F32)
    local_z = lax.broadcasted_iota(jnp.int32, (16, BLOCK), 0)
    turn_of = local_z // 4
    c = 2 * (turn_of & 1) + turn_of // 2
    z_cell = (place[0] * 16 + 4 * (local_z % 4) + c).astype(F32)
    jobs = 2 * ((place[2] + 1) // 2)

    def copies(slot, job):
        return (
            pltpu.make_async_copy(phase.at[slot], phases.at[job], sent_phase.at[slot]),
            pltpu.make_async_copy(plane.at[slot], planes.at[job], sent_plane.at[slot]),
        )

    def one_job(job, carry):
        slot = job & (SLOTS - 1)

        @pl.when(job >= SLOTS)
        def _():
            for copy in copies(slot, job):
                copy.wait()

        entry, block = place[HEAD + job], place[HEAD + JOBS + job]
        owner = place[HEAD + 2 * JOBS + job]
        data = particles[entry, :, pl.ds(pl.multiple_of(block * BLOCK, BLOCK), BLOCK)]
        chosen = jnp.where(y_cell == data[1:2], 1.0, 0.0).astype(BF16)
        base = dot(table[...], jnp.concatenate([chosen, chosen], axis=0), NN)
        weight_y = weight(support, data[4:5])
        high = weight_y.astype(BF16).astype(F32)
        near = jnp.concatenate([high, weight_y - high, high, jnp.zeros_like(high)], axis=0)
        near = dot(near_table[...], near.astype(BF16), NN)
        phase[slot, 0:32] = base[0:32] * near[0:32] - base[32:64] * near[32:64]
        phase[slot, 32:64] = base[0:32] * near[32:64] + base[32:64] * near[0:32]
        weight_x = weight(x_cell + (owner * 32).astype(F32) - data[0:1], data[3:4])
        weight_z = weight(wrapped(z_cell - data[2:3]), data[5:6]) * data[6:7]
        for z in range(16):
            plane[slot, z * WINDOW : (z + 1) * WINDOW] = (weight_x * weight_z[z : z + 1]).astype(
                BF16
            )
        for copy in copies(slot, job):
            copy.start()
        return carry

    lax.fori_loop(0, jobs, one_job, 0)
    for slot in range(SLOTS):

        @pl.when(jobs > slot)
        def _():
            for copy in copies(slot, 0):
                copy.wait()


def row_stage(place, particles, table, near_table):
    return pl.pallas_call(
        row_kernel,
        out_shape=(
            jax.ShapeDtypeStruct((JOBS, 64, BLOCK), F32),
            jax.ShapeDtypeStruct((JOBS, 16 * WINDOW, BLOCK), BF16),
        ),
        grid_spec=pltpu.PrefetchScalarGridSpec(
            num_scalar_prefetch=1,
            grid=(1,),
            in_specs=[
                pl.BlockSpec((N_GY, 8, ROWS), lambda i, _: (0, 0, 0)),
                pl.BlockSpec((64, 512), lambda i, _: (0, 0)),
                pl.BlockSpec((64, 32), lambda i, _: (0, 0)),
            ],
            out_specs=(pl.BlockSpec(memory_space=pl.ANY), pl.BlockSpec(memory_space=pl.ANY)),
            scratch_shapes=[
                pltpu.VMEM((SLOTS, 64, BLOCK), F32),
                pltpu.VMEM((SLOTS, 16 * WINDOW, BLOCK), BF16),
                pltpu.SemaphoreType.DMA((SLOTS,)),
                pltpu.SemaphoreType.DMA((SLOTS,)),
            ],
        ),
        name="row_stage",
    )(place, particles, table, near_table)


def field_kernel(steps, place, main, extra, t_even, t_odd, phases, planes, *rest):
    previous = rest[0] if len(rest) == 11 else None
    out, field, work0, work1, work2, work3, window, phase, plane, arrived = rest[-10:]
    work = (work0, work1, work2, work3)
    first_c = ORDER.index(steps[0])
    depth = 4 * len(steps)
    step_c = pl.program_id(0)
    turn_of = first_c + step_c
    c = 2 * (turn_of & 1) + turn_of // 2
    pairs = (place[2] + 1) // 2

    def copies(pair, base):
        found = []
        for side in range(2):
            job, slot = 2 * pair + side, base + side
            rows = pl.ds(first_c * 4 * WINDOW, depth * WINDOW)
            found.append(
                pltpu.make_async_copy(phases.at[job], phase.at[slot], arrived.at[0, slot])
            )
            found.append(
                pltpu.make_async_copy(planes.at[job, rows], plane.at[slot], arrived.at[1, slot])
            )
        return found

    for ahead in range(AHEAD - 1):

        @pl.when((step_c == 0) & (pairs > ahead))
        def _():
            for copy in copies(ahead, 2 * ahead):
                copy.start()

    lane = lax.broadcasted_iota(jnp.int32, (HALF, 128), 1)
    group = lane // 32
    row = lax.broadcasted_iota(jnp.int32, (HALF, 128), 0)
    wave_y = WAVE * signed(lane % 32 + place[1] * 32)
    cross_y = jnp.where((group == 1) | (group == 3), 0.5 * wave_y, 0.0)
    half_same = jnp.where((group == 1) | (group == 2), 0.5, 0.0)
    plain_left = group == 2
    plain_extra = group == 3
    flat_main = main.reshape(GRID * 8, 128)
    flat_extra = extra.reshape(GRID * 8, 128)
    waves = [WAVE * signed(2 * row + parity) for parity in range(2)]
    for step in range(4):
        results = []
        for parity in range(2):
            target = work[2 * (step % 2) + parity]
            wave_x = waves[parity]
            cross_x = half_same * wave_x

            def load(flat, q):
                top = parity * 64 + q * 4 + step
                return jnp.concatenate(
                    [flat[pl.ds(source * 128 + top, 8, stride=8), :] for source in range(N_GX)]
                )

            parts = []
            for q in range(2):
                value = load(flat_main, q)
                moved = pltpu.roll(load(flat_extra, q), 32 * (3 - c), 1)
                left = pltpu.roll(value, 96, 1)
                right = pltpu.roll(value, 32, 1)
                cross = cross_y * right + cross_x * value
                plain = jnp.where(plain_left, left, jnp.where(plain_extra, moved, 0.0))
                parts.append((value, wave_x * left, cross, plain))
            (a_re, x_re, c_re, p_re), (a_im, x_im, c_im, p_im) = parts
            for top, left, value in (
                (0, 0, jnp.where(plain_extra, -x_im, a_re)),
                (HALF, 0, jnp.where(plain_extra, x_re, a_im)),
                (0, 128, p_re - c_im),
                (HALF, 128, p_im + c_re),
            ):
                high, low = split(value)
                lanes = slice(left, left + 128)
                target[top : top + HALF, lanes] = high
                target[GRID + top : GRID + top + HALF, lanes] = low
                target[2 * GRID + top : 2 * GRID + top + HALF, lanes] = high
            results.append(dot((t_even, t_odd)[parity][...], target[...], NN))
        from_even, from_odd = results
        near = (from_even + from_odd).astype(BF16)
        far = (from_even - from_odd).astype(BF16)
        z = step_c * 4 + step
        for q in range(2):
            lanes = slice(q * 256, q * 256 + 256)
            field[z, 0:HALF, lanes] = near[q * HALF : q * HALF + HALF]
            field[z, HALF:GRID, lanes] = far[q * HALF : q * HALF + HALF]
            field[z, GRID : GRID + 16, lanes] = near[q * HALF : q * HALF + 16]

    @pl.when(step_c == len(steps) - 1)
    def _():
        if previous is None:
            out[...] = jnp.zeros_like(out)
        else:
            out[...] = previous[...]

        for owner in range(N_GY):
            block = field[:, owner * 32 : owner * 32 + WINDOW, :]
            turned = block.reshape(depth * WINDOW, 512).T
            for q in range(2):
                top = q * 32 * FIELDS
                window[owner, top : top + 128] = turned[q * 256 : q * 256 + 128]
                window[owner, top + 128 : top + 224] = turned[q * 256 + 160 : q * 256 + 256]
        wave_rows = WAVE * signed(
            lax.broadcasted_iota(jnp.int32, (32, BLOCK), 0) + place[1] * 32
        )

        def one_pair(pair, carry):
            base = 2 * (pair & (AHEAD - 1))
            for copy in copies(pair, base):
                copy.wait()

            @pl.when(pair + AHEAD - 1 < pairs)
            def _():
                for copy in copies(pair + AHEAD - 1, 2 * ((pair + AHEAD - 1) & (AHEAD - 1))):
                    copy.start()

            for side in range(2):
                job = 2 * pair + side
                owner, block = place[HEAD + 2 * JOBS + job], place[HEAD + JOBS + job]
                lanes = pl.ds(pl.multiple_of(block * BLOCK, BLOCK), BLOCK)
                summed = dot(window[owner], plane[base + side], NN)
                summed = summed.reshape(2, FIELDS, 32, BLOCK)
                turn_re, turn_im = phase[base + side, 0:32], phase[base + side, 32:64]
                product = summed[0] * turn_re[None] + summed[1] * turn_im[None]
                along_y = wave_rows * (summed[0, 1] * turn_im - summed[1, 1] * turn_re)
                value = jnp.concatenate(
                    [jnp.sum(product, axis=1), jnp.sum(along_y, axis=0, keepdims=True)], axis=0
                )
                if previous is not None:
                    value = value + previous[owner, :, lanes]
                out[owner, :, lanes] = value
            return carry

        lax.fori_loop(0, pairs, one_pair, 0)


def field_stage(steps, first, place, main, extra, extra_at, t_even, t_odd, rows, previous):
    def whole(shape):
        return pl.BlockSpec(
            shape, lambda i, _: (0,) * len(shape), pipeline_mode=pl.Buffered(1)
        )

    def kernel(*refs):
        field_kernel(steps, *refs)

    piece = (N_GX, None, 2, 8, 8, 128)
    in_specs = [
        pl.BlockSpec(piece, lambda i, _: (0, first + i, 0, 0, 0, 0)),
        pl.BlockSpec(piece, lambda i, _: (0, extra_at, 0, 0, 0, 0)),
        whole((256, 768)),
        whole((256, 768)),
        pl.BlockSpec(memory_space=pl.ANY),
        pl.BlockSpec(memory_space=pl.ANY),
    ]
    operands = [place, main, extra, t_even, t_odd, *rows]
    if previous is not None:
        in_specs.append(whole((N_GY, 8, ROWS)))
        operands.append(previous)
    depth = 4 * len(steps)
    return pl.pallas_call(
        kernel,
        out_shape=jax.ShapeDtypeStruct((N_GY, 8, ROWS), F32),
        grid_spec=pltpu.PrefetchScalarGridSpec(
            num_scalar_prefetch=1,
            grid=(len(steps),),
            in_specs=in_specs,
            out_specs=whole((N_GY, 8, ROWS)),
            scratch_shapes=[
                pltpu.VMEM((depth, GRID + 16, 512), BF16),
                pltpu.VMEM((768, 256), BF16),
                pltpu.VMEM((768, 256), BF16),
                pltpu.VMEM((768, 256), BF16),
                pltpu.VMEM((768, 256), BF16),
                pltpu.VMEM((N_GY, 64 * FIELDS, depth * WINDOW), BF16),
                pltpu.VMEM((2 * AHEAD, 64, BLOCK), F32),
                pltpu.VMEM((2 * AHEAD, depth * WINDOW, BLOCK), BF16),
                pltpu.SemaphoreType.DMA((2, 2 * AHEAD)),
            ],
        ),
        name="field_stage",
    )(*operands)


def ghost_kernel(counts, values, slots, own, back):
    total = values[0]
    for source in range(1, N_GY):
        total = total + values[source]
    lane = lax.broadcasted_iota(jnp.int32, (8, OWN), 1)
    own[...] = jnp.where(lane < counts[0, 0], total[:, :OWN], 0.0)
    ghosts = pltpu.roll(total, ROWS - counts[0, 0], 1)[:, :GHOST]
    cell = lax.broadcasted_iota(jnp.int32, (OWN, GHOST), 0)
    chosen = (cell == slots[1:2]).astype(F32).astype(BF16)
    first, _ = split(ghosts)
    second, third = split(ghosts - first.astype(F32))
    parts = jnp.concatenate([first.astype(F32), second.astype(F32), third.astype(F32)], axis=0)
    placed = dot(parts.astype(BF16), chosen, NT)
    back[...] = placed[0:8] + (placed[8:16] + placed[16:24])


def ghost_stage(counts, values, slots):
    vmem = pl.BlockSpec(memory_space=pltpu.VMEM)
    return pl.pallas_call(
        ghost_kernel,
        out_shape=(
            jax.ShapeDtypeStruct((8, OWN), F32),
            jax.ShapeDtypeStruct((8, OWN), F32),
        ),
        in_specs=[pl.BlockSpec(memory_space=pltpu.SMEM), vmem, vmem],
        out_specs=(vmem, vmem),
        name="ghost_stage",
    )(counts, values, slots)


def final_kernel(own, arrived, velocity, strain):
    total = own[...] + arrived[...]
    velocity[...] = total[:3]
    strain[0:1] = total[3:4]
    strain[1:2] = total[7:8]
    strain[2:5] = total[4:7]


def final_stage(own, arrived):
    return pl.pallas_call(
        final_kernel,
        out_shape=(
            jax.ShapeDtypeStruct((3, OWN), F32),
            jax.ShapeDtypeStruct((5, OWN), F32),
        ),
        name="final_stage",
    )(own, arrived)


def job_list(live, owners, index_gx, index_gy):
    needed = (live + BLOCK - 1) // BLOCK
    valid = jnp.arange(BLOCKS, dtype=jnp.int32)[None, :] < needed[:, None]
    valid = valid.reshape(-1).astype(jnp.int32)
    item = jnp.arange(N_GY * BLOCKS, dtype=jnp.int32)
    before = jnp.sum(jnp.where(item[None, :] < item[:, None], valid[None, :], 0), axis=1)
    jobs = jnp.sum(valid)
    wanted = jnp.minimum(jnp.arange(JOBS, dtype=jnp.int32), jobs - 1)
    chosen = (before[None, :] == wanted[:, None]) & (valid[None, :] > 0)
    found = jnp.sum(jnp.where(chosen, item[None, :], 0), axis=1)
    entry = found // BLOCKS
    at_entry = entry[:, None] == jnp.arange(N_GY, dtype=jnp.int32)[None, :]
    owner = jnp.sum(jnp.where(at_entry, owners[None, :], 0), axis=1)
    return jnp.concatenate(
        [jnp.stack([index_gx, index_gy, jobs]), entry, found % BLOCKS, owner]
    )


def per_device(
    source_hat, particle_start, particle_offset, ghost_start, ghost_offset, ghost_slot, counts
):
    index_gx = lax.axis_index("gx").astype(jnp.int32)
    index_gy = lax.axis_index("gy").astype(jnp.int32)
    members = range(N_GY)
    mine = gather_stage(counts, particle_start, particle_offset, ghost_start, ghost_offset)
    partner = lax.ppermute(mine, "gy", [(i, i ^ 1) for i in members])

    table_z = jnp.asarray(left_triple(z_table()))
    twiddle = jnp.asarray(twiddles())
    groups = (CHUNKS[0] + (EXTRA,),) + CHUNKS[1:]
    sent = z_stage(groups, source_hat, table_z, twiddle)
    received = []
    for piece in sent:
        received.append(lax.all_to_all(piece, "gx", split_axis=0, concat_axis=0, tiled=True))
    pair = jnp.stack([mine, partner])
    pairs = [pair]
    for shift in (2, 6, 4):
        route = [(i, (i + shift) % N_GY) for i in members]
        pairs.append(lax.ppermute(pair, "gy", route))
    particles = jnp.concatenate(pairs, axis=0)
    shifts = jnp.array([0, 0, 2, 2, 6, 6, 4, 4], jnp.int32)
    owners = jnp.bitwise_xor(
        (index_gy - shifts) & (N_GY - 1), jnp.arange(N_GY, dtype=jnp.int32) & 1
    )
    place = job_list(particles[:, 7, 0].astype(jnp.int32), owners, index_gx, index_gy)
    tables_y = y_tables()
    table_y = lax.dynamic_index_in_dim(jnp.asarray(tables_y), index_gy, 0, keepdims=False)
    rows = row_stage(place, particles, table_y[:, :512], table_y[:, 512:])

    t_even = jnp.asarray(left_triple(x_table(0)))
    t_odd = jnp.asarray(left_triple(x_table(1)))
    partial = None
    for number, chunk in enumerate(CHUNKS):
        partial = field_stage(
            chunk, 0, place, received[number], received[0], len(CHUNKS[0]),
            t_even, t_odd, rows, partial,
        )
    partial = lax.all_to_all(partial, "gy", split_axis=0, concat_axis=0, tiled=True)
    own, back = ghost_stage(counts, partial, ghost_slot)
    devices = range(N_GX)
    route = [((i + 1) % N_GX, i) for i in devices]
    return final_stage(own, lax.ppermute(back, "gx", route))


def solution(mesh):
    in_specs = (
        P(None, None, "gx", "gy", None),
        P(None, ("gx", "gy")),
        P(None, ("gx", "gy")),
        P(None, None, ("gx", "gy")),
        P(None, None, ("gx", "gy")),
        P(None, ("gx", "gy")),
        P(("gx", "gy"), None),
    )
    out_specs = (P(None, ("gx", "gy")), P(None, ("gx", "gy")))
    return jax.shard_map(
        per_device, mesh=mesh, in_specs=in_specs, out_specs=out_specs, check_vma=False
    )
```

```python
import math

import jax
import jax.numpy as jnp
import numpy as np
from jax import lax
from jax.experimental import pallas as pl
from jax.experimental.pallas import tpu as pltpu
from jax.sharding import PartitionSpec as P


F32 = jnp.float32
BF16 = jnp.bfloat16
SUPPORT = 8
GRID = 256
HALF = GRID // 2
N_GX = 16
N_GY = 8
OWN = 2048
GHOST = 512
ROWS = OWN + GHOST
WAVE = 2.0 * math.pi / GRID
WINDOW = 48
BLOCK = 256
CHUNKS = ((0, 2, 1, 3),)
ORDER = (0, 2, 1, 3)
FIELDS = 7
EXTRA = 4
BLOCKS = ROWS // BLOCK
JOBS = N_GY * BLOCKS + 2
HEAD = 3
AHEAD = 8
SLOTS = 8


def numpy_halves(table):
    import ml_dtypes

    high = table.astype(ml_dtypes.bfloat16)
    low = (table - high.astype(np.float64)).astype(ml_dtypes.bfloat16)
    return high, low


def left_triple(table):
    high, low = numpy_halves(table)
    return np.concatenate([high, high, low], axis=-1)


def z_table():
    c1, slab, part, step = np.meshgrid(
        np.arange(2), np.arange(N_GX), np.arange(2), np.arange(4), indexing="ij"
    )
    position = (8 * slab + 2 * step + c1).reshape(-1, 1)
    part = part.reshape(-1, 1)
    angle = (position * np.arange(HALF)[None, :] % HALF) * (2.0 * np.pi / HALF)
    cosine, sine = np.cos(angle), np.sin(angle)
    from_real = np.where(part == 0, cosine, sine)
    from_imag = np.where(part == 0, -sine, cosine)
    return np.concatenate([from_real, from_imag], axis=1)


def x_table(parity):
    modes = 2 * np.arange(HALF) + parity
    angle = (np.arange(HALF)[:, None] * modes[None, :] % GRID) * (2.0 * np.pi / GRID)
    cosine, sine = np.cos(angle), np.sin(angle)
    return np.block([[cosine, -sine], [sine, cosine]])


def y_table():
    index = np.arange(GRID)
    angle = (index[:, None] * index[None, :] % GRID) * (2.0 * np.pi / GRID)
    cosine = np.cos(angle).reshape(N_GY, 1, GRID // N_GY, GRID)
    sine = -np.sin(angle).reshape(N_GY, 1, GRID // N_GY, GRID)
    return np.concatenate([cosine, sine], axis=1).reshape(N_GY, 2 * (GRID // N_GY), GRID)


def y_tables():
    full = y_table()
    high, low = numpy_halves(full)
    none = np.zeros_like(high[..., :SUPPORT])
    near_high, near_low = high[..., :SUPPORT], low[..., :SUPPORT]
    return np.concatenate([high, low, near_high, near_high, near_low, none], axis=-1)


def twiddles():
    angle = np.arange(HALF) * (2.0 * np.pi / GRID)
    table = np.stack([np.cos(angle), np.sin(angle)])
    return np.repeat(table[:, None, :], 32, axis=1).astype(np.float32)


def split(value):
    high = value.astype(BF16)
    return high, (value - high.astype(F32)).astype(BF16)


def signed(index):
    return jnp.where(index < GRID // 2, index, index - GRID).astype(F32)


NT = (((1,), (1,)), ((), ()))
NN = (((1,), (0,)), ((), ()))


def dot(a, b, dims):
    return lax.dot_general(a, b, dims, preferred_element_type=F32)


def z_kernel(groups, source, table, twiddle, *rest):
    outs, even, odd = rest[:-2], rest[-2], rest[-1]
    home = {c: (outs[g], group.index(c)) for g, group in enumerate(groups) for c in group}
    pieces = tuple(home)
    quad = pl.program_id(0)
    with_extra = EXTRA in pieces
    parities = [p for p in range(2) if any(c != EXTRA and c % 2 == p for c in pieces)]
    row = lax.broadcasted_iota(jnp.int32, (32, GRID), 0)
    mode_y = signed(row + lax.axis_index("gy") * 32)
    mode_z = signed(lax.broadcasted_iota(jnp.int32, (32, GRID), 1))
    half_wave_z = 0.5 * WAVE * mode_z
    partial_square = mode_y * mode_y + mode_z * mode_z
    turn_re, turn_im = twiddle[0], twiddle[1]

    def build(k):
        index_x = lax.axis_index("gx") * 16 + quad * 4 + k
        mode_x = jnp.where(index_x < GRID // 2, index_x, index_x - GRID).astype(F32)
        inverse = 1.0 / jnp.maximum(mode_x * mode_x + partial_square, 1.0)
        v = []
        for r in range(2):
            s1, s2, s3 = source[r, 0, k], source[r, 1, k], source[r, 2, k]
            ratio = (s1 * mode_x + s2 * mode_y + s3 * mode_z) * inverse
            v.append((s1 - mode_x * ratio, s2 - mode_y * ratio, s3 - mode_z * ratio))
        rows = [
            (v[0][0], v[1][0], k * 128),
            (v[0][1], v[1][1], k * 128 + 32),
            (v[0][2], v[1][2], k * 128 + 64),
            (-half_wave_z * v[1][0], half_wave_z * v[0][0], k * 128 + 96),
        ]
        if with_extra:
            rows.append((-half_wave_z * v[1][1], half_wave_z * v[0][1], 512 + k * 32))
        for real, imag, start in rows:
            here = slice(start, start + 32)
            for p in parities if start < 512 else range(2):
                if p == 0:
                    re = real[:, :HALF] + real[:, HALF:]
                    im = imag[:, :HALF] + imag[:, HALF:]
                    target = even
                else:
                    re0 = real[:, :HALF] - real[:, HALF:]
                    im0 = imag[:, :HALF] - imag[:, HALF:]
                    re = re0 * turn_re - im0 * turn_im
                    im = re0 * turn_im + im0 * turn_re
                    target = odd
                for r, value in ((0, re), (1, im)):
                    high, low = split(value)
                    target[here, r * HALF : (r + 1) * HALF] = high
                    target[here, GRID + r * HALF : GRID + (r + 1) * HALF] = low
                    target[here, 2 * GRID + r * HALF : 2 * GRID + (r + 1) * HALF] = high

    def transform(pair):
        for p in parities:
            wanted = [c for c in pieces if c != EXTRA and c % 2 == p]
            if not wanted:
                continue
            c_low, c_high = min(wanted) // 2, max(wanted) // 2 + 1
            data = (even, odd)[p][pair * 256 : pair * 256 + 256]
            result = dot(table[c_low * 128 : c_high * 128], data, NT)
            for c in wanted:
                top = (c // 2 - c_low) * 128
                out, at = home[c]
                for side in range(2):
                    out[:, at, side, pair] = result[
                        top : top + 128, side * 128 : side * 128 + 128
                    ].reshape(N_GX, 8, 128)

    build(0)
    build(1)
    transform(0)
    build(2)
    build(3)
    transform(1)
    if with_extra:
        halves = [dot(table[...], data[512:640], NT) for data in (even, odd)]
        v = [halves[c % 2][(c // 2) * 128 : (c // 2) * 128 + 128] for c in range(4)]
        lane = lax.broadcasted_iota(jnp.int32, (128, 128), 1)
        lower64 = lane < 64
        lower32 = (lane & 32) == 0
        p0 = [jnp.where(lower64, v[c], pltpu.roll(v[c + 2], 64, 1)) for c in range(2)]
        p1 = [jnp.where(lower64, pltpu.roll(v[c], 64, 1), v[c + 2]) for c in range(2)]
        out, at = home[EXTRA]
        for k1, p in ((0, p0), (1, p1)):
            q0 = jnp.where(lower32, p[0], pltpu.roll(p[1], 32, 1))
            q1 = jnp.where(lower32, pltpu.roll(p[0], 96, 1), p[1])
            out[:, at, 0, k1] = q0.reshape(N_GX, 8, 128)
            out[:, at, 1, k1] = q1.reshape(N_GX, 8, 128)


def z_stage(groups, source, table, twiddle):
    def kernel(*refs):
        z_kernel(groups, *refs)

    return pl.pallas_call(
        kernel,
        out_shape=tuple(
            jax.ShapeDtypeStruct((N_GX, len(group), 2, 8, 8, 128), F32) for group in groups
        ),
        grid=(4,),
        in_specs=[
            pl.BlockSpec((2, 3, 4, 32, GRID), lambda i: (0, 0, i, 0, 0)),
            pl.BlockSpec((256, 768), lambda i: (0, 0)),
            pl.BlockSpec((2, 32, HALF), lambda i: (0, 0, 0)),
        ],
        out_specs=tuple(
            pl.BlockSpec((N_GX, len(group), 2, 2, 8, 128), lambda i: (0, 0, 0, i, 0, 0))
            for group in groups
        ),
        scratch_shapes=[pltpu.VMEM((640, 768), BF16), pltpu.VMEM((640, 768), BF16)],
        name="z_stage",
    )(source, table, twiddle)


def weight(distance, offset):
    shifted = distance - (SUPPORT // 2 - 1) - offset
    inside = (distance >= 0.0) & (distance < SUPPORT)
    return jnp.where(inside, jnp.exp(-5.6 / SUPPORT * shifted * shifted), 0.0)


def wrapped(distance):
    return jnp.where(distance < 0.0, distance + GRID, distance)


def gather_kernel(counts, start, offset, other_start, other_offset, out, packed):
    own, ghosts = counts[0, 0], counts[0, 2]
    lane = lax.broadcasted_iota(jnp.int32, (8, ROWS), 1)
    packed[...] = jnp.zeros_like(packed)
    packed[0:3, :GHOST] = other_start[:, 1].astype(F32)
    packed[3:6, :GHOST] = other_offset[:, 1]
    moved = pltpu.roll(packed[...], own, 1)
    packed[0:3, :OWN] = start[...].astype(F32)
    packed[3:6, :OWN] = offset[...]
    out[...] = jnp.where(lane < own, packed[...], moved)
    lane = lane[0:1]
    out[6:7, :] = jnp.where(lane < own + ghosts, 1.0, 0.0)
    out[7:8, :] = jnp.where(lane == 0, own + ghosts, 0).astype(F32)


def gather_stage(counts, start, offset, other_start, other_offset):
    vmem = pl.BlockSpec(memory_space=pltpu.VMEM)
    return pl.pallas_call(
        gather_kernel,
        out_shape=jax.ShapeDtypeStruct((8, ROWS), F32),
        in_specs=[
            pl.BlockSpec(memory_space=pltpu.SMEM),
            vmem,
            vmem,
            vmem,
            vmem,
        ],
        out_specs=vmem,
        scratch_shapes=[pltpu.VMEM((8, ROWS), F32)],
        name="gather_stage",
    )(counts, start, offset, other_start, other_offset)


def row_kernel(place, particles, table, near_table, phases, planes, phase, plane, sent_phase, sent_plane):
    y_cell = lax.broadcasted_iota(jnp.int32, (GRID, BLOCK), 0).astype(F32)
    support = lax.broadcasted_iota(jnp.int32, (SUPPORT, BLOCK), 0).astype(F32)
    x_cell = lax.broadcasted_iota(jnp.int32, (WINDOW, BLOCK), 0).astype(F32)
    local_z = lax.broadcasted_iota(jnp.int32, (16, BLOCK), 0)
    turn_of = local_z // 4
    c = 2 * (turn_of & 1) + turn_of // 2
    z_cell = (place[0] * 16 + 4 * (local_z % 4) + c).astype(F32)
    jobs = 2 * ((place[2] + 1) // 2)

    def copies(slot, job):
        return (
            pltpu.make_async_copy(phase.at[slot], phases.at[job], sent_phase.at[slot]),
            pltpu.make_async_copy(plane.at[slot], planes.at[job], sent_plane.at[slot]),
        )

    def one_job(job, carry):
        slot = job & (SLOTS - 1)

        @pl.when(job >= SLOTS)
        def _():
            for copy in copies(slot, job):
                copy.wait()

        entry, block = place[HEAD + job], place[HEAD + JOBS + job]
        owner = place[HEAD + 2 * JOBS + job]
        data = particles[entry, :, pl.ds(pl.multiple_of(block * BLOCK, BLOCK), BLOCK)]
        chosen = jnp.where(y_cell == data[1:2], 1.0, 0.0).astype(BF16)
        base = dot(table[...], jnp.concatenate([chosen, chosen], axis=0), NN)
        weight_y = weight(support, data[4:5])
        high = weight_y.astype(BF16).astype(F32)
        near = jnp.concatenate([high, weight_y - high, high, jnp.zeros_like(high)], axis=0)
        near = dot(near_table[...], near.astype(BF16), NN)
        phase[slot, 0:32] = base[0:32] * near[0:32] - base[32:64] * near[32:64]
        phase[slot, 32:64] = base[0:32] * near[32:64] + base[32:64] * near[0:32]
        weight_x = weight(x_cell + (owner * 32).astype(F32) - data[0:1], data[3:4])
        weight_z = weight(wrapped(z_cell - data[2:3]), data[5:6]) * data[6:7]
        for z in range(16):
            plane[slot, z * WINDOW : (z + 1) * WINDOW] = (weight_x * weight_z[z : z + 1]).astype(
                BF16
            )
        for copy in copies(slot, job):
            copy.start()
        return carry

    lax.fori_loop(0, jobs, one_job, 0)
    for slot in range(SLOTS):

        @pl.when(jobs > slot)
        def _():
            for copy in copies(slot, 0):
                copy.wait()


def row_stage(place, particles, table, near_table):
    return pl.pallas_call(
        row_kernel,
        out_shape=(
            jax.ShapeDtypeStruct((JOBS, 64, BLOCK), F32),
            jax.ShapeDtypeStruct((JOBS, 16 * WINDOW, BLOCK), BF16),
        ),
        grid_spec=pltpu.PrefetchScalarGridSpec(
            num_scalar_prefetch=1,
            grid=(1,),
            in_specs=[
                pl.BlockSpec((N_GY, 8, ROWS), lambda i, _: (0, 0, 0)),
                pl.BlockSpec((64, 512), lambda i, _: (0, 0)),
                pl.BlockSpec((64, 32), lambda i, _: (0, 0)),
            ],
            out_specs=(pl.BlockSpec(memory_space=pl.ANY), pl.BlockSpec(memory_space=pl.ANY)),
            scratch_shapes=[
                pltpu.VMEM((SLOTS, 64, BLOCK), F32),
                pltpu.VMEM((SLOTS, 16 * WINDOW, BLOCK), BF16),
                pltpu.SemaphoreType.DMA((SLOTS,)),
                pltpu.SemaphoreType.DMA((SLOTS,)),
            ],
        ),
        name="row_stage",
    )(place, particles, table, near_table)


def field_kernel(steps, place, main, extra, t_even, t_odd, phases, planes, *rest):
    previous = rest[0] if len(rest) == 11 else None
    out, field, work0, work1, work2, work3, window, phase, plane, arrived = rest[-10:]
    work = (work0, work1, work2, work3)
    first_c = ORDER.index(steps[0])
    depth = 4 * len(steps)
    step_c = pl.program_id(0)
    turn_of = first_c + step_c
    c = 2 * (turn_of & 1) + turn_of // 2
    pairs = (place[2] + 1) // 2

    def copies(pair, base):
        found = []
        for side in range(2):
            job, slot = 2 * pair + side, base + side
            rows = pl.ds(first_c * 4 * WINDOW, depth * WINDOW)
            found.append(
                pltpu.make_async_copy(phases.at[job], phase.at[slot], arrived.at[0, slot])
            )
            found.append(
                pltpu.make_async_copy(planes.at[job, rows], plane.at[slot], arrived.at[1, slot])
            )
        return found

    for ahead in range(AHEAD - 1):

        @pl.when((step_c == 0) & (pairs > ahead))
        def _():
            for copy in copies(ahead, 2 * ahead):
                copy.start()

    lane = lax.broadcasted_iota(jnp.int32, (HALF, 128), 1)
    group = lane // 32
    row = lax.broadcasted_iota(jnp.int32, (HALF, 128), 0)
    wave_y = WAVE * signed(lane % 32 + place[1] * 32)
    cross_y = jnp.where((group == 1) | (group == 3), 0.5 * wave_y, 0.0)
    half_same = jnp.where((group == 1) | (group == 2), 0.5, 0.0)
    plain_left = group == 2
    plain_extra = group == 3
    flat_main = main.reshape(GRID * 8, 128)
    flat_extra = extra.reshape(GRID * 8, 128)
    waves = [WAVE * signed(2 * row + parity) for parity in range(2)]
    for step in range(4):
        results = []
        for parity in range(2):
            target = work[2 * (step % 2) + parity]
            wave_x = waves[parity]
            cross_x = half_same * wave_x

            def load(flat, q):
                top = parity * 64 + q * 4 + step
                return jnp.concatenate(
                    [flat[pl.ds(source * 128 + top, 8, stride=8), :] for source in range(N_GX)]
                )

            parts = []
            for q in range(2):
                value = load(flat_main, q)
                moved = pltpu.roll(load(flat_extra, q), 32 * (3 - c), 1)
                left = pltpu.roll(value, 96, 1)
                right = pltpu.roll(value, 32, 1)
                cross = cross_y * right + cross_x * value
                plain = jnp.where(plain_left, left, jnp.where(plain_extra, moved, 0.0))
                parts.append((value, wave_x * left, cross, plain))
            (a_re, x_re, c_re, p_re), (a_im, x_im, c_im, p_im) = parts
            for top, left, value in (
                (0, 0, jnp.where(plain_extra, -x_im, a_re)),
                (HALF, 0, jnp.where(plain_extra, x_re, a_im)),
                (0, 128, p_re - c_im),
                (HALF, 128, p_im + c_re),
            ):
                high, low = split(value)
                lanes = slice(left, left + 128)
                target[top : top + HALF, lanes] = high
                target[GRID + top : GRID + top + HALF, lanes] = low
                target[2 * GRID + top : 2 * GRID + top + HALF, lanes] = high
            results.append(dot((t_even, t_odd)[parity][...], target[...], NN))
        from_even, from_odd = results
        near = (from_even + from_odd).astype(BF16)
        far = (from_even - from_odd).astype(BF16)
        z = step_c * 4 + step
        for q in range(2):
            lanes = slice(q * 256, q * 256 + 256)
            field[z, 0:HALF, lanes] = near[q * HALF : q * HALF + HALF]
            field[z, HALF:GRID, lanes] = far[q * HALF : q * HALF + HALF]
            field[z, GRID : GRID + 16, lanes] = near[q * HALF : q * HALF + 16]

    @pl.when(step_c == len(steps) - 1)
    def _():
        if previous is None:
            out[...] = jnp.zeros_like(out)
        else:
            out[...] = previous[...]

        for owner in range(N_GY):
            block = field[:, owner * 32 : owner * 32 + WINDOW, :]
            turned = block.reshape(depth * WINDOW, 512).T
            for q in range(2):
                top = q * 32 * FIELDS
                window[owner, top : top + 128] = turned[q * 256 : q * 256 + 128]
                window[owner, top + 128 : top + 224] = turned[q * 256 + 160 : q * 256 + 256]
        wave_rows = WAVE * signed(
            lax.broadcasted_iota(jnp.int32, (32, BLOCK), 0) + place[1] * 32
        )

        def one_pair(pair, carry):
            base = 2 * (pair & (AHEAD - 1))
            for copy in copies(pair, base):
                copy.wait()

            @pl.when(pair + AHEAD - 1 < pairs)
            def _():
                for copy in copies(pair + AHEAD - 1, 2 * ((pair + AHEAD - 1) & (AHEAD - 1))):
                    copy.start()

            for side in range(2):
                job = 2 * pair + side
                owner, block = place[HEAD + 2 * JOBS + job], place[HEAD + JOBS + job]
                lanes = pl.ds(pl.multiple_of(block * BLOCK, BLOCK), BLOCK)
                summed = dot(window[owner], plane[base + side], NN)
                summed = summed.reshape(2, FIELDS, 32, BLOCK)
                turn_re, turn_im = phase[base + side, 0:32], phase[base + side, 32:64]
                product = summed[0] * turn_re[None] + summed[1] * turn_im[None]
                along_y = wave_rows * (summed[0, 1] * turn_im - summed[1, 1] * turn_re)
                value = jnp.concatenate(
                    [jnp.sum(product, axis=1), jnp.sum(along_y, axis=0, keepdims=True)], axis=0
                )
                if previous is not None:
                    value = value + previous[owner, :, lanes]
                out[owner, :, lanes] = value
            return carry

        lax.fori_loop(0, pairs, one_pair, 0)


def field_stage(steps, first, place, main, extra, extra_at, t_even, t_odd, rows, previous):
    def whole(shape):
        return pl.BlockSpec(
            shape, lambda i, _: (0,) * len(shape), pipeline_mode=pl.Buffered(1)
        )

    def kernel(*refs):
        field_kernel(steps, *refs)

    piece = (N_GX, None, 2, 8, 8, 128)
    in_specs = [
        pl.BlockSpec(piece, lambda i, _: (0, first + i, 0, 0, 0, 0)),
        pl.BlockSpec(piece, lambda i, _: (0, extra_at, 0, 0, 0, 0)),
        whole((256, 768)),
        whole((256, 768)),
        pl.BlockSpec(memory_space=pl.ANY),
        pl.BlockSpec(memory_space=pl.ANY),
    ]
    operands = [place, main, extra, t_even, t_odd, *rows]
    if previous is not None:
        in_specs.append(whole((N_GY, 8, ROWS)))
        operands.append(previous)
    depth = 4 * len(steps)
    return pl.pallas_call(
        kernel,
        out_shape=jax.ShapeDtypeStruct((N_GY, 8, ROWS), F32),
        grid_spec=pltpu.PrefetchScalarGridSpec(
            num_scalar_prefetch=1,
            grid=(len(steps),),
            in_specs=in_specs,
            out_specs=whole((N_GY, 8, ROWS)),
            scratch_shapes=[
                pltpu.VMEM((depth, GRID + 16, 512), BF16),
                pltpu.VMEM((768, 256), BF16),
                pltpu.VMEM((768, 256), BF16),
                pltpu.VMEM((768, 256), BF16),
                pltpu.VMEM((768, 256), BF16),
                pltpu.VMEM((N_GY, 64 * FIELDS, depth * WINDOW), BF16),
                pltpu.VMEM((2 * AHEAD, 64, BLOCK), F32),
                pltpu.VMEM((2 * AHEAD, depth * WINDOW, BLOCK), BF16),
                pltpu.SemaphoreType.DMA((2, 2 * AHEAD)),
            ],
        ),
        name="field_stage",
    )(*operands)


def ghost_kernel(counts, values, slots, own, back):
    total = values[0]
    for source in range(1, N_GY):
        total = total + values[source]
    lane = lax.broadcasted_iota(jnp.int32, (8, OWN), 1)
    own[...] = jnp.where(lane < counts[0, 0], total[:, :OWN], 0.0)
    ghosts = pltpu.roll(total, ROWS - counts[0, 0], 1)[:, :GHOST]
    cell = lax.broadcasted_iota(jnp.int32, (OWN, GHOST), 0)
    chosen = jnp.where(cell == slots[1:2], 1.0, 0.0).astype(BF16)
    first, _ = split(ghosts)
    second, third = split(ghosts - first.astype(F32))
    parts = jnp.concatenate([first.astype(F32), second.astype(F32), third.astype(F32)], axis=0)
    placed = dot(parts.astype(BF16), chosen, NT)
    back[...] = placed[0:8] + (placed[8:16] + placed[16:24])


def ghost_stage(counts, values, slots):
    vmem = pl.BlockSpec(memory_space=pltpu.VMEM)
    return pl.pallas_call(
        ghost_kernel,
        out_shape=(
            jax.ShapeDtypeStruct((8, OWN), F32),
            jax.ShapeDtypeStruct((8, OWN), F32),
        ),
        in_specs=[pl.BlockSpec(memory_space=pltpu.SMEM), vmem, vmem],
        out_specs=(vmem, vmem),
        name="ghost_stage",
    )(counts, values, slots)


def final_kernel(own, arrived, velocity, strain):
    total = own[...] + arrived[...]
    velocity[...] = total[:3]
    strain[0:1] = total[3:4]
    strain[1:2] = total[7:8]
    strain[2:5] = total[4:7]


def final_stage(own, arrived):
    vmem = pl.BlockSpec(memory_space=pltpu.VMEM)
    return pl.pallas_call(
        final_kernel,
        out_shape=(
            jax.ShapeDtypeStruct((3, OWN), F32),
            jax.ShapeDtypeStruct((5, OWN), F32),
        ),
        in_specs=[vmem, vmem],
        out_specs=(vmem, vmem),
        name="final_stage",
    )(own, arrived)


def job_list(live, owners, index_gx, index_gy):
    needed = (live + BLOCK - 1) // BLOCK
    valid = jnp.arange(BLOCKS, dtype=jnp.int32)[None, :] < needed[:, None]
    valid = valid.reshape(-1).astype(jnp.int32)
    item = jnp.arange(N_GY * BLOCKS, dtype=jnp.int32)
    before = jnp.sum(jnp.where(item[None, :] < item[:, None], valid[None, :], 0), axis=1)
    jobs = jnp.sum(valid)
    wanted = jnp.minimum(jnp.arange(JOBS, dtype=jnp.int32), jobs - 1)
    chosen = (before[None, :] == wanted[:, None]) & (valid[None, :] > 0)
    found = jnp.sum(jnp.where(chosen, item[None, :], 0), axis=1)
    entry = found // BLOCKS
    at_entry = entry[:, None] == jnp.arange(N_GY, dtype=jnp.int32)[None, :]
    owner = jnp.sum(jnp.where(at_entry, owners[None, :], 0), axis=1)
    return jnp.concatenate(
        [jnp.stack([index_gx, index_gy, jobs]), entry, found % BLOCKS, owner]
    )


def per_device(
    source_hat, particle_start, particle_offset, ghost_start, ghost_offset, ghost_slot, counts
):
    index_gx = lax.axis_index("gx").astype(jnp.int32)
    index_gy = lax.axis_index("gy").astype(jnp.int32)
    members = range(N_GY)
    mine = gather_stage(counts, particle_start, particle_offset, ghost_start, ghost_offset)
    partner = lax.ppermute(mine, "gy", [(i, i ^ 1) for i in members])

    table_z = jnp.asarray(left_triple(z_table()))
    twiddle = jnp.asarray(twiddles())
    groups = (CHUNKS[0] + (EXTRA,),) + CHUNKS[1:]
    sent = z_stage(groups, source_hat, table_z, twiddle)
    received = []
    for piece in sent:
        received.append(lax.all_to_all(piece, "gx", split_axis=0, concat_axis=0, tiled=True))
    pair = jnp.stack([mine, partner])
    pairs = [pair]
    for shift in (2, 6, 4):
        route = [(i, (i + shift) % N_GY) for i in members]
        pairs.append(lax.ppermute(pair, "gy", route))
    particles = jnp.concatenate(pairs, axis=0)
    shifts = jnp.array([0, 0, 2, 2, 6, 6, 4, 4], jnp.int32)
    owners = jnp.bitwise_xor(
        (index_gy - shifts) & (N_GY - 1), jnp.arange(N_GY, dtype=jnp.int32) & 1
    )
    place = job_list(particles[:, 7, 0].astype(jnp.int32), owners, index_gx, index_gy)
    tables_y = y_tables()
    table_y = lax.dynamic_index_in_dim(jnp.asarray(tables_y), index_gy, 0, keepdims=False)
    rows = row_stage(place, particles, table_y[:, :512], table_y[:, 512:])

    t_even = jnp.asarray(left_triple(x_table(0)))
    t_odd = jnp.asarray(left_triple(x_table(1)))
    partial = None
    for number, chunk in enumerate(CHUNKS):
        partial = field_stage(
            chunk, 0, place, received[number], received[0], len(CHUNKS[0]),
            t_even, t_odd, rows, partial,
        )
    partial = lax.all_to_all(partial, "gy", split_axis=0, concat_axis=0, tiled=True)
    own, back = ghost_stage(counts, partial, ghost_slot)
    devices = range(N_GX)
    route = [((i + 1) % N_GX, i) for i in devices]
    return final_stage(own, lax.ppermute(back, "gx", route))


def solution(mesh):
    in_specs = (
        P(None, None, "gx", "gy", None),
        P(None, ("gx", "gy")),
        P(None, ("gx", "gy")),
        P(None, None, ("gx", "gy")),
        P(None, None, ("gx", "gy")),
        P(None, ("gx", "gy")),
        P(("gx", "gy"), None),
    )
    out_specs = (P(None, ("gx", "gy")), P(None, ("gx", "gy")))
    return jax.shard_map(
        per_device, mesh=mesh, in_specs=in_specs, out_specs=out_specs, check_vma=False
    )
```
